32 devices in a mesh: groups: 2 (over y), store: 16 (over z, x, core).
Axes of the slice: x: 2, y: 2, z: 4, core: 2. Of those that a mesh axis runs over, the one named last changes fastest.
Arguments:
- queries: bfloat16 [2, 32, 8192], P(None, ('groups', 'store')), parts along dimension 1, may hold values from -6 to 206
- new_keys: bfloat16 [2, 32, 1024], P(None, ('groups', 'store')), parts along dimension 1, may hold values from -6 to 12.5
- incoming_values: bfloat16 [2, 32, 1024], P(None, ('groups', 'store')), parts along dimension 1, may hold values from -6 to 6
- key_left: bfloat16 [32, 4096, 160], P(('groups', 'store')), parts along dimension 0, may hold values from -12 to 12
- right_key_factor: bfloat16 [32, 160, 1024], P(('groups', 'store')), parts along dimension 0, may hold values from -0.5 to 0.5
- value_tile_store: bfloat16 [131072, 1024], P(('groups', 'store')), parts along dimension 0, may hold values from -6 to 6
- slot_map: int32 [32, 8, 512], P(('groups', 'store')), parts along dimension 0, may hold values from 0 to 65535, as said below
- chosen: int32 [2, 32, 8, 64], P(None, ('groups', 'store')), parts along dimension 1, may hold values from 0 to 511, as said below
- lengths: int32 [32], P(('groups', 'store')), parts along dimension 0, may hold values from 1024 to 4096
Outputs:
- attended: bfloat16 [2, 32, 8192], P(None, ('groups', 'store')), parts along dimension 1
The draws below stay inside these ranges and needn't reach their ends.
There are 2 independent parts, one for each index of `groups`. The reference program is written for one: setup_inputs(seed, part) draws one part's arguments, and reference() takes and returns one part's arrays. A program takes and returns all parts, laid end to end along the dimension named above; each array names one. Nothing has to cross between parts.
Inputs may be any that keep to these rules, and one draw needn't show every extreme that they name: `slot_map`: the entries are distinct; pool rows r * 4096 to (r+1) * 4096 - 1 stand on index r of store. `chosen`: the 64 blocks of one step, request and key head are distinct; at most 8 of them have their slot_map row on one index of store, and in every step some index of store holds exactly 8 of them for every request and key head.
All inputs are finite; a program needn't handle non-finite values.
Results may differ from the reference program's by a relative error of at most 0.005.
The reference program's roundings to bfloat16 on the way count: a program that leaves them out, or rounds other values in their place, can miss the bound.
Values may be sent and summed in bfloat16 or wider, within the bound.
A program may use at most 64 MiB of HBM per device.

```python
import jax
import jax.numpy as jnp
from jax import lax

QUERY_HEADS = 64
KEY_VALUE_HEADS = 8
HEAD_SIZE = 128
FACTOR_RANK = 160
BLOCK_TOKENS = 8
SELECTED_BLOCKS = 64
DECODE_STEPS = 2
CTX = 4096
TOTAL_REQUESTS = 16
CACHE_BLOCKS = 512
PER_HOLDER = 8
DEVICE_TILES = 4096
POOL = 65536
N_STORE = 16


def layout(key):
    child_seed = jax.random.fold_in(key, 11)
    child_seeds = jax.random.split(child_seed, TOTAL_REQUESTS * KEY_VALUE_HEADS)
    tile_ordering = jax.vmap(lambda single: jax.random.permutation(single, CACHE_BLOCKS))(child_seeds)
    return tile_ordering.reshape(TOTAL_REQUESTS, KEY_VALUE_HEADS, CACHE_BLOCKS).astype(jnp.int32)


def draw_slot_map(key, part):
    tile_ordering = layout(key)
    device_share = CACHE_BLOCKS // N_STORE
    tile_keeper = tile_ordering // device_share
    inner_offset = tile_ordering % device_share
    row_ids = jnp.arange(TOTAL_REQUESTS, dtype=jnp.int32)[:, None, None]
    head_numbers = jnp.arange(KEY_VALUE_HEADS, dtype=jnp.int32)[None, :, None]
    canonical = (row_ids * KEY_VALUE_HEADS + head_numbers) * device_share + inner_offset
    holder_seeds = jax.random.split(jax.random.fold_in(key, 13), N_STORE)
    holder_orders = jax.vmap(lambda single: jax.random.permutation(single, DEVICE_TILES))(holder_seeds).astype(jnp.int32)
    placed = holder_orders[tile_keeper, canonical]
    return (tile_keeper * DEVICE_TILES + placed).astype(jnp.int32)


def draw_chosen(key, part):
    tile_ordering = layout(key)
    device_share = CACHE_BLOCKS // N_STORE
    tile_keeper = tile_ordering // device_share
    inner_offset = tile_ordering % device_share
    block_numbers = jnp.arange(CACHE_BLOCKS, dtype=jnp.int32)
    picks = []
    for step_index in range(DECODE_STEPS):
        step_key = jax.random.fold_in(key, 100 + step_index)
        heat_key, hot_key, noise_seed, window_key = jax.random.split(step_key, 4)
        window_start = jax.random.randint(window_key, (TOTAL_REQUESTS, KEY_VALUE_HEADS, N_STORE), 0, device_share).astype(jnp.int32)
        start_here = jnp.take_along_axis(window_start, tile_keeper, axis=2)
        eligible = (inner_offset - start_here + device_share) % device_share < PER_HOLDER
        heat_level = jax.random.randint(heat_key, (N_STORE,), 0, 4)
        hottest = jax.random.randint(hot_key, (), 0, N_STORE)
        heat_level = jnp.where(jnp.arange(N_STORE) == hottest, 16, heat_level)
        random_noise = jax.random.randint(noise_seed, (TOTAL_REQUESTS, KEY_VALUE_HEADS, CACHE_BLOCKS), 0, 4096)
        scores = jnp.where(eligible, (heat_level[tile_keeper] + 1) * (4096 * CACHE_BLOCKS) + random_noise * CACHE_BLOCKS + block_numbers, block_numbers)
        top_idx = lax.top_k(scores.astype(jnp.int32), SELECTED_BLOCKS)[1]
        picks.append(top_idx.astype(jnp.int32))
    return jnp.stack(picks)


def draw_queries(key, part):
    gaussian_seed = jax.random.fold_in(jax.random.fold_in(key, 21), 0)
    sampled_blocks = jnp.clip(jax.random.normal(gaussian_seed, (DECODE_STEPS, TOTAL_REQUESTS, QUERY_HEADS, HEAD_SIZE), jnp.float32), -6.0, 6.0)
    return sampled_blocks.reshape(DECODE_STEPS, TOTAL_REQUESTS, QUERY_HEADS * HEAD_SIZE).astype(jnp.bfloat16)


def draw_new_keys(key, part):
    gaussian_seed = jax.random.fold_in(jax.random.fold_in(key, 31), 0)
    sampled_blocks = jnp.clip(jax.random.normal(gaussian_seed, (DECODE_STEPS, TOTAL_REQUESTS, KEY_VALUE_HEADS, HEAD_SIZE), jnp.float32), -6.0, 6.0)
    sampled_blocks = jnp.clip(sampled_blocks, -6.0, 12.5)
    return sampled_blocks.reshape(DECODE_STEPS, TOTAL_REQUESTS, KEY_VALUE_HEADS * HEAD_SIZE).astype(jnp.bfloat16)


def touch_ends(entries, rng, low, largest):
    spot = [jax.random.randint(jax.random.fold_in(rng, axis), (), 0, length) for axis, length in enumerate(entries.shape)]
    longest = entries.shape.index(max(entries.shape))
    beside = spot[:longest] + [(spot[longest] + 1) % entries.shape[longest]] + spot[longest + 1:]
    return entries.at[tuple(spot)].set(low).at[tuple(beside)].set(largest)


def block_scale(key, dims, cuts, low, largest):
    def one(axis_at, shards_of):
        heights = jax.random.uniform(jax.random.fold_in(jax.random.fold_in(key, 6), axis_at), (shards_of,), jnp.float32, low / len(cuts), largest / len(cuts))
        return jnp.repeat(jnp.exp(heights), dims[axis_at] // shards_of).reshape((-1,) + (1,) * (len(dims) - axis_at - 1))

    factor_of = one(*cuts[0])
    for cut in cuts[1:]:
        factor_of = factor_of * one(*cut)
    return factor_of


def centred(stream_key, dims, deviation, bound, cuts=(), kind=jnp.bfloat16):
    result = jax.random.normal(stream_key, dims, jnp.float32) * deviation
    if len(cuts) > 0:
        result = block_scale(stream_key, dims, cuts, -0.22, 0.18) * result
    return jnp.clip(result, min=-bound, max=bound).astype(kind)


def setup_inputs(seed: int = 0, part: int = 0) -> dict:
    keys = jax.random.split(jax.random.key(seed), 10)
    own_keys = jax.random.split(jax.random.fold_in(keys[9], part), 10)
    queries = draw_queries(jax.random.fold_in(jax.random.fold_in(keys[9], part), 71), part)
    new_keys = draw_new_keys(jax.random.fold_in(jax.random.fold_in(keys[9], part), 71), part)
    incoming_values = centred(own_keys[2], (DECODE_STEPS, TOTAL_REQUESTS, KEY_VALUE_HEADS * HEAD_SIZE), 1.0, 6.0, ((1, 16),))
    key_left = centred(own_keys[3], (TOTAL_REQUESTS, CTX, FACTOR_RANK), 2.0, 12.0, ((0, 16),))
    right_key_factor = centred(own_keys[4], (TOTAL_REQUESTS, FACTOR_RANK, KEY_VALUE_HEADS * HEAD_SIZE), FACTOR_RANK ** -0.5, 0.5, ((0, 16),))
    value_tile_store = centred(own_keys[5], (POOL, BLOCK_TOKENS * HEAD_SIZE), 1.0, 6.0, ((0, 16),))
    slot_map = draw_slot_map(jax.random.fold_in(jax.random.fold_in(keys[9], part), 71), part)
    chosen = draw_chosen(jax.random.fold_in(jax.random.fold_in(keys[9], part), 71), part)
    lengths = touch_ends(jax.random.randint(own_keys[8], (TOTAL_REQUESTS,), CTX // 4, CTX + 1), jax.random.fold_in(own_keys[8], 1), CTX // 4, CTX).astype(jnp.int32)
    return {"queries": queries, "new_keys": new_keys, "incoming_values": incoming_values, "key_left": key_left, "right_key_factor": right_key_factor, "value_tile_store": value_tile_store, "slot_map": slot_map, "chosen": chosen, "lengths": lengths}


ROPE_BASE = 500000.0


def apply_rotary(tensor, token_positions):
    half_dim = tensor.shape[-1] // 2
    inverse = ROPE_BASE ** (-(jnp.arange(half_dim, dtype=jnp.float32) * 2.0 / tensor.shape[-1]))
    angles = jnp.asarray(token_positions).astype(jnp.float32)[..., None] * inverse
    cosine = jnp.cos(angles)
    sine_vals = jnp.sin(angles)
    first_half = tensor[..., :half_dim]
    second_half = tensor[..., half_dim:]
    return jnp.concatenate([first_half * cosine - second_half * sine_vals, second_half * cosine + first_half * sine_vals], -1)


def reference(queries, new_keys, incoming_values, key_left, right_key_factor, value_tile_store, slot_map, chosen, lengths):
    query_group_size = QUERY_HEADS // KEY_VALUE_HEADS
    score_scale = HEAD_SIZE ** -0.5

    def row_fn(per_row):
        query_full, incoming_keys_full, incoming_values_full, left_rows, right_factor_rows, slot_row, chosen_row, length = per_row
        right_factor_heads = right_factor_rows.reshape(FACTOR_RANK, KEY_VALUE_HEADS, HEAD_SIZE).astype(jnp.float32)
        results = []
        for step_index in range(DECODE_STEPS):
            block_numbers = chosen_row[step_index]
            token_positions = (block_numbers[:, :, None] * BLOCK_TOKENS + jnp.arange(BLOCK_TOKENS, dtype=jnp.int32)).reshape(KEY_VALUE_HEADS, SELECTED_BLOCKS * BLOCK_TOKENS)
            picked = left_rows[token_positions].astype(jnp.float32)
            raw_keys = jnp.einsum('htr,rhd->htd', picked, right_factor_heads)
            cache_keys = apply_rotary(raw_keys, token_positions).astype(jnp.bfloat16)
            rotated_query = apply_rotary(query_full[step_index].reshape(QUERY_HEADS, HEAD_SIZE).astype(jnp.float32), length + step_index).astype(jnp.bfloat16)
            current_position = (length + jnp.arange(step_index + 1, dtype=jnp.int32))[:, None]
            current_keys = apply_rotary(incoming_keys_full[:step_index + 1].reshape(step_index + 1, KEY_VALUE_HEADS, HEAD_SIZE).astype(jnp.float32), current_position).astype(jnp.bfloat16)
            current_keys = jnp.transpose(current_keys, (1, 0, 2))
            current_values = jnp.transpose(incoming_values_full[:step_index + 1].reshape(step_index + 1, KEY_VALUE_HEADS, HEAD_SIZE), (1, 0, 2))
            slot_numbers = jnp.take_along_axis(slot_row, block_numbers, axis=1)
            tile_row_index = value_tile_store[slot_numbers].reshape(KEY_VALUE_HEADS, SELECTED_BLOCKS * BLOCK_TOKENS, HEAD_SIZE)
            grouped_queries = rotated_query.reshape(KEY_VALUE_HEADS, query_group_size, HEAD_SIZE).astype(jnp.float32)
            cache_scores = jnp.einsum('hgd,htd->hgt', grouped_queries, cache_keys.astype(jnp.float32)) * score_scale
            inside_len = token_positions < length
            cache_scores = jnp.where(inside_len[:, None, :], cache_scores, -jnp.inf)
            fresh_scores = jnp.einsum('hgd,hnd->hgn', grouped_queries, current_keys.astype(jnp.float32)) * score_scale
            highest = jnp.maximum(jnp.max(cache_scores, -1, keepdims=True), jnp.max(fresh_scores, -1, keepdims=True))
            cache_exp = jnp.exp(cache_scores - highest)
            fresh_exp = jnp.exp(fresh_scores - highest)
            denominator = jnp.sum(cache_exp, -1, keepdims=True) + jnp.sum(fresh_exp, -1, keepdims=True)
            cache_weight = (cache_exp / denominator).astype(jnp.bfloat16)
            fresh_weight = (fresh_exp / denominator).astype(jnp.bfloat16)
            attended = jnp.einsum('hgt,htd->hgd', cache_weight.astype(jnp.float32), tile_row_index.astype(jnp.float32))
            attended = attended + jnp.einsum('hgn,hnd->hgd', fresh_weight.astype(jnp.float32), current_values.astype(jnp.float32))
            results.append(attended.reshape(QUERY_HEADS * HEAD_SIZE).astype(jnp.bfloat16))
        return jnp.stack(results)

    per_row = (jnp.transpose(queries, (1, 0, 2)), jnp.transpose(new_keys, (1, 0, 2)), jnp.transpose(incoming_values, (1, 0, 2)), key_left, right_key_factor, slot_map, jnp.transpose(chosen, (1, 0, 2, 3)), lengths)
    output = lax.map(row_fn, per_row)
    return jnp.transpose(output, (1, 0, 2))
```

```python
import functools

import jax
import jax.numpy as jnp
import numpy as np
from jax import lax
from jax.experimental import pallas as pl
from jax.experimental.pallas import tpu as pltpu
from jax.sharding import PartitionSpec as P

KEY_VALUE_HEADS = 8
HEAD_SIZE = 128
BLOCK_TOKENS = 8


ROPE_BASE = 500000.0


def apply_rotary(tensor, token_positions):
    half_dim = tensor.shape[-1] // 2
    inverse = ROPE_BASE ** (-(jnp.arange(half_dim, dtype=jnp.float32) * 2.0 / tensor.shape[-1]))
    angles = jnp.asarray(token_positions).astype(jnp.float32)[..., None] * inverse
    cosine = jnp.cos(angles)
    sine_vals = jnp.sin(angles)
    first_half = tensor[..., :half_dim]
    second_half = tensor[..., half_dim:]
    return jnp.concatenate(
        [
            first_half * cosine - second_half * sine_vals,
            second_half * cosine + first_half * sine_vals,
        ],
        -1,
    )


def fetch_tiles(requests, value_tile_store):
    tile_row_index = jnp.take(
        value_tile_store,
        lax.all_to_all(requests, "store", split_axis=0, concat_axis=0, tiled=True),
        axis=0,
    )
    return lax.all_to_all(tile_row_index, "store", split_axis=0, concat_axis=0, tiled=True)


def build_requests(flat_idx, inside, total):
    buffer = jnp.zeros((total,), jnp.int32)
    return buffer.at[flat_idx.reshape(-1)].set(inside.reshape(-1))


def attend_row(
    query_full,
    incoming_keys_full,
    incoming_values_full,
    left_rows,
    right_factor_rows,
    block_numbers,
    tile_row_index,
    length,
    step_index,
):
    query_group_size = query_full.shape[-1] // HEAD_SIZE // KEY_VALUE_HEADS
    every_head = query_group_size * KEY_VALUE_HEADS
    selected_count = block_numbers.shape[1]
    score_scale = HEAD_SIZE ** (-0.5)
    right_factor_heads = right_factor_rows.reshape(
        right_factor_rows.shape[0], KEY_VALUE_HEADS, HEAD_SIZE
    )
    token_positions = (
        block_numbers[:, :, None] * BLOCK_TOKENS + jnp.arange(BLOCK_TOKENS, dtype=jnp.int32)
    ).reshape(KEY_VALUE_HEADS, selected_count * BLOCK_TOKENS)
    picked = left_rows[token_positions]
    raw_keys = jnp.einsum(
        "htr,rhd->htd", picked, right_factor_heads, preferred_element_type=jnp.float32
    )
    cache_keys = apply_rotary(raw_keys, token_positions).astype(jnp.bfloat16)
    rotated_query = apply_rotary(
        query_full[step_index].reshape(every_head, HEAD_SIZE).astype(jnp.float32),
        length + step_index,
    ).astype(jnp.bfloat16)
    current_position = (length + jnp.arange(step_index + 1, dtype=jnp.int32))[:, None]
    current_keys = apply_rotary(
        incoming_keys_full[: step_index + 1]
        .reshape(step_index + 1, KEY_VALUE_HEADS, HEAD_SIZE)
        .astype(jnp.float32),
        current_position,
    ).astype(jnp.bfloat16)
    current_keys = jnp.transpose(current_keys, (1, 0, 2))
    current_values = jnp.transpose(
        incoming_values_full[: step_index + 1].reshape(step_index + 1, KEY_VALUE_HEADS, HEAD_SIZE),
        (1, 0, 2),
    )
    local_values = tile_row_index.reshape(KEY_VALUE_HEADS, selected_count * BLOCK_TOKENS, HEAD_SIZE)
    grouped_queries = rotated_query.reshape(KEY_VALUE_HEADS, query_group_size, HEAD_SIZE)
    cache_scores = (
        jnp.einsum("hgd,htd->hgt", grouped_queries, cache_keys, preferred_element_type=jnp.float32)
        * score_scale
    )
    inside_len = token_positions < length
    cache_scores = jnp.where(inside_len[:, None, :], cache_scores, -jnp.inf)
    fresh_scores = (
        jnp.einsum(
            "hgd,hnd->hgn", grouped_queries, current_keys, preferred_element_type=jnp.float32
        )
        * score_scale
    )
    highest = jnp.maximum(
        jnp.max(cache_scores, -1, keepdims=True), jnp.max(fresh_scores, -1, keepdims=True)
    )
    cache_exp = jnp.exp(cache_scores - highest)
    fresh_exp = jnp.exp(fresh_scores - highest)
    denominator = jnp.sum(cache_exp, -1, keepdims=True) + jnp.sum(fresh_exp, -1, keepdims=True)
    cache_weight = (cache_exp / denominator).astype(jnp.bfloat16)
    fresh_weight = (fresh_exp / denominator).astype(jnp.bfloat16)
    attended = jnp.einsum(
        "hgt,htd->hgd", cache_weight, local_values, preferred_element_type=jnp.float32
    )
    attended = attended + jnp.einsum(
        "hgn,hnd->hgd", fresh_weight, current_values, preferred_element_type=jnp.float32
    )
    return attended.reshape(every_head * HEAD_SIZE).astype(jnp.bfloat16)


def per_device(
    queries,
    new_keys,
    incoming_values,
    key_left,
    right_key_factor,
    value_tile_store,
    slot_map,
    chosen,
    lengths,
):
    nstore = lax.axis_size("store")
    local_rows = key_left.shape[0]
    nchunk = slot_map.shape[2]
    step_count = chosen.shape[0]
    selected_count = chosen.shape[3]
    keeper_share = max(1, nchunk // nstore // 4)
    tile_limit = local_rows * KEY_VALUE_HEADS * keeper_share
    pool_here = value_tile_store.shape[0]
    slot_numbers = jnp.take_along_axis(
        jnp.broadcast_to(slot_map[None], (step_count,) + slot_map.shape), chosen, axis=3
    )
    tile_keeper = slot_numbers // pool_here
    inside = slot_numbers % pool_here
    matched = tile_keeper[..., :, None] == tile_keeper[..., None, :]
    earlier = jnp.arange(selected_count)[None, :] < jnp.arange(selected_count)[:, None]
    order_in = jnp.sum(jnp.logical_and(matched, earlier), -1)
    row_head = (
        jnp.arange(local_rows, dtype=jnp.int32)[:, None, None] * KEY_VALUE_HEADS
        + jnp.arange(KEY_VALUE_HEADS, dtype=jnp.int32)[None, :, None]
    )
    position = row_head * keeper_share + order_in
    tiles_all = []
    slot_span = step_count * tile_limit
    flat_idx = (
        tile_keeper * slot_span
        + jnp.arange(step_count, dtype=jnp.int32)[:, None, None, None] * tile_limit
        + position
    )
    requests = build_requests(flat_idx, inside, nstore * slot_span).reshape(nstore, slot_span)
    received = fetch_tiles(requests, value_tile_store).reshape(nstore * slot_span, -1)
    for step_index in range(step_count):
        tiles_all.append(received[flat_idx[step_index]])
    results = []
    for step_index in range(step_count):
        per_rows = [
            attend_row(
                queries[:, 0],
                new_keys[:, 0],
                incoming_values[:, 0],
                key_left[0],
                right_key_factor[0],
                chosen[step_index, 0],
                tiles_all[step_index][0],
                lengths[0],
                step_index,
            )
        ]
        results.append(jnp.stack(per_rows))
    return jnp.stack(results)


def fused_kernel(
    share, pool_here,
    length_ref, turn_cos_ref, turn_sin_ref, query_ref, new_key_ref, new_value_ref,
    chosen_ref, slot_ref, right_ref, coarse_cos_ref, coarse_sin_ref, fine_cos_ref, fine_sin_ref,
    spread_ref, left_hbm, regroup_hbm, pool_hbm,
    out_ref,
    left_ref, regroup_ref, pool_ref, send_ref, ask_ref, asked_ref, row_ref,
    place_ref, sign_ref, rotated_ref, fresh_key_ref, fresh_value_ref, flip_ref, token_ref,
    cosine_ref, sine_ref, score_ref, fresh_ref, routed_ref, wire_ref, got_ref,
    core_out, core_in, side_out, side_in, line_out, line_in, keep_ref,
    left_sem, regroup_sem, pool_sem, row_sem, ask_send, ask_recv, wire_send, wire_recv,
    core_send, core_recv, side_send, side_recv, line_send, line_recv,
):
    me = lax.axis_index("store")
    holders = send_ref.shape[0]
    depth = holders // 4
    rows, picks = chosen_ref.shape
    heads, blocks = slot_ref.shape
    steps = rows // heads
    rank = right_ref.shape[0]
    group = query_ref.shape[1] // HEAD_SIZE // heads
    both = steps * group
    half = HEAD_SIZE // 2
    quad = heads // 2
    scale = HEAD_SIZE ** (-0.5)
    core, side, layer = lax.rem(me, 2), lax.rem(me // 2, 2), me // 4

    def peer(j):
        far, across, ahead = j // (2 * depth), j // depth % 2, j % depth
        return (
            lax.rem(layer + ahead, depth) * 4
            + (1 - side if across else side) * 2
            + (1 - core if far else core)
        )

    def remote(src, dst, send, recv, target):
        return pltpu.make_async_remote_copy(
            src_ref=src, dst_ref=dst, send_sem=send, recv_sem=recv,
            device_id={"store": target}, device_id_type=pl.DeviceIdType.MESH,
        )

    barrier = pltpu.get_barrier_semaphore()

    def greet(k, _):
        pl.semaphore_signal(
            barrier, inc=1, device_id={"store": lax.rem(me + k, holders)},
            device_id_type=pl.DeviceIdType.MESH,
        )
        return 0

    lax.fori_loop(1, holders, greet, 0)

    left_copy = pltpu.make_async_copy(left_hbm, left_ref, left_sem.at[0])
    regroup_copy = pltpu.make_async_copy(regroup_hbm, regroup_ref, regroup_sem.at[0])
    left_copy.start()
    regroup_copy.start()
    octets = pool_here // 8
    pool_copies = [
        pltpu.make_async_copy(
            pool_hbm.at[:, pl.ds(2 * q, 2), pl.ds(HEAD_SIZE * t, HEAD_SIZE)],
            pool_ref.at[pl.ds(q * octets, octets), pl.ds(2 * t, 2), :],
            pool_sem.at[q * BLOCK_TOKENS + t],
        )
        for q in range(4)
        for t in range(BLOCK_TOKENS)
    ]
    for copy in pool_copies:
        copy.start()

    total = holders * share
    block_at = lax.broadcasted_iota(jnp.int32, (rows, blocks), 1)
    chosen = chosen_ref[...]
    hit = jnp.zeros((rows, blocks), jnp.int32)
    for pick in range(picks):
        hit = jnp.where(chosen[:, pick : pick + 1] == block_at, 1, hit)
    slot = slot_ref[...]
    if pool_here & (pool_here - 1) == 0:
        keeper_head = slot >> (pool_here.bit_length() - 1)
        inside = slot & (pool_here - 1)
    else:
        keeper_head = lax.div(slot, jnp.full_like(slot, pool_here))
        inside = slot - keeper_head * pool_here
    sign_ref[...] = (1 - 2 * (inside & 1)).astype(jnp.float32)
    inside = ((inside >> 1) & 3) * octets + (inside >> 3)
    keeper = jnp.concatenate([keeper_head] * steps, 0)
    kept = jnp.where(hit == 1, keeper, -1)
    before = (
        lax.broadcasted_iota(jnp.int32, (blocks, blocks), 0)
        < lax.broadcasted_iota(jnp.int32, (blocks, blocks), 1)
    ).astype(jnp.float32).astype(jnp.bfloat16)
    mine = [jnp.where(kept == holder, 1.0, 0.0) for holder in range(holders)]
    counts = jnp.dot(
        jnp.concatenate(mine, 0).astype(jnp.bfloat16), before, preferred_element_type=jnp.float32
    )
    order = jnp.zeros((rows, blocks), jnp.float32)
    for holder in range(holders):
        order = order + mine[holder] * counts[holder * rows : (holder + 1) * rows]
    place = jnp.where(hit == 1, keeper * share + order.astype(jnp.int32), -1)
    place_ref[...] = place
    low = (inside & 255).astype(jnp.float32)
    middle = ((inside >> 8) & 255).astype(jnp.float32)
    high = (inside >> 16).astype(jnp.float32)
    slot_at = lax.broadcasted_iota(jnp.int32, (total, blocks), 0)
    moved = []
    for row in range(rows):
        head = row % heads
        digits = jnp.concatenate(
            [low[head : head + 1], middle[head : head + 1], high[head : head + 1],
             jnp.zeros((5, blocks), jnp.float32)], 0
        ).astype(jnp.bfloat16)
        table = jnp.where(place[row : row + 1] == slot_at, 1.0, 0.0).astype(jnp.bfloat16)
        found = lax.dot_general(
            digits, table, (((1,), (1,)), ((), ())), preferred_element_type=jnp.float32
        ).astype(jnp.int32)
        found = found[0:1] + found[1:2] * 256 + found[2:3] * 65536
        moved.append(pltpu.roll(found, row * share, 1) if row else found)
    moved = jnp.concatenate(moved, 0)
    own_lanes = (
        lax.broadcasted_iota(jnp.int32, (rows, total), 1) // share
        == lax.broadcasted_iota(jnp.int32, (rows, total), 0)
    )
    for holder in range(holders):
        turned = pltpu.roll(moved, total - holder * share, 1) if holder else moved
        send_ref[holder] = jnp.sum(jnp.where(own_lanes, turned, 0), 0, keepdims=True)

    def ask_copy(j):
        target = peer(j)
        return remote(
            send_ref.at[target], ask_ref.at[j], ask_send.at[j], ask_recv.at[j], target
        )

    far_first = sorted(
        range(1, holders), key=lambda j: (-(min(j % depth, depth - j % depth)), -j)
    )
    pl.semaphore_wait(barrier, holders - 1)
    for j in far_first:
        ask_copy(j).start()
    ask_ref[0] = send_ref[me]

    spin_cos = [
        jnp.broadcast_to(
            jnp.concatenate([turn_cos_ref[s : s + 1]] * 2, 1), (group, HEAD_SIZE)
        )
        for s in range(steps)
    ]
    spin_sin = [
        jnp.broadcast_to(
            jnp.concatenate([-turn_sin_ref[s : s + 1], turn_sin_ref[s : s + 1]], 1),
            (group, HEAD_SIZE),
        )
        for s in range(steps)
    ]
    query_all = query_ref[...].astype(jnp.float32)
    key_all = new_key_ref[...].astype(jnp.float32)
    value_all = new_value_ref[...].astype(jnp.float32)
    fresh_cos = jnp.concatenate([spin_cos[s][:1] for s in range(steps)] + [spin_cos[0][: 8 - steps]], 0)
    fresh_sin = jnp.concatenate([spin_sin[s][:1] for s in range(steps)] + [spin_sin[0][: 8 - steps]], 0)
    both_cos = jnp.concatenate(spin_cos, 0)
    both_sin = jnp.concatenate(spin_sin, 0)
    empty = jnp.zeros((8 - steps, HEAD_SIZE), jnp.float32)
    for head in range(heads):
        lanes = slice(head * HEAD_SIZE, (head + 1) * HEAD_SIZE)
        flat = jnp.concatenate(
            [
                query_all[s : s + 1, (head * group + g) * HEAD_SIZE : (head * group + g + 1) * HEAD_SIZE]
                for s in range(steps)
                for g in range(group)
            ],
            0,
        )
        rotated_ref[head] = (
            flat * both_cos + pltpu.roll(flat, half, 1) * both_sin
        ).astype(jnp.bfloat16)
        flat = jnp.concatenate([key_all[:, lanes], empty], 0)
        fresh_key_ref[head] = (
            flat * fresh_cos + pltpu.roll(flat, half, 1) * fresh_sin
        ).astype(jnp.bfloat16)
        fresh_value_ref[head] = jnp.concatenate([value_all[:, lanes], empty], 0).astype(
            jnp.bfloat16
        )
        flip_ref[lanes, :] = right_ref[:, lanes].astype(jnp.float32).T.astype(jnp.bfloat16)
    for t in range(BLOCK_TOKENS):
        fine_cos, fine_sin = fine_cos_ref[t], fine_sin_ref[t]
        cosine_ref[t] = coarse_cos_ref[...] * fine_cos - coarse_sin_ref[...] * fine_sin
        sine_ref[t] = coarse_sin_ref[...] * fine_cos + coarse_cos_ref[...] * fine_sin
    left_copy.wait()
    regroup_copy.wait()
    wide = regroup_ref.shape[0]
    low_half = lax.broadcasted_iota(jnp.int32, (rank, 128), 1) < 64
    for m in range(blocks // 128):
        grouped = [
            jnp.dot(
                left_ref[:, (2 * m + n) * wide : (2 * m + n + 1) * wide], regroup_ref[...],
                preferred_element_type=jnp.float32,
            )
            for n in range(2)
        ]
        for t in range(0, BLOCK_TOKENS, 2):
            a, b = (value[:, t * 64 : (t + 2) * 64] for value in grouped)
            for odd, value in enumerate(
                (
                    jnp.where(low_half, a, pltpu.roll(b, 64, 1)),
                    jnp.where(low_half, pltpu.roll(a, 64, 1), b),
                )
            ):
                token_ref[t + odd, :, m * 128 : (m + 1) * 128] = value.astype(jnp.bfloat16)

    length = length_ref[0]
    place_at = lax.broadcasted_iota(jnp.int32, (total, blocks), 0)
    first_token = lax.broadcasted_iota(jnp.int32, (both, blocks), 1) * BLOCK_TOKENS
    fresh_keep = (
        lax.broadcasted_iota(jnp.int32, (both, 8), 1)
        <= lax.broadcasted_iota(jnp.int32, (both, 8), 0) // group
    )
    chunk = min(256, blocks)

    def one_head(head, _):
        query = rotated_ref[head]
        factor = flip_ref[pl.ds(pl.multiple_of(head * HEAD_SIZE, HEAD_SIZE), HEAD_SIZE)]
        for t in range(BLOCK_TOKENS):
            for at in range(0, blocks, chunk):
                lanes = slice(at, at + chunk)
                raw = jnp.dot(
                    factor, token_ref[t, :, lanes], preferred_element_type=jnp.float32
                )
                first, second = raw[:half], raw[half:]
                cosine, sine = cosine_ref[t, :, lanes], sine_ref[t, :, lanes]
                keys = jnp.concatenate(
                    [first * cosine - second * sine, second * cosine + first * sine], 0
                ).astype(jnp.bfloat16)
                score_ref[t, :, lanes] = (
                    jnp.dot(query, keys, preferred_element_type=jnp.float32) * scale
                )
        place = [place_ref[pl.ds(s * heads + head, 1)] for s in range(steps)]
        place_rows = jnp.concatenate(
            [jnp.broadcast_to(place[s], (group, blocks)) for s in range(steps)], 0
        )
        inside_at = jnp.where(place_rows >= 0, first_token, length)
        scores = [
            jnp.where(inside_at + t < length, score_ref[t], -jnp.inf)
            for t in range(BLOCK_TOKENS)
        ]
        fresh = lax.dot_general(
            query, fresh_key_ref[head], (((1,), (1,)), ((), ())),
            preferred_element_type=jnp.float32,
        ) * scale
        fresh = jnp.where(fresh_keep, fresh, -jnp.inf)
        top = scores[0]
        for t in range(1, BLOCK_TOKENS):
            top = jnp.maximum(top, scores[t])
        highest = jnp.maximum(
            jnp.max(top, -1, keepdims=True), jnp.max(fresh, -1, keepdims=True)
        )
        powers = [jnp.exp(score - highest) for score in scores]
        fresh_power = jnp.exp(fresh - highest)
        whole = powers[0]
        for t in range(1, BLOCK_TOKENS):
            whole = whole + powers[t]
        denominator = jnp.sum(whole, -1, keepdims=True) + jnp.sum(
            fresh_power, -1, keepdims=True
        )
        inverse = 1.0 / denominator
        fresh_ref[pl.ds(pl.multiple_of(head * both, both), both)] = jnp.dot(
            (fresh_power * inverse).astype(jnp.bfloat16), fresh_value_ref[head],
            preferred_element_type=jnp.float32,
        )
        sign = sign_ref[pl.ds(head, 1)]
        for s in range(steps):
            table = jnp.where(
                place[s] == place_at, jnp.broadcast_to(sign, (total, blocks)), 0.0
            ).astype(jnp.bfloat16)
            stacked = jnp.concatenate(
                [(power * inverse)[s * group : (s + 1) * group] for power in powers], 0
            ).astype(jnp.bfloat16)
            routed = lax.dot_general(
                stacked, table, (((1,), (1,)), ((), ())), preferred_element_type=jnp.float32
            )
            for t in range(BLOCK_TOKENS):
                routed_ref[t, head, s * group : (s + 1) * group] = routed[
                    t * group : (t + 1) * group
                ]
        return 0

    lane = lax.broadcasted_iota(jnp.int32, (both, total), 1) // share
    middle_t = BLOCK_TOKENS // 2

    def wire_copy(part, j):
        target = peer(j)
        return remote(
            wire_ref.at[part, target], got_ref.at[part, j],
            wire_send.at[part * holders + j], wire_recv.at[part * holders + j], target,
        )

    for part in range(2):
        lax.fori_loop(part * quad, (part + 1) * quad, one_head, 0)
        for upper in range(2):
            cells = [
                routed_ref[upper * middle_t + t, part * quad + h]
                for t in range(middle_t)
                for h in range(quad)
            ]
            step = 1
            while step < holders:
                low_side = lane // step % 2 == 0
                turned = list(cells)
                for at in range(holders):
                    if at // step % 2 == 0:
                        a, b = cells[at], cells[at + step]
                        turned[at] = jnp.where(
                            low_side, a, pltpu.roll(b, step * share, 1)
                        )
                        turned[at + step] = jnp.where(
                            low_side, pltpu.roll(a, total - step * share, 1), b
                        )
                cells = turned
                step *= 2
            for holder in range(holders):
                wire_ref[part, holder, :, upper * total : (upper + 1) * total] = cells[
                    holder
                ].astype(jnp.bfloat16)
        for j in far_first:
            wire_copy(part, j).start()

    for j in range(1, holders):
        ask_copy(j).wait_recv()
    asked_ref[...] = jnp.clip(ask_ref[...], 0, pool_ref.shape[0] - 1)
    row_copy = pltpu.make_async_copy(asked_ref, row_ref, row_sem.at[0])
    row_copy.start()
    row_copy.wait()
    for copy in pool_copies:
        copy.wait()

    early = lax.broadcasted_iota(jnp.int32, (both, HEAD_SIZE), 0) < group

    def partial(part, j):
        if j:
            arrived = got_ref[part, j]
        else:
            arrived = wire_ref[part, me]
        weight = jnp.maximum(
            jnp.dot(arrived, spread_ref[...], preferred_element_type=jnp.float32), 0.0
        )
        results = []
        for h in range(0, quad, 2):
            lhs, columns = [], []
            for h_at in (h, h + 1):
                own = weight[:, h_at * HEAD_SIZE : (h_at + 1) * HEAD_SIZE]
                lhs.append(
                    jnp.concatenate(
                        [jnp.where(early, own, 0.0), jnp.where(early, 0.0, own)], 1
                    ).astype(jnp.bfloat16)
                )
                columns.append(
                    jnp.concatenate(
                        [
                            pool_ref[
                                row_ref[j, 0, (s * heads + part * quad + h_at) * share + n]
                            ]
                            for s in range(steps)
                            for n in range(share)
                        ],
                        0,
                    )
                )
            product = jnp.dot(
                jnp.concatenate(lhs, 0), jnp.concatenate(columns, 1),
                preferred_element_type=jnp.float32,
            )
            results += [product[:both, :HEAD_SIZE], product[both:, HEAD_SIZE:]]
        return jnp.concatenate(results, 0)

    own_core = peer(2 * depth)
    own_side = peer(depth)
    piece = quad * both

    def core_copy(part, across):
        at = part * 2 + across
        return remote(
            core_out.at[at], core_in.at[at], core_send.at[at], core_recv.at[at], own_core
        )

    def side_copy(part):
        return remote(
            side_out.at[part], side_in.at[part], side_send.at[part], side_recv.at[part], own_side
        )

    def line_copy(part, ahead):
        at = part * depth + ahead
        return remote(
            line_out.at[at], line_in.at[at], line_send.at[at], line_recv.at[at],
            lax.rem(layer - ahead + depth, depth) * 4 + side * 2 + core,
        )

    def stage(part, far, across):
        first = far * 2 * depth + across * depth
        js = [first + ahead for ahead in range(depth)]
        for j in js:
            if j:
                wire_copy(part, j).wait_recv()
        return [partial(part, j) for j in js]

    def far_stage(part, across):
        for ahead, value in enumerate(stage(part, 1, across)):
            core_out[part * 2 + across, ahead * piece : (ahead + 1) * piece] = value
        core_copy(part, across).start()

    def side_stage(part):
        values = stage(part, 0, 1)
        core_copy(part, 1).wait_recv()
        for ahead, value in enumerate(values):
            span = slice(ahead * piece, (ahead + 1) * piece)
            side_out[part, span] = (value + core_in[part * 2 + 1, span]).astype(jnp.bfloat16)
        side_copy(part).start()

    def line_stage(part):
        values = stage(part, 0, 0)
        core_copy(part, 0).wait_recv()
        side_copy(part).wait_recv()
        for ahead, value in enumerate(values):
            span = slice(ahead * piece, (ahead + 1) * piece)
            value = value + core_in[part * 2, span] + side_in[part, span].astype(jnp.float32)
            if ahead:
                line_out[part * depth + ahead] = value.astype(jnp.bfloat16)
                line_copy(part, ahead).start()
            else:
                keep_ref[part * piece : (part + 1) * piece] = value

    far_stage(0, 1)
    side_stage(0)
    far_stage(0, 0)
    far_stage(1, 1)
    line_stage(0)
    side_stage(1)
    far_stage(1, 0)
    line_stage(1)

    for part in range(2):
        span = slice(part * piece, (part + 1) * piece)
        value = keep_ref[span] + fresh_ref[span]
        for ahead in range(1, depth):
            line_copy(part, ahead).wait_recv()
            value = value + line_in[part * depth + ahead].astype(jnp.float32)
        keep_ref[span] = value
    for head in range(heads):
        for g in range(group):
            at = (head * group + g) * HEAD_SIZE
            out_ref[:, at : at + HEAD_SIZE] = jnp.concatenate(
                [
                    keep_ref[head * both + s * group + g : head * both + s * group + g + 1]
                    for s in range(steps)
                ],
                0,
            ).astype(jnp.bfloat16)

    for j in range(1, holders):
        ask_copy(j).wait_send()
        for part in range(2):
            wire_copy(part, j).wait_send()
    for part in range(2):
        core_copy(part, 0).wait_send()
        core_copy(part, 1).wait_send()
        side_copy(part).wait_send()
        for ahead in range(1, depth):
            line_copy(part, ahead).wait_send()


def fused_device(
    queries, new_keys, incoming_values, key_left, right_key_factor, value_tile_store, slot_map,
    chosen, lengths,
):
    holders = lax.axis_size("store")
    steps, _, heads, picks = chosen.shape
    blocks = slot_map.shape[2]
    share = max(1, blocks // holders // 4)
    pool_here = value_tile_store.shape[0]
    group = queries.shape[2] // HEAD_SIZE // heads
    rank = key_left.shape[2]
    slots = steps * heads * share
    rows = steps * heads * group
    both = steps * group
    quad = heads // 2
    depth = holders // 4
    piece = quad * both
    half = HEAD_SIZE // 2
    tokens = blocks * BLOCK_TOKENS

    inverse = ROPE_BASE ** (-(jnp.arange(half, dtype=jnp.float32) * 2.0 / HEAD_SIZE))
    angles = (lengths[0] + jnp.arange(steps, dtype=jnp.int32)).astype(jnp.float32)[:, None] * inverse

    inverse = ROPE_BASE ** (-(np.arange(half, dtype=np.float32) * 2.0 / HEAD_SIZE))
    coarse = inverse[:, None] * (np.arange(blocks) * BLOCK_TOKENS)[None, :]
    fine = (np.arange(BLOCK_TOKENS)[:, None] * inverse[None, :])[..., None]
    constant = lambda table: jnp.asarray(table.astype(np.float32))
    wide = BLOCK_TOKENS * 64
    regroup = np.zeros((wide, wide), np.float32)
    for t in range(BLOCK_TOKENS):
        regroup[np.arange(64) * BLOCK_TOKENS + t, t * 64 + np.arange(64)] = 1.0
    spread = np.zeros((BLOCK_TOKENS, quad, share, quad, share, BLOCK_TOKENS, 2), np.float32)
    for t in range(BLOCK_TOKENS):
        for h in range(quad):
            for n in range(share):
                spread[t, h, n, h, n, t] = (1.0, -1.0)
    lines = BLOCK_TOKENS * quad * share
    spread = spread.reshape(lines, 2 * lines)

    vmem = pl.BlockSpec(memory_space=pltpu.VMEM)
    anywhere = pl.BlockSpec(memory_space=pl.ANY)
    bf16, f32 = jnp.bfloat16, jnp.float32
    dma = pltpu.SemaphoreType.DMA
    attended = pl.pallas_call(
        functools.partial(fused_kernel, share, pool_here),
        in_specs=[pl.BlockSpec(memory_space=pltpu.SMEM)] + [vmem] * 13 + [anywhere] * 3,
        out_specs=vmem,
        out_shape=jax.ShapeDtypeStruct((steps, heads * group * HEAD_SIZE), bf16),
        scratch_shapes=[
            pltpu.VMEM((rank, tokens), bf16),
            pltpu.VMEM((wide, wide), bf16),
            pltpu.VMEM((pool_here // 2, 2 * BLOCK_TOKENS, HEAD_SIZE), bf16),
            pltpu.VMEM((holders, 1, slots), jnp.int32),
            pltpu.VMEM((holders, 1, slots), jnp.int32),
            pltpu.VMEM((holders, 1, slots), jnp.int32),
            pltpu.SMEM((holders, 1, slots), jnp.int32),
            pltpu.VMEM((steps * heads, blocks), jnp.int32),
            pltpu.VMEM((heads, blocks), f32),
            pltpu.VMEM((heads, both, HEAD_SIZE), bf16),
            pltpu.VMEM((heads, 8, HEAD_SIZE), bf16),
            pltpu.VMEM((heads, 8, HEAD_SIZE), bf16),
            pltpu.VMEM((heads * HEAD_SIZE, rank), bf16),
            pltpu.VMEM((BLOCK_TOKENS, rank, blocks), bf16),
            pltpu.VMEM((BLOCK_TOKENS, half, blocks), f32),
            pltpu.VMEM((BLOCK_TOKENS, half, blocks), f32),
            pltpu.VMEM((BLOCK_TOKENS, both, blocks), f32),
            pltpu.VMEM((rows, HEAD_SIZE), f32),
            pltpu.VMEM((BLOCK_TOKENS, heads, both, holders * share), f32),
            pltpu.VMEM((2, holders, both, lines), bf16),
            pltpu.VMEM((2, holders, both, lines), bf16),
            pltpu.VMEM((4, depth * piece, HEAD_SIZE), f32),
            pltpu.VMEM((4, depth * piece, HEAD_SIZE), f32),
            pltpu.VMEM((2, depth * piece, HEAD_SIZE), bf16),
            pltpu.VMEM((2, depth * piece, HEAD_SIZE), bf16),
            pltpu.VMEM((2 * depth, piece, HEAD_SIZE), bf16),
            pltpu.VMEM((2 * depth, piece, HEAD_SIZE), bf16),
            pltpu.VMEM((rows, HEAD_SIZE), f32),
            dma((1,)), dma((1,)), dma((4 * BLOCK_TOKENS,)), dma((1,)),
            dma((holders,)), dma((holders,)), dma((2 * holders,)), dma((2 * holders,)),
            dma((4,)), dma((4,)), dma((2,)), dma((2,)), dma((2 * depth,)), dma((2 * depth,)),
        ],
        compiler_params=pltpu.CompilerParams(collective_id=0, has_side_effects=True),
        name="fused",
    )(
        lengths, jnp.cos(angles), jnp.sin(angles), queries[:, 0], new_keys[:, 0],
        incoming_values[:, 0], chosen[:, 0].reshape(steps * heads, picks), slot_map[0],
        right_key_factor[0], constant(np.cos(coarse)), constant(np.sin(coarse)),
        constant(np.cos(fine)), constant(np.sin(fine)), jnp.asarray(spread, bf16),
        key_left[0].T, jnp.asarray(regroup, bf16),
        value_tile_store.reshape(pool_here // 8, 8, -1),
    )
    return attended.reshape(steps, 1, -1)


def solution(mesh):
    in_specs = (
        P(None, ("groups", "store"), None),
        P(None, ("groups", "store"), None),
        P(None, ("groups", "store"), None),
        P(("groups", "store"), None, None),
        P(("groups", "store"), None, None),
        P(("groups", "store"), None),
        P(("groups", "store"), None, None),
        P(None, ("groups", "store"), None, None),
        P(("groups", "store")),
    )
    out_specs = P(None, ("groups", "store"), None)

    def body(*args):
        holders = mesh.shape["store"]
        blocks = args[6].shape[2]
        share = max(1, blocks // holders // 4)
        square = args[7].shape[0] * args[7].shape[2] == holders
        fits = square and share == 8 and holders == 16 and blocks % 128 == 0
        return (fused_device if fits else per_device)(*args)

    return jax.shard_map(
        body, mesh=mesh, in_specs=in_specs, out_specs=out_specs, check_vma=False
    )
```

```python
import functools

import jax
import jax.numpy as jnp
import numpy as np
from jax import lax
from jax.experimental import pallas as pl
from jax.experimental.pallas import tpu as pltpu
from jax.sharding import PartitionSpec as P

KEY_VALUE_HEADS = 8
HEAD_SIZE = 128
BLOCK_TOKENS = 8


ROPE_BASE = 500000.0


def apply_rotary(tensor, token_positions):
    half_dim = tensor.shape[-1] // 2
    inverse = ROPE_BASE ** (-(jnp.arange(half_dim, dtype=jnp.float32) * 2.0 / tensor.shape[-1]))
    angles = jnp.asarray(token_positions).astype(jnp.float32)[..., None] * inverse
    cosine = jnp.cos(angles)
    sine_vals = jnp.sin(angles)
    first_half = tensor[..., :half_dim]
    second_half = tensor[..., half_dim:]
    return jnp.concatenate(
        [
            first_half * cosine - second_half * sine_vals,
            second_half * cosine + first_half * sine_vals,
        ],
        -1,
    )


def fetch_tiles(requests, value_tile_store):
    tile_row_index = jnp.take(
        value_tile_store,
        lax.all_to_all(requests, "store", split_axis=0, concat_axis=0, tiled=True),
        axis=0,
    )
    return lax.all_to_all(tile_row_index, "store", split_axis=0, concat_axis=0, tiled=True)


def build_requests(flat_idx, inside, total):
    buffer = jnp.zeros((total,), jnp.int32)
    return buffer.at[flat_idx.reshape(-1)].set(inside.reshape(-1))


def attend_row(
    query_full,
    incoming_keys_full,
    incoming_values_full,
    left_rows,
    right_factor_rows,
    block_numbers,
    tile_row_index,
    length,
    step_index,
):
    query_group_size = query_full.shape[-1] // HEAD_SIZE // KEY_VALUE_HEADS
    every_head = query_group_size * KEY_VALUE_HEADS
    selected_count = block_numbers.shape[1]
    score_scale = HEAD_SIZE ** (-0.5)
    right_factor_heads = right_factor_rows.reshape(
        right_factor_rows.shape[0], KEY_VALUE_HEADS, HEAD_SIZE
    )
    token_positions = (
        block_numbers[:, :, None] * BLOCK_TOKENS + jnp.arange(BLOCK_TOKENS, dtype=jnp.int32)
    ).reshape(KEY_VALUE_HEADS, selected_count * BLOCK_TOKENS)
    picked = left_rows[token_positions]
    raw_keys = jnp.einsum(
        "htr,rhd->htd", picked, right_factor_heads, preferred_element_type=jnp.float32
    )
    cache_keys = apply_rotary(raw_keys, token_positions).astype(jnp.bfloat16)
    rotated_query = apply_rotary(
        query_full[step_index].reshape(every_head, HEAD_SIZE).astype(jnp.float32),
        length + step_index,
    ).astype(jnp.bfloat16)
    current_position = (length + jnp.arange(step_index + 1, dtype=jnp.int32))[:, None]
    current_keys = apply_rotary(
        incoming_keys_full[: step_index + 1]
        .reshape(step_index + 1, KEY_VALUE_HEADS, HEAD_SIZE)
        .astype(jnp.float32),
        current_position,
    ).astype(jnp.bfloat16)
    current_keys = jnp.transpose(current_keys, (1, 0, 2))
    current_values = jnp.transpose(
        incoming_values_full[: step_index + 1].reshape(step_index + 1, KEY_VALUE_HEADS, HEAD_SIZE),
        (1, 0, 2),
    )
    local_values = tile_row_index.reshape(KEY_VALUE_HEADS, selected_count * BLOCK_TOKENS, HEAD_SIZE)
    grouped_queries = rotated_query.reshape(KEY_VALUE_HEADS, query_group_size, HEAD_SIZE)
    cache_scores = (
        jnp.einsum("hgd,htd->hgt", grouped_queries, cache_keys, preferred_element_type=jnp.float32)
        * score_scale
    )
    inside_len = token_positions < length
    cache_scores = jnp.where(inside_len[:, None, :], cache_scores, -jnp.inf)
    fresh_scores = (
        jnp.einsum(
            "hgd,hnd->hgn", grouped_queries, current_keys, preferred_element_type=jnp.float32
        )
        * score_scale
    )
    highest = jnp.maximum(
        jnp.max(cache_scores, -1, keepdims=True), jnp.max(fresh_scores, -1, keepdims=True)
    )
    cache_exp = jnp.exp(cache_scores - highest)
    fresh_exp = jnp.exp(fresh_scores - highest)
    denominator = jnp.sum(cache_exp, -1, keepdims=True) + jnp.sum(fresh_exp, -1, keepdims=True)
    cache_weight = (cache_exp / denominator).astype(jnp.bfloat16)
    fresh_weight = (fresh_exp / denominator).astype(jnp.bfloat16)
    attended = jnp.einsum(
        "hgt,htd->hgd", cache_weight, local_values, preferred_element_type=jnp.float32
    )
    attended = attended + jnp.einsum(
        "hgn,hnd->hgd", fresh_weight, current_values, preferred_element_type=jnp.float32
    )
    return attended.reshape(every_head * HEAD_SIZE).astype(jnp.bfloat16)


def per_device(
    queries,
    new_keys,
    incoming_values,
    key_left,
    right_key_factor,
    value_tile_store,
    slot_map,
    chosen,
    lengths,
):
    nstore = lax.axis_size("store")
    local_rows = key_left.shape[0]
    nchunk = slot_map.shape[2]
    step_count = chosen.shape[0]
    selected_count = chosen.shape[3]
    keeper_share = max(1, nchunk // nstore // 4)
    tile_limit = local_rows * KEY_VALUE_HEADS * keeper_share
    pool_here = value_tile_store.shape[0]
    slot_numbers = jnp.take_along_axis(
        jnp.broadcast_to(slot_map[None], (step_count,) + slot_map.shape), chosen, axis=3
    )
    tile_keeper = slot_numbers // pool_here
    inside = slot_numbers % pool_here
    matched = tile_keeper[..., :, None] == tile_keeper[..., None, :]
    earlier = jnp.arange(selected_count)[None, :] < jnp.arange(selected_count)[:, None]
    order_in = jnp.sum(jnp.logical_and(matched, earlier), -1)
    row_head = (
        jnp.arange(local_rows, dtype=jnp.int32)[:, None, None] * KEY_VALUE_HEADS
        + jnp.arange(KEY_VALUE_HEADS, dtype=jnp.int32)[None, :, None]
    )
    position = row_head * keeper_share + order_in
    tiles_all = []
    slot_span = step_count * tile_limit
    flat_idx = (
        tile_keeper * slot_span
        + jnp.arange(step_count, dtype=jnp.int32)[:, None, None, None] * tile_limit
        + position
    )
    requests = build_requests(flat_idx, inside, nstore * slot_span).reshape(nstore, slot_span)
    received = fetch_tiles(requests, value_tile_store).reshape(nstore * slot_span, -1)
    for step_index in range(step_count):
        tiles_all.append(received[flat_idx[step_index]])
    results = []
    for step_index in range(step_count):
        per_rows = [
            attend_row(
                queries[:, 0],
                new_keys[:, 0],
                incoming_values[:, 0],
                key_left[0],
                right_key_factor[0],
                chosen[step_index, 0],
                tiles_all[step_index][0],
                lengths[0],
                step_index,
            )
        ]
        results.append(jnp.stack(per_rows))
    return jnp.stack(results)


def fused_kernel(
    share, pool_here,
    length_ref, pick_ref, turn_cos_ref, turn_sin_ref, query_ref, new_key_ref, new_value_ref,
    chosen_ref, slot_ref, right_hbm, table_hbm, expand_hbm, spread_hbm, regroup_hbm, left_hbm,
    pool_hbm,
    out_ref,
    left_ref, right_ref, expand_ref, spread_ref, regroup_ref, pool_ref, block_ref,
    send_ref, ask_ref, asked_ref, row_ref, place_ref, sign_ref, bound_ref,
    rotated_ref, fresh_score_ref, fresh_value_ref, factor_ref, score_ref, fresh_ref,
    routed_ref, wire_ref, got_ref,
    core_out, core_in, side_out, side_in, line_out, line_in, keep_ref,
    in_sem, pool_sem, row_sem, ask_send, ask_recv, wire_send, wire_recv,
    core_send, core_recv, side_send, side_recv, line_send, line_recv,
):
    me = lax.axis_index("store")
    holders = send_ref.shape[0]
    depth = holders // 4
    rows, picks = chosen_ref.shape
    heads, blocks = slot_ref.shape
    steps = rows // heads
    rank = left_hbm.shape[0]
    deep = left_ref.shape[0]
    group = query_ref.shape[1] // HEAD_SIZE // heads
    both = steps * group
    half = HEAD_SIZE // 2
    quad = heads // 2
    scale = HEAD_SIZE ** (-0.5)
    core, side, layer = lax.rem(me, 2), lax.rem(me // 2, 2), me // 4

    def peer(j):
        far, across, ahead = j // (2 * depth), j // depth % 2, j % depth
        return (
            lax.rem(layer + ahead, depth) * 4
            + (1 - side if across else side) * 2
            + (1 - core if far else core)
        )

    def remote(src, dst, send, recv, target):
        return pltpu.make_async_remote_copy(
            src_ref=src, dst_ref=dst, send_sem=send, recv_sem=recv,
            device_id={"store": target}, device_id_type=pl.DeviceIdType.MESH,
        )

    barrier = pltpu.get_barrier_semaphore()

    def greet(k, _):
        pl.semaphore_signal(
            barrier, inc=1, device_id={"store": lax.rem(me + k, holders)},
            device_id_type=pl.DeviceIdType.MESH,
        )
        return 0

    lax.fori_loop(1, holders, greet, 0)

    loads = [
        pltpu.make_async_copy(src, dst, in_sem.at[at])
        for at, (src, dst) in enumerate(
            (
                (left_hbm, left_ref.at[pl.ds(0, rank)]),
                (right_hbm, right_ref),
                (table_hbm, block_ref.at[:, :, pl.ds(deep, 2 * HEAD_SIZE)]),
                (expand_hbm, expand_ref),
                (regroup_hbm, regroup_ref),
                (spread_hbm, spread_ref),
            )
        )
    ]
    for copy in loads:
        copy.start()
    octets = pool_here // 8
    pool_copies = [
        pltpu.make_async_copy(
            pool_hbm.at[:, pl.ds(2 * q, 2), pl.ds(HEAD_SIZE * t, HEAD_SIZE)],
            pool_ref.at[pl.ds(q * octets, octets), pl.ds(2 * t, 2), :],
            pool_sem.at[q * BLOCK_TOKENS + t],
        )
        for q in range(4)
        for t in range(BLOCK_TOKENS)
    ]
    for copy in pool_copies:
        copy.start()

    total = holders * share
    length = length_ref[0]
    lane_at = lax.broadcasted_iota(jnp.int32, (heads, total), 1)
    first_step = lane_at < picks
    chosen = jnp.concatenate([chosen_ref[s * heads : (s + 1) * heads] for s in range(steps)], 1)
    slot = jnp.zeros((heads, total), jnp.int32)
    for at in range(0, blocks, total):
        found = jnp.take_along_axis(slot_ref[:, at : at + total], chosen & (total - 1), axis=1)
        slot = jnp.where(chosen // total == at // total, found, slot)
    if pool_here & (pool_here - 1) == 0:
        keeper = slot >> (pool_here.bit_length() - 1)
        inside = slot & (pool_here - 1)
    else:
        keeper = lax.div(slot, jnp.full_like(slot, pool_here))
        inside = slot - keeper * pool_here
    sign_ref[...] = (1 - 2 * (inside & 1)).astype(jnp.float32)
    inside = ((inside >> 1) & 3) * octets + (inside >> 3)
    before_row = lax.broadcasted_iota(jnp.int32, (total, total), 0)
    before_lane = lax.broadcasted_iota(jnp.int32, (total, total), 1)
    before = jnp.where(
        jnp.logical_and(before_row < before_lane, before_row // picks == before_lane // picks),
        1.0, 0.0,
    ).astype(jnp.bfloat16)
    mine = [jnp.where(keeper == holder, 1.0, 0.0) for holder in range(holders)]
    counts = jnp.dot(
        jnp.concatenate(mine, 0).astype(jnp.bfloat16), before, preferred_element_type=jnp.float32
    )
    order = jnp.zeros((heads, total), jnp.float32)
    for holder in range(holders):
        order = order + mine[holder] * counts[holder * heads : (holder + 1) * heads]
    place = keeper * share + order.astype(jnp.int32)
    place_ref[...] = place
    digits = []
    for s in range(steps):
        for shift in (0, 8, 16):
            digit = ((inside >> shift) & 255).astype(jnp.float32)
            digits.append(jnp.where(first_step == (s == 0), digit, 0.0))
    slot_at = before_row
    moved = [None] * rows
    for head in range(heads):
        lines = jnp.concatenate(
            [digit[head : head + 1] for digit in digits]
            + [jnp.zeros((8 - len(digits), total), jnp.float32)], 0
        ).astype(jnp.bfloat16)
        table = jnp.where(place[head : head + 1] == slot_at, 1.0, 0.0).astype(jnp.bfloat16)
        found = lax.dot_general(
            lines, table, (((1,), (1,)), ((), ())), preferred_element_type=jnp.float32
        ).astype(jnp.int32)
        for s in range(steps):
            row = s * heads + head
            whole = found[3 * s : 3 * s + 1] + found[3 * s + 1 : 3 * s + 2] * 256
            whole = whole + found[3 * s + 2 : 3 * s + 3] * 65536
            moved[row] = pltpu.roll(whole, row * share, 1) if row else whole
    moved = jnp.concatenate(moved, 0)
    own_lanes = (
        lax.broadcasted_iota(jnp.int32, (rows, total), 1) // share
        == lax.broadcasted_iota(jnp.int32, (rows, total), 0)
    )
    for holder in range(holders):
        turned = pltpu.roll(moved, total - holder * share, 1) if holder else moved
        send_ref[holder] = jnp.sum(jnp.where(own_lanes, turned, 0), 0, keepdims=True)

    def ask_copy(j):
        target = peer(j)
        return remote(
            send_ref.at[target], ask_ref.at[j], ask_send.at[j], ask_recv.at[j], target
        )

    far_first = sorted(
        range(1, holders), key=lambda j: (-(min(j % depth, depth - j % depth)), -j)
    )
    pl.semaphore_wait(barrier, holders - 1)
    for j in far_first:
        ask_copy(j).start()
    ask_ref[0] = send_ref[me]

    spin_cos = [
        jnp.broadcast_to(
            jnp.concatenate([turn_cos_ref[s : s + 1]] * 2, 1), (group, HEAD_SIZE)
        )
        for s in range(steps)
    ]
    spin_sin = [
        jnp.broadcast_to(
            jnp.concatenate([-turn_sin_ref[s : s + 1], turn_sin_ref[s : s + 1]], 1),
            (group, HEAD_SIZE),
        )
        for s in range(steps)
    ]
    query_all = query_ref[...].astype(jnp.float32)
    key_all = new_key_ref[...].astype(jnp.float32)
    value_all = new_value_ref[...].astype(jnp.float32)
    fresh_cos = jnp.concatenate([spin_cos[s][:1] for s in range(steps)] + [spin_cos[0][: 8 - steps]], 0)
    fresh_sin = jnp.concatenate([spin_sin[s][:1] for s in range(steps)] + [spin_sin[0][: 8 - steps]], 0)
    both_cos = jnp.concatenate(spin_cos, 0)
    both_sin = jnp.concatenate(spin_sin, 0)
    empty = jnp.zeros((8 - steps, HEAD_SIZE), jnp.float32)
    fresh_keep = (
        lax.broadcasted_iota(jnp.int32, (both, 8), 1)
        <= lax.broadcasted_iota(jnp.int32, (both, 8), 0) // group
    )
    for head in range(heads):
        lanes = slice(head * HEAD_SIZE, (head + 1) * HEAD_SIZE)
        flat = jnp.concatenate(
            [
                query_all[s : s + 1, (head * group + g) * HEAD_SIZE : (head * group + g + 1) * HEAD_SIZE]
                for s in range(steps)
                for g in range(group)
            ],
            0,
        )
        query = (flat * both_cos + pltpu.roll(flat, half, 1) * both_sin).astype(jnp.bfloat16)
        for s in range(steps):
            rotated_ref[s * heads + head] = query[s * group : (s + 1) * group]
        flat = jnp.concatenate([key_all[:, lanes], empty], 0)
        fresh_key = (flat * fresh_cos + pltpu.roll(flat, half, 1) * fresh_sin).astype(jnp.bfloat16)
        fresh = lax.dot_general(
            query, fresh_key, (((1,), (1,)), ((), ())), preferred_element_type=jnp.float32
        ) * scale
        fresh_score_ref[head] = jnp.where(fresh_keep, fresh, -jnp.inf)
        fresh_value_ref[head] = jnp.concatenate([value_all[:, lanes], empty], 0).astype(
            jnp.bfloat16
        )
    left_ref[rank:, :] = jnp.zeros((deep - rank, left_ref.shape[1]), jnp.bfloat16)
    factor_ref[:, rank:, :] = jnp.zeros((heads, deep - rank, HEAD_SIZE), jnp.bfloat16)
    loads[1].wait()
    for head in range(heads):
        factor_ref[head, :rank, :] = right_ref[:, head * HEAD_SIZE : (head + 1) * HEAD_SIZE]
    loads[3].wait()
    remaining = jnp.clip(length - chosen * BLOCK_TOKENS, 0, BLOCK_TOKENS)
    bound_ref[...] = jnp.dot(
        remaining.astype(jnp.float32).astype(jnp.bfloat16), expand_ref[...],
        preferred_element_type=jnp.float32,
    )
    same = jnp.where(
        lax.broadcasted_iota(jnp.int32, (deep, deep), 0)
        == lax.broadcasted_iota(jnp.int32, (deep, deep), 1),
        1.0, 0.0,
    ).astype(jnp.bfloat16)
    loads[0].wait()
    turned_blocks = deep // BLOCK_TOKENS
    for at in range(0, left_ref.shape[1], deep):
        turned = lax.dot_general(
            same, left_ref[:, at : at + deep], (((1,), (1,)), ((), ())),
            preferred_element_type=jnp.float32,
        )
        first = at // BLOCK_TOKENS
        block_ref[first : first + turned_blocks, :, :deep] = turned.reshape(
            turned_blocks, BLOCK_TOKENS, deep
        )
    loads[2].wait()

    token_at = (
        lax.broadcasted_iota(jnp.int32, (group, picks * BLOCK_TOKENS), 1) % BLOCK_TOKENS
    ).astype(jnp.float32)
    low_half = lax.broadcasted_iota(jnp.int32, (group, total), 1) < picks

    def one_row(row):
        head = row // steps
        s = row - head * steps
        at = s * heads + head
        found = [block_ref[pick_ref[at, pick]] for pick in range(picks)]
        raw = jnp.dot(
            jnp.concatenate([value[:, :deep] for value in found], 0).astype(jnp.bfloat16),
            factor_ref[head], preferred_element_type=jnp.float32,
        )
        cosine = jnp.concatenate([value[:, deep : deep + HEAD_SIZE] for value in found], 0)
        sine = jnp.concatenate([value[:, deep + HEAD_SIZE :] for value in found], 0)
        keys = (raw * cosine + pltpu.roll(raw, half, 1) * sine).astype(jnp.bfloat16)
        score_ref[row] = lax.dot_general(
            rotated_ref[at], keys, (((1,), (1,)), ((), ())), preferred_element_type=jnp.float32
        )

    def key_rows(at, _):
        for n in range(2):
            one_row(at * 2 + n)
        return 0

    def weigh(part):
        weights = []
        for head in range(part * quad, (part + 1) * quad):
            fresh_weights = []
            for s in range(steps):
                bound = jnp.broadcast_to(
                    bound_ref[head : head + 1, s * picks * BLOCK_TOKENS : (s + 1) * picks * BLOCK_TOKENS],
                    token_at.shape,
                )
                scores = jnp.where(token_at < bound, score_ref[head * steps + s] * scale, -jnp.inf)
                fresh = fresh_score_ref[head, s * group : (s + 1) * group]
                highest = jnp.maximum(
                    jnp.max(scores, -1, keepdims=True), jnp.max(fresh, -1, keepdims=True)
                )
                power = jnp.exp(scores - highest)
                fresh_power = jnp.exp(fresh - highest)
                inverse = 1.0 / (
                    jnp.sum(power, -1, keepdims=True) + jnp.sum(fresh_power, -1, keepdims=True)
                )
                weights.append(power * inverse)
                fresh_weights.append(fresh_power * inverse)
            fresh_ref[head * both : (head + 1) * both] = jnp.dot(
                jnp.concatenate(fresh_weights, 0).astype(jnp.bfloat16), fresh_value_ref[head],
                preferred_element_type=jnp.float32,
            )
        grouped = jnp.dot(
            jnp.concatenate(weights, 0).astype(jnp.bfloat16), regroup_ref[...],
            preferred_element_type=jnp.float32,
        )
        for h in range(quad):
            head = part * quad + h
            lines = []
            for s in range(steps):
                line = grouped[(h * steps + s) * group : (h * steps + s + 1) * group]
                for t in range(BLOCK_TOKENS):
                    value = line[:, t // 2 * total : (t // 2 + 1) * total]
                    if t % 2 != s:
                        value = pltpu.roll(value, picks, 1)
                    lines.append(
                        jnp.where(low_half, value, 0.0) if s == 0 else jnp.where(low_half, 0.0, value)
                    )
            table = jnp.where(
                place_ref[head : head + 1] == slot_at,
                jnp.broadcast_to(sign_ref[head : head + 1], (total, total)), 0.0,
            ).astype(jnp.bfloat16)
            routed = lax.dot_general(
                jnp.concatenate(lines, 0).astype(jnp.bfloat16), table, (((1,), (1,)), ((), ())),
                preferred_element_type=jnp.float32,
            )
            for s in range(steps):
                for t in range(BLOCK_TOKENS):
                    at = (s * BLOCK_TOKENS + t) * group
                    routed_ref[t, h, s * group : (s + 1) * group] = routed[at : at + group]

    lane = lax.broadcasted_iota(jnp.int32, (both, total), 1) // share
    middle_t = BLOCK_TOKENS // 2

    def wire_copy(part, j):
        target = peer(j)
        return remote(
            wire_ref.at[part, target], got_ref.at[part, j],
            wire_send.at[part * holders + j], wire_recv.at[part * holders + j], target,
        )

    loads[4].wait()
    for part in range(2):
        lax.fori_loop(part * quad * steps // 2, (part + 1) * quad * steps // 2, key_rows, 0)
        weigh(part)
        if part == 0:
            loads[5].wait()
        for upper in range(2):
            cells = [
                routed_ref[upper * middle_t + t, h]
                for t in range(middle_t)
                for h in range(quad)
            ]
            step = 1
            while step < holders:
                low_side = lane // step % 2 == 0
                turned = list(cells)
                for at in range(holders):
                    if at // step % 2 == 0:
                        a, b = cells[at], cells[at + step]
                        turned[at] = jnp.where(
                            low_side, a, pltpu.roll(b, step * share, 1)
                        )
                        turned[at + step] = jnp.where(
                            low_side, pltpu.roll(a, total - step * share, 1), b
                        )
                cells = turned
                step *= 2
            for holder in range(holders):
                wire_ref[part, holder, :, upper * total : (upper + 1) * total] = cells[
                    holder
                ].astype(jnp.bfloat16)
        for j in far_first:
            wire_copy(part, j).start()

    for j in range(1, holders):
        ask_copy(j).wait_recv()
    asked_ref[...] = jnp.clip(ask_ref[...], 0, pool_ref.shape[0] - 1)
    row_copy = pltpu.make_async_copy(asked_ref, row_ref, row_sem.at[0])
    row_copy.start()
    row_copy.wait()
    for copy in pool_copies:
        copy.wait()

    early = lax.broadcasted_iota(jnp.int32, (both, HEAD_SIZE), 0) < group

    def partial(part, j):
        if j:
            arrived = got_ref[part, j]
        else:
            arrived = wire_ref[part, me]
        weight = jnp.maximum(
            jnp.dot(arrived, spread_ref[...], preferred_element_type=jnp.float32), 0.0
        )
        results = []
        for h in range(0, quad, 2):
            lhs, columns = [], []
            for h_at in (h, h + 1):
                own = weight[:, h_at * HEAD_SIZE : (h_at + 1) * HEAD_SIZE]
                lhs.append(
                    jnp.concatenate(
                        [jnp.where(early, own, 0.0), jnp.where(early, 0.0, own)], 1
                    ).astype(jnp.bfloat16)
                )
                columns.append(
                    jnp.concatenate(
                        [
                            pool_ref[
                                row_ref[j, 0, (s * heads + part * quad + h_at) * share + n]
                            ]
                            for s in range(steps)
                            for n in range(share)
                        ],
                        0,
                    )
                )
            product = jnp.dot(
                jnp.concatenate(lhs, 0), jnp.concatenate(columns, 1),
                preferred_element_type=jnp.float32,
            )
            results += [product[:both, :HEAD_SIZE], product[both:, HEAD_SIZE:]]
        return jnp.concatenate(results, 0)

    own_core = peer(2 * depth)
    own_side = peer(depth)
    piece = quad * both

    def core_copy(part, across):
        at = part * 2 + across
        return remote(
            core_out.at[at], core_in.at[at], core_send.at[at], core_recv.at[at], own_core
        )

    def side_copy(part):
        return remote(
            side_out.at[part], side_in.at[part], side_send.at[part], side_recv.at[part], own_side
        )

    def line_copy(part, ahead):
        at = part * depth + ahead
        return remote(
            line_out.at[at], line_in.at[at], line_send.at[at], line_recv.at[at],
            lax.rem(layer - ahead + depth, depth) * 4 + side * 2 + core,
        )

    def stage(part, far, across):
        first = far * 2 * depth + across * depth
        js = [first + ahead for ahead in range(depth)]
        for j in js:
            if j:
                wire_copy(part, j).wait_recv()
        return [partial(part, j) for j in js]

    def far_stage(part, across):
        for ahead, value in enumerate(stage(part, 1, across)):
            core_out[part * 2 + across, ahead * piece : (ahead + 1) * piece] = value
        core_copy(part, across).start()

    def side_stage(part):
        values = stage(part, 0, 1)
        core_copy(part, 1).wait_recv()
        for ahead, value in enumerate(values):
            span = slice(ahead * piece, (ahead + 1) * piece)
            side_out[part, span] = (value + core_in[part * 2 + 1, span]).astype(jnp.bfloat16)
        side_copy(part).start()

    def line_stage(part):
        values = stage(part, 0, 0)
        core_copy(part, 0).wait_recv()
        side_copy(part).wait_recv()
        for ahead, value in enumerate(values):
            span = slice(ahead * piece, (ahead + 1) * piece)
            value = value + core_in[part * 2, span] + side_in[part, span].astype(jnp.float32)
            if ahead:
                line_out[part * depth + ahead] = value.astype(jnp.bfloat16)
                line_copy(part, ahead).start()
            else:
                keep_ref[part * piece : (part + 1) * piece] = value

    far_stage(0, 1)
    side_stage(0)
    far_stage(0, 0)
    far_stage(1, 1)
    line_stage(0)
    side_stage(1)
    far_stage(1, 0)
    line_stage(1)

    for part in range(2):
        span = slice(part * piece, (part + 1) * piece)
        value = keep_ref[span] + fresh_ref[span]
        for ahead in range(1, depth):
            line_copy(part, ahead).wait_recv()
            value = value + line_in[part * depth + ahead].astype(jnp.float32)
        keep_ref[span] = value
    for head in range(heads):
        for g in range(group):
            at = (head * group + g) * HEAD_SIZE
            out_ref[:, at : at + HEAD_SIZE] = jnp.concatenate(
                [
                    keep_ref[head * both + s * group + g : head * both + s * group + g + 1]
                    for s in range(steps)
                ],
                0,
            ).astype(jnp.bfloat16)

    for j in range(1, holders):
        ask_copy(j).wait_send()
        for part in range(2):
            wire_copy(part, j).wait_send()
    for part in range(2):
        core_copy(part, 0).wait_send()
        core_copy(part, 1).wait_send()
        side_copy(part).wait_send()
        for ahead in range(1, depth):
            line_copy(part, ahead).wait_send()


def fused_device(
    queries, new_keys, incoming_values, key_left, right_key_factor, value_tile_store, slot_map,
    chosen, lengths,
):
    holders = lax.axis_size("store")
    steps, _, heads, picks = chosen.shape
    blocks = slot_map.shape[2]
    share = max(1, blocks // holders // 4)
    pool_here = value_tile_store.shape[0]
    group = queries.shape[2] // HEAD_SIZE // heads
    rank = key_left.shape[2]
    slots = steps * heads * share
    rows = steps * heads * group
    both = steps * group
    quad = heads // 2
    depth = holders // 4
    piece = quad * both
    half = HEAD_SIZE // 2
    tokens = blocks * BLOCK_TOKENS

    inverse = ROPE_BASE ** (-(jnp.arange(half, dtype=jnp.float32) * 2.0 / HEAD_SIZE))
    angles = (lengths[0] + jnp.arange(steps, dtype=jnp.int32)).astype(jnp.float32)[:, None] * inverse

    turns = np.arange(tokens)[:, None] * ROPE_BASE ** (-(np.arange(half) * 2.0 / HEAD_SIZE))[None]
    cosine, sine = np.cos(turns), np.sin(turns)
    table = np.concatenate([cosine, cosine, -sine, sine], 1).astype(np.float32)
    table = jnp.asarray(table.reshape(blocks, BLOCK_TOKENS, 2 * HEAD_SIZE))
    expand = np.repeat(np.eye(steps * picks, dtype=np.float32), BLOCK_TOKENS, 1)
    deep = -(-rank // 128) * 128
    wide = BLOCK_TOKENS * 64
    regroup = np.zeros((wide, wide), np.float32)
    for t in range(BLOCK_TOKENS):
        regroup[np.arange(64) * BLOCK_TOKENS + t, t * 64 + np.arange(64)] = 1.0
    spread = np.zeros((BLOCK_TOKENS, quad, share, quad, share, BLOCK_TOKENS, 2), np.float32)
    for t in range(BLOCK_TOKENS):
        for h in range(quad):
            for n in range(share):
                spread[t, h, n, h, n, t] = (1.0, -1.0)
    lines = BLOCK_TOKENS * quad * share
    spread = spread.reshape(lines, 2 * lines)

    vmem = pl.BlockSpec(memory_space=pltpu.VMEM)
    anywhere = pl.BlockSpec(memory_space=pl.ANY)
    bf16, f32 = jnp.bfloat16, jnp.float32
    dma = pltpu.SemaphoreType.DMA
    attended = pl.pallas_call(
        functools.partial(fused_kernel, share, pool_here),
        in_specs=[pl.BlockSpec(memory_space=pltpu.SMEM)] * 2 + [vmem] * 7 + [anywhere] * 7,
        out_specs=vmem,
        out_shape=jax.ShapeDtypeStruct((steps, heads * group * HEAD_SIZE), bf16),
        scratch_shapes=[
            pltpu.VMEM((deep, tokens), bf16),
            pltpu.VMEM((rank, heads * HEAD_SIZE), bf16),
            pltpu.VMEM((steps * picks, steps * picks * BLOCK_TOKENS), bf16),
            pltpu.VMEM((lines, 2 * lines), bf16),
            pltpu.VMEM((wide, wide), bf16),
            pltpu.VMEM((pool_here // 2, 2 * BLOCK_TOKENS, HEAD_SIZE), bf16),
            pltpu.VMEM((blocks, BLOCK_TOKENS, deep + 2 * HEAD_SIZE), f32),
            pltpu.VMEM((holders, 1, slots), jnp.int32),
            pltpu.VMEM((holders, 1, slots), jnp.int32),
            pltpu.VMEM((holders, 1, slots), jnp.int32),
            pltpu.SMEM((holders, 1, slots), jnp.int32),
            pltpu.VMEM((heads, steps * picks), jnp.int32),
            pltpu.VMEM((heads, steps * picks), f32),
            pltpu.VMEM((heads, steps * picks * BLOCK_TOKENS), f32),
            pltpu.VMEM((steps * heads, group, HEAD_SIZE), bf16),
            pltpu.VMEM((heads, both, 8), f32),
            pltpu.VMEM((heads, 8, HEAD_SIZE), bf16),
            pltpu.VMEM((heads, deep, HEAD_SIZE), bf16),
            pltpu.VMEM((heads * steps, group, picks * BLOCK_TOKENS), f32),
            pltpu.VMEM((rows, HEAD_SIZE), f32),
            pltpu.VMEM((BLOCK_TOKENS, quad, both, holders * share), f32),
            pltpu.VMEM((2, holders, both, lines), bf16),
            pltpu.VMEM((2, holders, both, lines), bf16),
            pltpu.VMEM((4, depth * piece, HEAD_SIZE), f32),
            pltpu.VMEM((4, depth * piece, HEAD_SIZE), f32),
            pltpu.VMEM((2, depth * piece, HEAD_SIZE), bf16),
            pltpu.VMEM((2, depth * piece, HEAD_SIZE), bf16),
            pltpu.VMEM((2 * depth, piece, HEAD_SIZE), bf16),
            pltpu.VMEM((2 * depth, piece, HEAD_SIZE), bf16),
            pltpu.VMEM((rows, HEAD_SIZE), f32),
            dma((6,)), dma((4 * BLOCK_TOKENS,)), dma((1,)),
            dma((holders,)), dma((holders,)), dma((2 * holders,)), dma((2 * holders,)),
            dma((4,)), dma((4,)), dma((2,)), dma((2,)), dma((2 * depth,)), dma((2 * depth,)),
        ],
        compiler_params=pltpu.CompilerParams(collective_id=0, has_side_effects=True),
        name="fused",
    )(
        lengths, chosen[:, 0].reshape(steps * heads, picks), jnp.cos(angles), jnp.sin(angles),
        queries[:, 0], new_keys[:, 0], incoming_values[:, 0],
        chosen[:, 0].reshape(steps * heads, picks), slot_map[0],
        right_key_factor[0], table, jnp.asarray(expand, bf16), jnp.asarray(spread, bf16),
        jnp.asarray(regroup, bf16), key_left[0].T,
        value_tile_store.reshape(pool_here // 8, 8, -1),
    )
    return attended.reshape(steps, 1, -1)


def solution(mesh):
    in_specs = (
        P(None, ("groups", "store"), None),
        P(None, ("groups", "store"), None),
        P(None, ("groups", "store"), None),
        P(("groups", "store"), None, None),
        P(("groups", "store"), None, None),
        P(("groups", "store"), None),
        P(("groups", "store"), None, None),
        P(None, ("groups", "store"), None, None),
        P(("groups", "store")),
    )
    out_specs = P(None, ("groups", "store"), None)

    def body(*args):
        holders = mesh.shape["store"]
        blocks = args[6].shape[2]
        share = max(1, blocks // holders // 4)
        square = args[7].shape[0] * args[7].shape[2] == holders
        packed = args[7].shape[0] * args[7].shape[3] == holders * share
        fits = square and packed and share == 8 and holders == 16 and blocks % 128 == 0
        return (fused_device if fits else per_device)(*args)

    return jax.shard_map(
        body, mesh=mesh, in_specs=in_specs, out_specs=out_specs, check_vma=False
    )
```

```python
import functools

import jax
import jax.numpy as jnp
import numpy as np
from jax import lax
from jax.experimental import pallas as pl
from jax.experimental.pallas import tpu as pltpu
from jax.sharding import PartitionSpec as P

KEY_VALUE_HEADS = 8
HEAD_SIZE = 128
BLOCK_TOKENS = 8


ROPE_BASE = 500000.0


def apply_rotary(tensor, token_positions):
    half_dim = tensor.shape[-1] // 2
    inverse = ROPE_BASE ** (-(jnp.arange(half_dim, dtype=jnp.float32) * 2.0 / tensor.shape[-1]))
    angles = jnp.asarray(token_positions).astype(jnp.float32)[..., None] * inverse
    cosine = jnp.cos(angles)
    sine_vals = jnp.sin(angles)
    first_half = tensor[..., :half_dim]
    second_half = tensor[..., half_dim:]
    return jnp.concatenate(
        [
            first_half * cosine - second_half * sine_vals,
            second_half * cosine + first_half * sine_vals,
        ],
        -1,
    )


def fetch_tiles(requests, value_tile_store):
    tile_row_index = jnp.take(
        value_tile_store,
        lax.all_to_all(requests, "store", split_axis=0, concat_axis=0, tiled=True),
        axis=0,
    )
    return lax.all_to_all(tile_row_index, "store", split_axis=0, concat_axis=0, tiled=True)


def build_requests(flat_idx, inside, total):
    buffer = jnp.zeros((total,), jnp.int32)
    return buffer.at[flat_idx.reshape(-1)].set(inside.reshape(-1))


def attend_row(
    query_full,
    incoming_keys_full,
    incoming_values_full,
    left_rows,
    right_factor_rows,
    block_numbers,
    tile_row_index,
    length,
    step_index,
):
    query_group_size = query_full.shape[-1] // HEAD_SIZE // KEY_VALUE_HEADS
    every_head = query_group_size * KEY_VALUE_HEADS
    selected_count = block_numbers.shape[1]
    score_scale = HEAD_SIZE ** (-0.5)
    right_factor_heads = right_factor_rows.reshape(
        right_factor_rows.shape[0], KEY_VALUE_HEADS, HEAD_SIZE
    )
    token_positions = (
        block_numbers[:, :, None] * BLOCK_TOKENS + jnp.arange(BLOCK_TOKENS, dtype=jnp.int32)
    ).reshape(KEY_VALUE_HEADS, selected_count * BLOCK_TOKENS)
    picked = left_rows[token_positions]
    raw_keys = jnp.einsum(
        "htr,rhd->htd", picked, right_factor_heads, preferred_element_type=jnp.float32
    )
    cache_keys = apply_rotary(raw_keys, token_positions).astype(jnp.bfloat16)
    rotated_query = apply_rotary(
        query_full[step_index].reshape(every_head, HEAD_SIZE).astype(jnp.float32),
        length + step_index,
    ).astype(jnp.bfloat16)
    current_position = (length + jnp.arange(step_index + 1, dtype=jnp.int32))[:, None]
    current_keys = apply_rotary(
        incoming_keys_full[: step_index + 1]
        .reshape(step_index + 1, KEY_VALUE_HEADS, HEAD_SIZE)
        .astype(jnp.float32),
        current_position,
    ).astype(jnp.bfloat16)
    current_keys = jnp.transpose(current_keys, (1, 0, 2))
    current_values = jnp.transpose(
        incoming_values_full[: step_index + 1].reshape(step_index + 1, KEY_VALUE_HEADS, HEAD_SIZE),
        (1, 0, 2),
    )
    local_values = tile_row_index.reshape(KEY_VALUE_HEADS, selected_count * BLOCK_TOKENS, HEAD_SIZE)
    grouped_queries = rotated_query.reshape(KEY_VALUE_HEADS, query_group_size, HEAD_SIZE)
    cache_scores = (
        jnp.einsum("hgd,htd->hgt", grouped_queries, cache_keys, preferred_element_type=jnp.float32)
        * score_scale
    )
    inside_len = token_positions < length
    cache_scores = jnp.where(inside_len[:, None, :], cache_scores, -jnp.inf)
    fresh_scores = (
        jnp.einsum(
            "hgd,hnd->hgn", grouped_queries, current_keys, preferred_element_type=jnp.float32
        )
        * score_scale
    )
    highest = jnp.maximum(
        jnp.max(cache_scores, -1, keepdims=True), jnp.max(fresh_scores, -1, keepdims=True)
    )
    cache_exp = jnp.exp(cache_scores - highest)
    fresh_exp = jnp.exp(fresh_scores - highest)
    denominator = jnp.sum(cache_exp, -1, keepdims=True) + jnp.sum(fresh_exp, -1, keepdims=True)
    cache_weight = (cache_exp / denominator).astype(jnp.bfloat16)
    fresh_weight = (fresh_exp / denominator).astype(jnp.bfloat16)
    attended = jnp.einsum(
        "hgt,htd->hgd", cache_weight, local_values, preferred_element_type=jnp.float32
    )
    attended = attended + jnp.einsum(
        "hgn,hnd->hgd", fresh_weight, current_values, preferred_element_type=jnp.float32
    )
    return attended.reshape(every_head * HEAD_SIZE).astype(jnp.bfloat16)


def per_device(
    queries,
    new_keys,
    incoming_values,
    key_left,
    right_key_factor,
    value_tile_store,
    slot_map,
    chosen,
    lengths,
):
    nstore = lax.axis_size("store")
    local_rows = key_left.shape[0]
    nchunk = slot_map.shape[2]
    step_count = chosen.shape[0]
    selected_count = chosen.shape[3]
    keeper_share = max(1, nchunk // nstore // 4)
    tile_limit = local_rows * KEY_VALUE_HEADS * keeper_share
    pool_here = value_tile_store.shape[0]
    slot_numbers = jnp.take_along_axis(
        jnp.broadcast_to(slot_map[None], (step_count,) + slot_map.shape), chosen, axis=3
    )
    tile_keeper = slot_numbers // pool_here
    inside = slot_numbers % pool_here
    matched = tile_keeper[..., :, None] == tile_keeper[..., None, :]
    earlier = jnp.arange(selected_count)[None, :] < jnp.arange(selected_count)[:, None]
    order_in = jnp.sum(jnp.logical_and(matched, earlier), -1)
    row_head = (
        jnp.arange(local_rows, dtype=jnp.int32)[:, None, None] * KEY_VALUE_HEADS
        + jnp.arange(KEY_VALUE_HEADS, dtype=jnp.int32)[None, :, None]
    )
    position = row_head * keeper_share + order_in
    tiles_all = []
    slot_span = step_count * tile_limit
    flat_idx = (
        tile_keeper * slot_span
        + jnp.arange(step_count, dtype=jnp.int32)[:, None, None, None] * tile_limit
        + position
    )
    requests = build_requests(flat_idx, inside, nstore * slot_span).reshape(nstore, slot_span)
    received = fetch_tiles(requests, value_tile_store).reshape(nstore * slot_span, -1)
    for step_index in range(step_count):
        tiles_all.append(received[flat_idx[step_index]])
    results = []
    for step_index in range(step_count):
        per_rows = [
            attend_row(
                queries[:, 0],
                new_keys[:, 0],
                incoming_values[:, 0],
                key_left[0],
                right_key_factor[0],
                chosen[step_index, 0],
                tiles_all[step_index][0],
                lengths[0],
                step_index,
            )
        ]
        results.append(jnp.stack(per_rows))
    return jnp.stack(results)


def fused_kernel(
    share, pool_here,
    length_ref, pick_ref, ahead_ref, query_ref, new_key_ref, new_value_ref,
    chosen_ref, slot_ref, right_hbm, table_hbm, expand_hbm, spread_hbm, regroup_hbm, left_hbm,
    pool_hbm,
    out_ref,
    left_ref, right_ref, expand_ref, spread_ref, regroup_ref, pool_ref, block_ref,
    send_ref, ask_ref, asked_ref, row_ref, place_ref, sign_ref, bound_ref,
    rotated_ref, fresh_score_ref, fresh_value_ref, factor_ref, raw_even, raw_odd, turn_even, turn_odd, score_ref, fresh_ref,
    routed_ref, wire_ref, got_ref,
    core_out, core_in, side_out, side_in, line_out, line_in, keep_ref,
    in_sem, pool_sem, row_sem, ask_send, ask_recv, wire_send, wire_recv,
    core_send, core_recv, side_send, side_recv, line_send, line_recv,
):
    me = lax.axis_index("store")
    raw_refs, turn_refs = (raw_even, raw_odd), (turn_even, turn_odd)
    holders = send_ref.shape[0]
    depth = holders // 4
    rows, picks = chosen_ref.shape
    heads, blocks = slot_ref.shape
    steps = rows // heads
    rank = left_hbm.shape[0]
    deep = left_ref.shape[0]
    group = query_ref.shape[1] // HEAD_SIZE // heads
    both = steps * group
    half = HEAD_SIZE // 2
    units = heads // 2
    parts = ((0, units - 1), (units - 1, units))
    scale = HEAD_SIZE ** (-0.5)
    core, side, layer = lax.rem(me, 2), lax.rem(me // 2, 2), me // 4

    def peer(j):
        far, across, ahead = j // (2 * depth), j // depth % 2, j % depth
        return (
            lax.rem(layer + ahead, depth) * 4
            + (1 - side if across else side) * 2
            + (1 - core if far else core)
        )

    def remote(src, dst, send, recv, target):
        return pltpu.make_async_remote_copy(
            src_ref=src, dst_ref=dst, send_sem=send, recv_sem=recv,
            device_id={"store": target}, device_id_type=pl.DeviceIdType.MESH,
        )

    barrier = pltpu.get_barrier_semaphore()

    def greet(k, _):
        pl.semaphore_signal(
            barrier, inc=1, device_id={"store": lax.rem(me + k, holders)},
            device_id_type=pl.DeviceIdType.MESH,
        )
        return 0

    lax.fori_loop(1, holders, greet, 0)

    loads = [
        pltpu.make_async_copy(src, dst, in_sem.at[at])
        for at, (src, dst) in enumerate(
            (
                (left_hbm, left_ref.at[pl.ds(0, rank)]),
                (right_hbm, right_ref),
                (table_hbm, block_ref.at[:, :, pl.ds(deep, 2 * HEAD_SIZE)]),
                (expand_hbm, expand_ref),
                (regroup_hbm, regroup_ref),
                (spread_hbm, spread_ref),
            )
        )
    ]
    for copy in loads:
        copy.start()
    octets = pool_here // 8
    pool_copies = [
        pltpu.make_async_copy(
            pool_hbm.at[:, pl.ds(2 * q, 2), pl.ds(HEAD_SIZE * t, HEAD_SIZE)],
            pool_ref.at[pl.ds(q * octets, octets), pl.ds(2 * t, 2), :],
            pool_sem.at[q * BLOCK_TOKENS + t],
        )
        for q in range(4)
        for t in range(BLOCK_TOKENS)
    ]

    total = holders * share
    length = length_ref[0]
    lane_at = lax.broadcasted_iota(jnp.int32, (heads, total), 1)
    first_step = lane_at < picks
    chosen = jnp.concatenate([chosen_ref[s * heads : (s + 1) * heads] for s in range(steps)], 1)
    slot = jnp.zeros((heads, total), jnp.int32)
    for at in range(0, blocks, total):
        found = jnp.take_along_axis(slot_ref[:, at : at + total], chosen & (total - 1), axis=1)
        slot = jnp.where(chosen // total == at // total, found, slot)
    if pool_here & (pool_here - 1) == 0:
        keeper = slot >> (pool_here.bit_length() - 1)
        inside = slot & (pool_here - 1)
    else:
        keeper = lax.div(slot, jnp.full_like(slot, pool_here))
        inside = slot - keeper * pool_here
    sign_ref[...] = (1 - 2 * (inside & 1)).astype(jnp.float32)
    inside = ((inside >> 1) & 3) * octets + (inside >> 3)
    before_row = lax.broadcasted_iota(jnp.int32, (total, total), 0)
    before_lane = lax.broadcasted_iota(jnp.int32, (total, total), 1)
    before = jnp.where(
        jnp.logical_and(before_row < before_lane, before_row // picks == before_lane // picks),
        1.0, 0.0,
    ).astype(jnp.bfloat16)
    mine = [jnp.where(keeper == holder, 1.0, 0.0) for holder in range(holders)]
    counts = jnp.dot(
        jnp.concatenate(mine, 0).astype(jnp.bfloat16), before, preferred_element_type=jnp.float32
    )
    order = jnp.zeros((heads, total), jnp.float32)
    for holder in range(holders):
        order = order + mine[holder] * counts[holder * heads : (holder + 1) * heads]
    place = keeper * share + order.astype(jnp.int32)
    place_ref[...] = place
    digits = []
    for s in range(steps):
        for shift in (0, 8, 16):
            digit = ((inside >> shift) & 255).astype(jnp.float32)
            digits.append(jnp.where(first_step == (s == 0), digit, 0.0))
    slot_at = before_row
    moved = [None] * rows
    for head in range(heads):
        lines = jnp.concatenate(
            [digit[head : head + 1] for digit in digits]
            + [jnp.zeros((8 - len(digits), total), jnp.float32)], 0
        ).astype(jnp.bfloat16)
        table = jnp.where(place[head : head + 1] == slot_at, 1.0, 0.0).astype(jnp.bfloat16)
        found = lax.dot_general(
            lines, table, (((1,), (1,)), ((), ())), preferred_element_type=jnp.float32
        ).astype(jnp.int32)
        for s in range(steps):
            row = s * heads + head
            whole = found[3 * s : 3 * s + 1] + found[3 * s + 1 : 3 * s + 2] * 256
            whole = whole + found[3 * s + 2 : 3 * s + 3] * 65536
            moved[row] = pltpu.roll(whole, row * share, 1) if row else whole
    moved = jnp.concatenate(moved, 0)
    own_lanes = (
        lax.broadcasted_iota(jnp.int32, (rows, total), 1) // share
        == lax.broadcasted_iota(jnp.int32, (rows, total), 0)
    )
    for holder in range(holders):
        turned = pltpu.roll(moved, total - holder * share, 1) if holder else moved
        send_ref[holder] = jnp.sum(jnp.where(own_lanes, turned, 0), 0, keepdims=True)

    def ask_copy(j):
        target = peer(j)
        return remote(
            send_ref.at[target], ask_ref.at[j], ask_send.at[j], ask_recv.at[j], target
        )

    far_first = sorted(
        range(1, holders), key=lambda j: (-(min(j % depth, depth - j % depth)), -j)
    )
    pl.semaphore_wait(barrier, holders - 1)
    for j in far_first:
        ask_copy(j).start()
    ask_ref[0] = send_ref[me]

    left_ref[rank:, :] = jnp.zeros((deep - rank, left_ref.shape[1]), jnp.bfloat16)
    factor_ref[:, rank:, :] = jnp.zeros((heads, deep - rank, HEAD_SIZE), jnp.bfloat16)
    loads[1].wait()
    for head in range(heads):
        factor_ref[head, :rank, :] = right_ref[:, head * HEAD_SIZE : (head + 1) * HEAD_SIZE]
    loads[3].wait()
    remaining = jnp.clip(length - chosen * BLOCK_TOKENS, 0, BLOCK_TOKENS)
    bound_ref[...] = jnp.dot(
        remaining.astype(jnp.float32).astype(jnp.bfloat16), expand_ref[...],
        preferred_element_type=jnp.float32,
    )
    same = jnp.where(before_row == before_lane, 1.0, 0.0).astype(jnp.bfloat16)
    loads[0].wait()
    turned_blocks = total // BLOCK_TOKENS
    for at in range(0, left_ref.shape[1], total):
        turned = lax.dot_general(
            same, left_ref[:, at : at + total], (((1,), (1,)), ((), ())),
            preferred_element_type=jnp.float32,
        )
        first = at // BLOCK_TOKENS
        block_ref[first : first + turned_blocks, :, :deep] = turned.reshape(
            turned_blocks, BLOCK_TOKENS, deep
        )
    loads[2].wait()
    for copy in pool_copies:
        copy.start()

    last = jnp.maximum(length - 1, 0)
    turn = block_ref[last // BLOCK_TOKENS, pl.ds(lax.rem(last, BLOCK_TOKENS), 1), deep:]
    last_cos, last_sin = turn[:, :HEAD_SIZE], turn[:, HEAD_SIZE:]
    spin_cos, spin_sin = [], []
    for s in range(steps):
        more_cos, more_sin = ahead_ref[2 * s : 2 * s + 1], ahead_ref[2 * s + 1 : 2 * s + 2]
        spin_cos.append(
            jnp.broadcast_to(last_cos * more_cos - last_sin * more_sin, (group, HEAD_SIZE))
        )
        spin_sin.append(
            jnp.broadcast_to(last_sin * more_cos + last_cos * more_sin, (group, HEAD_SIZE))
        )
    query_all = query_ref[...].astype(jnp.float32)
    key_all = new_key_ref[...].astype(jnp.float32)
    value_all = new_value_ref[...].astype(jnp.float32)
    fresh_cos = jnp.concatenate([spin_cos[s][:1] for s in range(steps)] + [spin_cos[0][: 8 - steps]], 0)
    fresh_sin = jnp.concatenate([spin_sin[s][:1] for s in range(steps)] + [spin_sin[0][: 8 - steps]], 0)
    both_cos = jnp.concatenate(spin_cos, 0)
    both_sin = jnp.concatenate(spin_sin, 0)
    empty = jnp.zeros((8 - steps, HEAD_SIZE), jnp.float32)
    fresh_keep = (
        lax.broadcasted_iota(jnp.int32, (both, 8), 1)
        <= lax.broadcasted_iota(jnp.int32, (both, 8), 0) // group
    )
    for head in range(heads):
        lanes = slice(head * HEAD_SIZE, (head + 1) * HEAD_SIZE)
        flat = jnp.concatenate(
            [
                query_all[s : s + 1, (head * group + g) * HEAD_SIZE : (head * group + g + 1) * HEAD_SIZE]
                for s in range(steps)
                for g in range(group)
            ],
            0,
        )
        query = (flat * both_cos + pltpu.roll(flat, half, 1) * both_sin).astype(jnp.bfloat16)
        for s in range(steps):
            rotated_ref[s * heads + head] = query[s * group : (s + 1) * group]
        flat = jnp.concatenate([key_all[:, lanes], empty], 0)
        fresh_key = (flat * fresh_cos + pltpu.roll(flat, half, 1) * fresh_sin).astype(jnp.bfloat16)
        fresh = lax.dot_general(
            query, fresh_key, (((1,), (1,)), ((), ())), preferred_element_type=jnp.float32
        ) * scale
        fresh_score_ref[head] = jnp.where(fresh_keep, fresh, -jnp.inf)
        fresh_value_ref[head] = jnp.concatenate([value_all[:, lanes], empty], 0).astype(
            jnp.bfloat16
        )

    token_at = (
        lax.broadcasted_iota(jnp.int32, (group, picks * BLOCK_TOKENS), 1) % BLOCK_TOKENS
    ).astype(jnp.float32)
    low_half = lax.broadcasted_iota(jnp.int32, (group, total), 1) < picks

    portion = total // BLOCK_TOKENS
    portions = picks // portion

    def gather(row, at):
        head, s = divmod(row, steps)
        found = [
            block_ref[pick_ref[s * heads + head, at * portion + n]] for n in range(portion)
        ]
        span = slice(at * total, (at + 1) * total)
        raw_refs[row % 2][span] = jnp.dot(
            jnp.concatenate([value[:, :deep] for value in found], 0).astype(jnp.bfloat16),
            factor_ref[head], preferred_element_type=jnp.float32,
        )
        turn_refs[row % 2][span] = jnp.concatenate([value[:, deep:] for value in found], 0)

    def compare(row, at):
        head, s = divmod(row, steps)
        span = slice(at * total, (at + 1) * total)
        raw = raw_refs[row % 2][span]
        keys = raw * turn_refs[row % 2][span, :HEAD_SIZE]
        keys = keys + pltpu.roll(raw, half, 1) * turn_refs[row % 2][span, HEAD_SIZE:]
        score_ref[row, :, span] = lax.dot_general(
            rotated_ref[s * heads + head], keys.astype(jnp.bfloat16), (((1,), (1,)), ((), ())),
            preferred_element_type=jnp.float32,
        )

    def key_rows(first, last):
        for row in range(first, last):
            for at in range(portions):
                if row + 1 < rows:
                    gather(row + 1, at)
                compare(row, at)

    def weigh(part):
        weights = []
        heads_here = range(2 * parts[part][0], 2 * parts[part][1])
        for head in heads_here:
            fresh_weights = []
            for s in range(steps):
                bound = jnp.broadcast_to(
                    bound_ref[head : head + 1, s * picks * BLOCK_TOKENS : (s + 1) * picks * BLOCK_TOKENS],
                    token_at.shape,
                )
                scores = jnp.where(token_at < bound, score_ref[head * steps + s] * scale, -jnp.inf)
                fresh = fresh_score_ref[head, s * group : (s + 1) * group]
                highest = jnp.maximum(
                    jnp.max(scores, -1, keepdims=True), jnp.max(fresh, -1, keepdims=True)
                )
                power = jnp.exp(scores - highest)
                fresh_power = jnp.exp(fresh - highest)
                inverse = 1.0 / (
                    jnp.sum(power, -1, keepdims=True) + jnp.sum(fresh_power, -1, keepdims=True)
                )
                weights.append(power * inverse)
                fresh_weights.append(fresh_power * inverse)
            fresh_ref[head * both : (head + 1) * both] = jnp.dot(
                jnp.concatenate(fresh_weights, 0).astype(jnp.bfloat16), fresh_value_ref[head],
                preferred_element_type=jnp.float32,
            )
        grouped = jnp.dot(
            jnp.concatenate(weights, 0).astype(jnp.bfloat16), regroup_ref[...],
            preferred_element_type=jnp.float32,
        )
        for h, head in enumerate(heads_here):
            lines = []
            for s in range(steps):
                line = grouped[(h * steps + s) * group : (h * steps + s + 1) * group]
                for t in range(BLOCK_TOKENS):
                    value = line[:, t // 2 * total : (t // 2 + 1) * total]
                    if t % 2 != s:
                        value = pltpu.roll(value, picks, 1)
                    lines.append(
                        jnp.where(low_half, value, 0.0) if s == 0 else jnp.where(low_half, 0.0, value)
                    )
            table = jnp.where(
                place_ref[head : head + 1] == slot_at,
                jnp.broadcast_to(sign_ref[head : head + 1], (total, total)), 0.0,
            ).astype(jnp.bfloat16)
            routed = lax.dot_general(
                jnp.concatenate(lines, 0).astype(jnp.bfloat16), table, (((1,), (1,)), ((), ())),
                preferred_element_type=jnp.float32,
            )
            for s in range(steps):
                for t in range(BLOCK_TOKENS):
                    at = (s * BLOCK_TOKENS + t) * group
                    routed_ref[t, head, s * group : (s + 1) * group] = routed[at : at + group]

    lane = lax.broadcasted_iota(jnp.int32, (both, total), 1) // share

    def wire_copy(part, j):
        target = peer(j)
        first, last = parts[part]
        return remote(
            wire_ref.at[target, pl.ds(first, last - first)],
            got_ref.at[j, pl.ds(first, last - first)],
            wire_send.at[part * holders + j], wire_recv.at[part * holders + j], target,
        )

    loads[4].wait()
    for at in range(portions):
        gather(0, at)
    for part, (first, last) in enumerate(parts):
        key_rows(2 * first * steps, 2 * last * steps)
        weigh(part)
        for unit in range(first, last):
            cells = [
                routed_ref[t, 2 * unit + h] for t in range(BLOCK_TOKENS) for h in range(2)
            ]
            step = 1
            while step < holders:
                low_side = lane // step % 2 == 0
                turned = list(cells)
                for at in range(holders):
                    if at // step % 2 == 0:
                        a, b = cells[at], cells[at + step]
                        turned[at] = jnp.where(
                            low_side, a, pltpu.roll(b, step * share, 1)
                        )
                        turned[at + step] = jnp.where(
                            low_side, pltpu.roll(a, total - step * share, 1), b
                        )
                cells = turned
                step *= 2
            for holder in range(holders):
                wire_ref[holder, unit] = cells[holder].astype(jnp.bfloat16)
        for j in far_first:
            wire_copy(part, j).start()

    loads[5].wait()
    for j in range(1, holders):
        ask_copy(j).wait_recv()
    asked_ref[...] = jnp.clip(ask_ref[...], 0, pool_ref.shape[0] - 1)
    row_copy = pltpu.make_async_copy(asked_ref, row_ref, row_sem.at[0])
    row_copy.start()
    row_copy.wait()
    for copy in pool_copies:
        copy.wait()

    early = lax.broadcasted_iota(jnp.int32, (both, HEAD_SIZE), 0) < group

    def partial(unit, j):
        arrived = got_ref[j, unit] if j else wire_ref[me, unit]
        weight = jnp.maximum(
            jnp.dot(arrived, spread_ref[...], preferred_element_type=jnp.float32), 0.0
        )
        lhs, columns = [], []
        for h in range(2):
            own = weight[:, h * HEAD_SIZE : (h + 1) * HEAD_SIZE]
            lhs.append(
                jnp.concatenate(
                    [jnp.where(early, own, 0.0), jnp.where(early, 0.0, own)], 1
                ).astype(jnp.bfloat16)
            )
            columns.append(
                jnp.concatenate(
                    [
                        pool_ref[row_ref[j, 0, (s * heads + 2 * unit + h) * share + n]]
                        for s in range(steps)
                        for n in range(share)
                    ],
                    0,
                )
            )
        product = jnp.dot(
            jnp.concatenate(lhs, 0), jnp.concatenate(columns, 1),
            preferred_element_type=jnp.float32,
        )
        return jnp.concatenate([product[:both, :HEAD_SIZE], product[both:, HEAD_SIZE:]], 0)

    own_core = peer(2 * depth)
    own_side = peer(depth)

    def span(part):
        first, last = parts[part]
        return pl.ds(first * 2 * both, (last - first) * 2 * both)

    def core_copy(part, across):
        at = part * 2 + across
        return remote(
            core_out.at[across, :, span(part)], core_in.at[across, :, span(part)],
            core_send.at[at], core_recv.at[at], own_core,
        )

    def side_copy(part):
        return remote(
            side_out.at[:, span(part)], side_in.at[:, span(part)],
            side_send.at[part], side_recv.at[part], own_side,
        )

    def line_copy(part, ahead):
        at = part * depth + ahead
        return remote(
            line_out.at[ahead, span(part)], line_in.at[ahead, span(part)],
            line_send.at[at], line_recv.at[at],
            lax.rem(layer - ahead + depth, depth) * 4 + side * 2 + core,
        )

    def stage(part, far, across):
        first = far * 2 * depth + across * depth
        js = [first + ahead for ahead in range(depth)]
        for j in js:
            if j:
                wire_copy(part, j).wait_recv()
        return [
            jnp.concatenate([partial(unit, j) for unit in range(*parts[part])], 0) for j in js
        ]

    def far_stage(part, across):
        for ahead, value in enumerate(stage(part, 1, across)):
            core_out[across, ahead, span(part)] = value
        core_copy(part, across).start()

    def side_stage(part):
        values = stage(part, 0, 1)
        core_copy(part, 1).wait_recv()
        for ahead, value in enumerate(values):
            side_out[ahead, span(part)] = (value + core_in[1, ahead, span(part)]).astype(
                jnp.bfloat16
            )
        side_copy(part).start()

    def line_stage(part):
        values = stage(part, 0, 0)
        core_copy(part, 0).wait_recv()
        side_copy(part).wait_recv()
        for ahead in list(range(1, depth)) + [0]:
            value = values[ahead] + core_in[0, ahead, span(part)]
            value = value + side_in[ahead, span(part)].astype(jnp.float32)
            if ahead:
                line_out[ahead, span(part)] = value.astype(jnp.bfloat16)
                line_copy(part, ahead).start()
            else:
                keep_ref[span(part)] = value

    far_stage(0, 1)
    side_stage(0)
    far_stage(1, 1)
    side_stage(1)
    far_stage(0, 0)
    line_stage(0)
    far_stage(1, 0)
    line_stage(1)

    for part in range(2):
        value = keep_ref[span(part)] + fresh_ref[span(part)]
        for ahead in range(1, depth):
            line_copy(part, ahead).wait_recv()
            value = value + line_in[ahead, span(part)].astype(jnp.float32)
        keep_ref[span(part)] = value
    for head in range(heads):
        for g in range(group):
            at = (head * group + g) * HEAD_SIZE
            out_ref[:, at : at + HEAD_SIZE] = jnp.concatenate(
                [
                    keep_ref[head * both + s * group + g : head * both + s * group + g + 1]
                    for s in range(steps)
                ],
                0,
            )

    for j in range(1, holders):
        ask_copy(j).wait_send()
        for part in range(2):
            wire_copy(part, j).wait_send()
    for part in range(2):
        core_copy(part, 0).wait_send()
        core_copy(part, 1).wait_send()
        side_copy(part).wait_send()
        for ahead in range(1, depth):
            line_copy(part, ahead).wait_send()


def fused_device(
    queries, new_keys, incoming_values, key_left, right_key_factor, value_tile_store, slot_map,
    chosen, lengths,
):
    holders = lax.axis_size("store")
    steps, _, heads, picks = chosen.shape
    blocks = slot_map.shape[2]
    share = max(1, blocks // holders // 4)
    pool_here = value_tile_store.shape[0]
    group = queries.shape[2] // HEAD_SIZE // heads
    rank = key_left.shape[2]
    slots = steps * heads * share
    rows = steps * heads * group
    both = steps * group
    units = heads // 2
    depth = holders // 4
    half = HEAD_SIZE // 2
    tokens = blocks * BLOCK_TOKENS

    turns = np.arange(tokens)[:, None] * ROPE_BASE ** (-(np.arange(half) * 2.0 / HEAD_SIZE))[None]
    cosine, sine = np.cos(turns), np.sin(turns)
    table = np.concatenate([cosine, cosine, -sine, sine], 1).astype(np.float32)
    ahead = jnp.asarray(table[1 : steps + 1].reshape(2 * steps, HEAD_SIZE))
    table = jnp.asarray(table.reshape(blocks, BLOCK_TOKENS, 2 * HEAD_SIZE))
    expand = np.repeat(np.eye(steps * picks, dtype=np.float32), BLOCK_TOKENS, 1)
    deep = -(-rank // 128) * 128
    wide = BLOCK_TOKENS * 64
    regroup = np.zeros((wide, wide), np.float32)
    for t in range(BLOCK_TOKENS):
        regroup[np.arange(64) * BLOCK_TOKENS + t, t * 64 + np.arange(64)] = 1.0
    spread = np.zeros((BLOCK_TOKENS, 2, share, 2, share, BLOCK_TOKENS, 2), np.float32)
    for t in range(BLOCK_TOKENS):
        for h in range(2):
            for n in range(share):
                spread[t, h, n, h, n, t] = (1.0, -1.0)
    lines = BLOCK_TOKENS * 2 * share
    spread = spread.reshape(lines, 2 * lines)

    vmem = pl.BlockSpec(memory_space=pltpu.VMEM)
    anywhere = pl.BlockSpec(memory_space=pl.ANY)
    bf16, f32 = jnp.bfloat16, jnp.float32
    dma = pltpu.SemaphoreType.DMA
    attended = pl.pallas_call(
        functools.partial(fused_kernel, share, pool_here),
        in_specs=[pl.BlockSpec(memory_space=pltpu.SMEM)] * 2 + [vmem] * 6 + [anywhere] * 7,
        out_specs=vmem,
        out_shape=pltpu.VMEM((steps, heads * group * HEAD_SIZE), f32),
        scratch_shapes=[
            pltpu.VMEM((deep, tokens), bf16),
            pltpu.VMEM((rank, heads * HEAD_SIZE), bf16),
            pltpu.VMEM((steps * picks, steps * picks * BLOCK_TOKENS), bf16),
            pltpu.VMEM((lines, 2 * lines), bf16),
            pltpu.VMEM((wide, wide), bf16),
            pltpu.VMEM((pool_here // 2, 2 * BLOCK_TOKENS, HEAD_SIZE), bf16),
            pltpu.VMEM((blocks, BLOCK_TOKENS, deep + 2 * HEAD_SIZE), f32),
            pltpu.VMEM((holders, 1, slots), jnp.int32),
            pltpu.VMEM((holders, 1, slots), jnp.int32),
            pltpu.VMEM((holders, 1, slots), jnp.int32),
            pltpu.SMEM((holders, 1, slots), jnp.int32),
            pltpu.VMEM((heads, steps * picks), jnp.int32),
            pltpu.VMEM((heads, steps * picks), f32),
            pltpu.VMEM((heads, steps * picks * BLOCK_TOKENS), f32),
            pltpu.VMEM((steps * heads, group, HEAD_SIZE), bf16),
            pltpu.VMEM((heads, both, 8), f32),
            pltpu.VMEM((heads, 8, HEAD_SIZE), bf16),
            pltpu.VMEM((heads, deep, HEAD_SIZE), bf16),
            pltpu.VMEM((picks * BLOCK_TOKENS, HEAD_SIZE), f32),
            pltpu.VMEM((picks * BLOCK_TOKENS, HEAD_SIZE), f32),
            pltpu.VMEM((picks * BLOCK_TOKENS, 2 * HEAD_SIZE), f32),
            pltpu.VMEM((picks * BLOCK_TOKENS, 2 * HEAD_SIZE), f32),
            pltpu.VMEM((heads * steps, group, picks * BLOCK_TOKENS), f32),
            pltpu.VMEM((rows, HEAD_SIZE), f32),
            pltpu.VMEM((BLOCK_TOKENS, heads, both, holders * share), f32),
            pltpu.VMEM((holders, units, both, lines), bf16),
            pltpu.VMEM((holders, units, both, lines), bf16),
            pltpu.VMEM((2, depth, rows, HEAD_SIZE), f32),
            pltpu.VMEM((2, depth, rows, HEAD_SIZE), f32),
            pltpu.VMEM((depth, rows, HEAD_SIZE), bf16),
            pltpu.VMEM((depth, rows, HEAD_SIZE), bf16),
            pltpu.VMEM((depth, rows, HEAD_SIZE), bf16),
            pltpu.VMEM((depth, rows, HEAD_SIZE), bf16),
            pltpu.VMEM((rows, HEAD_SIZE), f32),
            dma((6,)), dma((4 * BLOCK_TOKENS,)), dma((1,)),
            dma((holders,)), dma((holders,)), dma((2 * holders,)), dma((2 * holders,)),
            dma((4,)), dma((4,)), dma((2,)), dma((2,)), dma((2 * depth,)), dma((2 * depth,)),
        ],
        compiler_params=pltpu.CompilerParams(collective_id=0, has_side_effects=True),
        name="fused",
    )(
        lengths, chosen[:, 0].reshape(steps * heads, picks), ahead,
        queries[:, 0], new_keys[:, 0], incoming_values[:, 0],
        chosen[:, 0].reshape(steps * heads, picks), slot_map[0],
        right_key_factor[0], table, jnp.asarray(expand, bf16), jnp.asarray(spread, bf16),
        jnp.asarray(regroup, bf16), key_left[0].T,
        value_tile_store.reshape(pool_here // 8, 8, -1),
    )
    return attended.astype(bf16).reshape(steps, 1, -1)


def solution(mesh):
    in_specs = (
        P(None, ("groups", "store"), None),
        P(None, ("groups", "store"), None),
        P(None, ("groups", "store"), None),
        P(("groups", "store"), None, None),
        P(("groups", "store"), None, None),
        P(("groups", "store"), None),
        P(("groups", "store"), None, None),
        P(None, ("groups", "store"), None, None),
        P(("groups", "store")),
    )
    out_specs = P(None, ("groups", "store"), None)

    def body(*args):
        holders = mesh.shape["store"]
        blocks = args[6].shape[2]
        share = max(1, blocks // holders // 4)
        square = args[7].shape[0] * args[7].shape[2] == holders
        packed = args[7].shape[0] * args[7].shape[3] == holders * share
        fits = square and packed and share == 8 and holders == 16 and blocks % 128 == 0
        return (fused_device if fits else per_device)(*args)

    return jax.shard_map(
        body, mesh=mesh, in_specs=in_specs, out_specs=out_specs, check_vma=False
    )
```

```python
import functools

import jax
import jax.numpy as jnp
import numpy as np
from jax import lax
from jax.experimental import pallas as pl
from jax.experimental.pallas import tpu as pltpu
from jax.sharding import PartitionSpec as P

KEY_VALUE_HEADS = 8
HEAD_SIZE = 128
BLOCK_TOKENS = 8


ROPE_BASE = 500000.0


def apply_rotary(tensor, token_positions):
    half_dim = tensor.shape[-1] // 2
    inverse = ROPE_BASE ** (-(jnp.arange(half_dim, dtype=jnp.float32) * 2.0 / tensor.shape[-1]))
    angles = jnp.asarray(token_positions).astype(jnp.float32)[..., None] * inverse
    cosine = jnp.cos(angles)
    sine_vals = jnp.sin(angles)
    first_half = tensor[..., :half_dim]
    second_half = tensor[..., half_dim:]
    return jnp.concatenate(
        [
            first_half * cosine - second_half * sine_vals,
            second_half * cosine + first_half * sine_vals,
        ],
        -1,
    )


def fetch_tiles(requests, value_tile_store):
    tile_row_index = jnp.take(
        value_tile_store,
        lax.all_to_all(requests, "store", split_axis=0, concat_axis=0, tiled=True),
        axis=0,
    )
    return lax.all_to_all(tile_row_index, "store", split_axis=0, concat_axis=0, tiled=True)


def build_requests(flat_idx, inside, total):
    buffer = jnp.zeros((total,), jnp.int32)
    return buffer.at[flat_idx.reshape(-1)].set(inside.reshape(-1))


def attend_row(
    query_full,
    incoming_keys_full,
    incoming_values_full,
    left_rows,
    right_factor_rows,
    block_numbers,
    tile_row_index,
    length,
    step_index,
):
    query_group_size = query_full.shape[-1] // HEAD_SIZE // KEY_VALUE_HEADS
    every_head = query_group_size * KEY_VALUE_HEADS
    selected_count = block_numbers.shape[1]
    score_scale = HEAD_SIZE ** (-0.5)
    right_factor_heads = right_factor_rows.reshape(
        right_factor_rows.shape[0], KEY_VALUE_HEADS, HEAD_SIZE
    )
    token_positions = (
        block_numbers[:, :, None] * BLOCK_TOKENS + jnp.arange(BLOCK_TOKENS, dtype=jnp.int32)
    ).reshape(KEY_VALUE_HEADS, selected_count * BLOCK_TOKENS)
    picked = left_rows[token_positions]
    raw_keys = jnp.einsum(
        "htr,rhd->htd", picked, right_factor_heads, preferred_element_type=jnp.float32
    )
    cache_keys = apply_rotary(raw_keys, token_positions).astype(jnp.bfloat16)
    rotated_query = apply_rotary(
        query_full[step_index].reshape(every_head, HEAD_SIZE).astype(jnp.float32),
        length + step_index,
    ).astype(jnp.bfloat16)
    current_position = (length + jnp.arange(step_index + 1, dtype=jnp.int32))[:, None]
    current_keys = apply_rotary(
        incoming_keys_full[: step_index + 1]
        .reshape(step_index + 1, KEY_VALUE_HEADS, HEAD_SIZE)
        .astype(jnp.float32),
        current_position,
    ).astype(jnp.bfloat16)
    current_keys = jnp.transpose(current_keys, (1, 0, 2))
    current_values = jnp.transpose(
        incoming_values_full[: step_index + 1].reshape(step_index + 1, KEY_VALUE_HEADS, HEAD_SIZE),
        (1, 0, 2),
    )
    local_values = tile_row_index.reshape(KEY_VALUE_HEADS, selected_count * BLOCK_TOKENS, HEAD_SIZE)
    grouped_queries = rotated_query.reshape(KEY_VALUE_HEADS, query_group_size, HEAD_SIZE)
    cache_scores = (
        jnp.einsum("hgd,htd->hgt", grouped_queries, cache_keys, preferred_element_type=jnp.float32)
        * score_scale
    )
    inside_len = token_positions < length
    cache_scores = jnp.where(inside_len[:, None, :], cache_scores, -jnp.inf)
    fresh_scores = (
        jnp.einsum(
            "hgd,hnd->hgn", grouped_queries, current_keys, preferred_element_type=jnp.float32
        )
        * score_scale
    )
    highest = jnp.maximum(
        jnp.max(cache_scores, -1, keepdims=True), jnp.max(fresh_scores, -1, keepdims=True)
    )
    cache_exp = jnp.exp(cache_scores - highest)
    fresh_exp = jnp.exp(fresh_scores - highest)
    denominator = jnp.sum(cache_exp, -1, keepdims=True) + jnp.sum(fresh_exp, -1, keepdims=True)
    cache_weight = (cache_exp / denominator).astype(jnp.bfloat16)
    fresh_weight = (fresh_exp / denominator).astype(jnp.bfloat16)
    attended = jnp.einsum(
        "hgt,htd->hgd", cache_weight, local_values, preferred_element_type=jnp.float32
    )
    attended = attended + jnp.einsum(
        "hgn,hnd->hgd", fresh_weight, current_values, preferred_element_type=jnp.float32
    )
    return attended.reshape(every_head * HEAD_SIZE).astype(jnp.bfloat16)


def per_device(
    queries,
    new_keys,
    incoming_values,
    key_left,
    right_key_factor,
    value_tile_store,
    slot_map,
    chosen,
    lengths,
):
    nstore = lax.axis_size("store")
    local_rows = key_left.shape[0]
    nchunk = slot_map.shape[2]
    step_count = chosen.shape[0]
    selected_count = chosen.shape[3]
    keeper_share = max(1, nchunk // nstore // 4)
    tile_limit = local_rows * KEY_VALUE_HEADS * keeper_share
    pool_here = value_tile_store.shape[0]
    slot_numbers = jnp.take_along_axis(
        jnp.broadcast_to(slot_map[None], (step_count,) + slot_map.shape), chosen, axis=3
    )
    tile_keeper = slot_numbers // pool_here
    inside = slot_numbers % pool_here
    matched = tile_keeper[..., :, None] == tile_keeper[..., None, :]
    earlier = jnp.arange(selected_count)[None, :] < jnp.arange(selected_count)[:, None]
    order_in = jnp.sum(jnp.logical_and(matched, earlier), -1)
    row_head = (
        jnp.arange(local_rows, dtype=jnp.int32)[:, None, None] * KEY_VALUE_HEADS
        + jnp.arange(KEY_VALUE_HEADS, dtype=jnp.int32)[None, :, None]
    )
    position = row_head * keeper_share + order_in
    tiles_all = []
    slot_span = step_count * tile_limit
    flat_idx = (
        tile_keeper * slot_span
        + jnp.arange(step_count, dtype=jnp.int32)[:, None, None, None] * tile_limit
        + position
    )
    requests = build_requests(flat_idx, inside, nstore * slot_span).reshape(nstore, slot_span)
    received = fetch_tiles(requests, value_tile_store).reshape(nstore * slot_span, -1)
    for step_index in range(step_count):
        tiles_all.append(received[flat_idx[step_index]])
    results = []
    for step_index in range(step_count):
        per_rows = [
            attend_row(
                queries[:, 0],
                new_keys[:, 0],
                incoming_values[:, 0],
                key_left[0],
                right_key_factor[0],
                chosen[step_index, 0],
                tiles_all[step_index][0],
                lengths[0],
                step_index,
            )
        ]
        results.append(jnp.stack(per_rows))
    return jnp.stack(results)


def fused_kernel(
    share, pool_here,
    length_ref, pick_ref, ahead_ref, query_ref, new_key_ref, new_value_ref,
    chosen_ref, slot_ref, right_hbm, table_hbm, expand_hbm, spread_hbm, regroup_hbm, left_hbm,
    pool_hbm,
    out_ref,
    left_ref, right_ref, expand_ref, spread_ref, regroup_ref, pool_ref, block_ref,
    send_ref, ask_ref, asked_ref, row_ref, place_ref, sign_ref, bound_ref,
    rotated_ref, fresh_score_ref, fresh_value_ref, factor_ref, raw_even, raw_odd, turn_even, turn_odd, score_ref, fresh_ref,
    routed_ref, wire_ref, got_ref,
    core_out, core_in, side_out, side_in, line_out, line_in, keep_ref,
    in_sem, pool_sem, row_sem, ask_send, ask_recv, wire_send, wire_recv,
    core_send, core_recv, side_send, side_recv, line_send, line_recv,
):
    me = lax.axis_index("store")
    raw_refs, turn_refs = (raw_even, raw_odd), (turn_even, turn_odd)
    holders = send_ref.shape[0]
    depth = holders // 4
    rows, picks = chosen_ref.shape
    heads, blocks = slot_ref.shape
    steps = rows // heads
    rank = left_hbm.shape[0]
    deep = left_ref.shape[0]
    group = query_ref.shape[1] // HEAD_SIZE // heads
    both = steps * group
    half = HEAD_SIZE // 2
    units = heads // 2
    parts = ((0, units - 2), (units - 2, units - 1), (units - 1, units))
    scale = HEAD_SIZE ** (-0.5)
    core, side, layer = lax.rem(me, 2), lax.rem(me // 2, 2), me // 4

    def peer(j):
        far, across, ahead = j // (2 * depth), j // depth % 2, j % depth
        return (
            lax.rem(layer + ahead, depth) * 4
            + (1 - side if across else side) * 2
            + (1 - core if far else core)
        )

    def remote(src, dst, send, recv, target):
        return pltpu.make_async_remote_copy(
            src_ref=src, dst_ref=dst, send_sem=send, recv_sem=recv,
            device_id={"store": target}, device_id_type=pl.DeviceIdType.MESH,
        )

    barrier = pltpu.get_barrier_semaphore()

    def greet(k, _):
        pl.semaphore_signal(
            barrier, inc=1, device_id={"store": lax.rem(me + k, holders)},
            device_id_type=pl.DeviceIdType.MESH,
        )
        return 0

    lax.fori_loop(1, holders, greet, 0)

    loads = [
        pltpu.make_async_copy(src, dst, in_sem.at[at])
        for at, (src, dst) in enumerate(
            (
                (left_hbm, left_ref.at[pl.ds(0, rank)]),
                (right_hbm, right_ref),
                (table_hbm, block_ref.at[:, :, pl.ds(deep, 2 * HEAD_SIZE)]),
                (expand_hbm, expand_ref),
                (regroup_hbm, regroup_ref),
                (spread_hbm, spread_ref),
            )
        )
    ]
    for copy in loads:
        copy.start()
    octets = pool_here // 8
    pool_copies = [
        pltpu.make_async_copy(
            pool_hbm.at[:, pl.ds(2 * q, 2), pl.ds(HEAD_SIZE * t, HEAD_SIZE)],
            pool_ref.at[pl.ds(q * octets, octets), pl.ds(2 * t, 2), :],
            pool_sem.at[0],
        )
        for q in range(4)
        for t in range(BLOCK_TOKENS)
    ]

    total = holders * share
    length = length_ref[0]
    lane_at = lax.broadcasted_iota(jnp.int32, (heads, total), 1)
    first_step = lane_at < picks
    chosen = jnp.concatenate([chosen_ref[s * heads : (s + 1) * heads] for s in range(steps)], 1)
    slot = jnp.zeros((heads, total), jnp.int32)
    for at in range(0, blocks, total):
        found = jnp.take_along_axis(slot_ref[:, at : at + total], chosen & (total - 1), axis=1)
        slot = jnp.where(chosen // total == at // total, found, slot)
    if pool_here & (pool_here - 1) == 0:
        keeper = slot >> (pool_here.bit_length() - 1)
        inside = slot & (pool_here - 1)
    else:
        keeper = lax.div(slot, jnp.full_like(slot, pool_here))
        inside = slot - keeper * pool_here
    sign_ref[...] = (1 - 2 * (inside & 1)).astype(jnp.float32)
    inside = ((inside >> 1) & 3) * octets + (inside >> 3)
    before_row = lax.broadcasted_iota(jnp.int32, (total, total), 0)
    before_lane = lax.broadcasted_iota(jnp.int32, (total, total), 1)
    before = jnp.where(
        jnp.logical_and(before_row < before_lane, before_row // picks == before_lane // picks),
        1.0, 0.0,
    ).astype(jnp.bfloat16)
    mine = [jnp.where(keeper == holder, 1.0, 0.0) for holder in range(holders)]
    counts = jnp.dot(
        jnp.concatenate(mine, 0).astype(jnp.bfloat16), before, preferred_element_type=jnp.float32
    )
    order = jnp.zeros((heads, total), jnp.float32)
    for holder in range(holders):
        order = order + mine[holder] * counts[holder * heads : (holder + 1) * heads]
    place = keeper * share + order.astype(jnp.int32)
    place_ref[...] = place
    digits = []
    for s in range(steps):
        for shift in (0, 8, 16):
            digit = ((inside >> shift) & 255).astype(jnp.float32)
            digits.append(jnp.where(first_step == (s == 0), digit, 0.0))
    slot_at = before_row
    moved = [None] * rows
    for head in range(heads):
        lines = jnp.concatenate(
            [digit[head : head + 1] for digit in digits]
            + [jnp.zeros((8 - len(digits), total), jnp.float32)], 0
        ).astype(jnp.bfloat16)
        table = jnp.where(place[head : head + 1] == slot_at, 1.0, 0.0).astype(jnp.bfloat16)
        found = lax.dot_general(
            lines, table, (((1,), (1,)), ((), ())), preferred_element_type=jnp.float32
        ).astype(jnp.int32)
        for s in range(steps):
            row = s * heads + head
            whole = found[3 * s : 3 * s + 1] + found[3 * s + 1 : 3 * s + 2] * 256
            whole = whole + found[3 * s + 2 : 3 * s + 3] * 65536
            moved[row] = pltpu.roll(whole, row * share, 1) if row else whole
    moved = jnp.concatenate(moved, 0)
    own_lanes = (
        lax.broadcasted_iota(jnp.int32, (rows, total), 1) // share
        == lax.broadcasted_iota(jnp.int32, (rows, total), 0)
    )
    for holder in range(holders):
        turned = pltpu.roll(moved, total - holder * share, 1) if holder else moved
        send_ref[holder] = jnp.sum(jnp.where(own_lanes, turned, 0), 0, keepdims=True)

    def ask_copy(j):
        target = peer(j)
        return remote(
            send_ref.at[target], ask_ref.at[j], ask_send.at[0], ask_recv.at[0], target
        )

    far_first = sorted(
        range(1, holders), key=lambda j: (-(min(j % depth, depth - j % depth)), -j)
    )
    pl.semaphore_wait(barrier, holders - 1)
    for j in far_first:
        ask_copy(j).start()
    ask_ref[0] = send_ref[me]

    left_ref[rank:, :] = jnp.zeros((deep - rank, left_ref.shape[1]), jnp.bfloat16)
    factor_ref[:, rank:, :] = jnp.zeros((heads, deep - rank, 2 * HEAD_SIZE), jnp.bfloat16)
    loads[1].wait()
    for head in range(heads):
        factor = right_ref[:, head * HEAD_SIZE : (head + 1) * HEAD_SIZE]
        factor_ref[head, :rank, :HEAD_SIZE] = factor
        factor_ref[head, :rank, HEAD_SIZE:] = pltpu.roll(
            factor.astype(jnp.float32), half, 1
        ).astype(jnp.bfloat16)
    loads[3].wait()
    remaining = jnp.clip(length - chosen * BLOCK_TOKENS, 0, BLOCK_TOKENS)
    bound_ref[...] = jnp.dot(
        remaining.astype(jnp.float32).astype(jnp.bfloat16), expand_ref[...],
        preferred_element_type=jnp.float32,
    )
    same = jnp.where(before_row == before_lane, 1.0, 0.0).astype(jnp.bfloat16)
    loads[0].wait()
    turned_blocks = total // BLOCK_TOKENS
    for at in range(0, left_ref.shape[1], total):
        turned = lax.dot_general(
            same, left_ref[:, at : at + total], (((1,), (1,)), ((), ())),
            preferred_element_type=jnp.float32,
        )
        first = at // BLOCK_TOKENS
        block_ref[first : first + turned_blocks, :, :deep] = turned.reshape(
            turned_blocks, BLOCK_TOKENS, deep
        )
    loads[2].wait()
    for copy in pool_copies:
        copy.start()

    last = jnp.maximum(length - 1, 0)
    turn = block_ref[last // BLOCK_TOKENS, pl.ds(lax.rem(last, BLOCK_TOKENS), 1), deep:]
    last_cos, last_sin = turn[:, :HEAD_SIZE], turn[:, HEAD_SIZE:]
    spin_cos, spin_sin = [], []
    for s in range(steps):
        more_cos, more_sin = ahead_ref[2 * s : 2 * s + 1], ahead_ref[2 * s + 1 : 2 * s + 2]
        spin_cos.append(
            jnp.broadcast_to(last_cos * more_cos - last_sin * more_sin, (group, HEAD_SIZE))
        )
        spin_sin.append(
            jnp.broadcast_to(last_sin * more_cos + last_cos * more_sin, (group, HEAD_SIZE))
        )
    query_all = query_ref[...].astype(jnp.float32)
    key_all = new_key_ref[...].astype(jnp.float32)
    value_all = new_value_ref[...].astype(jnp.float32)
    fresh_cos = jnp.concatenate([spin_cos[s][:1] for s in range(steps)] + [spin_cos[0][: 8 - steps]], 0)
    fresh_sin = jnp.concatenate([spin_sin[s][:1] for s in range(steps)] + [spin_sin[0][: 8 - steps]], 0)
    both_cos = jnp.concatenate(spin_cos, 0)
    both_sin = jnp.concatenate(spin_sin, 0)
    empty = jnp.zeros((8 - steps, HEAD_SIZE), jnp.float32)
    fresh_keep = (
        lax.broadcasted_iota(jnp.int32, (both, 8), 1)
        <= lax.broadcasted_iota(jnp.int32, (both, 8), 0) // group
    )
    for head in range(heads):
        lanes = slice(head * HEAD_SIZE, (head + 1) * HEAD_SIZE)
        flat = jnp.concatenate(
            [
                query_all[s : s + 1, (head * group + g) * HEAD_SIZE : (head * group + g + 1) * HEAD_SIZE]
                for s in range(steps)
                for g in range(group)
            ],
            0,
        )
        query = (flat * both_cos + pltpu.roll(flat, half, 1) * both_sin).astype(jnp.bfloat16)
        for s in range(steps):
            rotated_ref[s * heads + head] = query[s * group : (s + 1) * group]
        flat = jnp.concatenate([key_all[:, lanes], empty], 0)
        fresh_key = (flat * fresh_cos + pltpu.roll(flat, half, 1) * fresh_sin).astype(jnp.bfloat16)
        fresh = lax.dot_general(
            query, fresh_key, (((1,), (1,)), ((), ())), preferred_element_type=jnp.float32
        ) * scale
        fresh_score_ref[head] = jnp.where(fresh_keep, fresh, -jnp.inf)
        fresh_value_ref[head] = jnp.concatenate([value_all[:, lanes], empty], 0).astype(
            jnp.bfloat16
        )

    token_at = (
        lax.broadcasted_iota(jnp.int32, (group, picks * BLOCK_TOKENS), 1) % BLOCK_TOKENS
    ).astype(jnp.float32)
    low_half = lax.broadcasted_iota(jnp.int32, (group, total), 1) < picks

    portion = 2 * total // BLOCK_TOKENS
    portions = picks // portion

    def gather(row, at):
        head, s = divmod(row, steps)
        found = [
            block_ref[pick_ref[s * heads + head, at * portion + n]] for n in range(portion)
        ]
        span = slice(2 * at * total, 2 * (at + 1) * total)
        raw_refs[row % 2][span] = jnp.dot(
            jnp.concatenate([value[:, :deep] for value in found], 0).astype(jnp.bfloat16),
            factor_ref[head], preferred_element_type=jnp.float32,
        )
        turn_refs[row % 2][span] = jnp.concatenate([value[:, deep:] for value in found], 0)

    def compare(row, at):
        head, s = divmod(row, steps)
        span = slice(2 * at * total, 2 * (at + 1) * total)
        raw = raw_refs[row % 2][span]
        keys = raw * turn_refs[row % 2][span]
        keys = keys[:, :HEAD_SIZE] + keys[:, HEAD_SIZE:]
        score_ref[row, :, span] = lax.dot_general(
            rotated_ref[s * heads + head], keys.astype(jnp.bfloat16), (((1,), (1,)), ((), ())),
            preferred_element_type=jnp.float32,
        )

    def key_rows(first, last):
        for row in range(first, last):
            for at in range(portions):
                if row + 1 < rows:
                    gather(row + 1, at)
                compare(row, at)

    def weigh(part):
        weights = []
        heads_here = range(2 * parts[part][0], 2 * parts[part][1])
        for head in heads_here:
            fresh_weights = []
            for s in range(steps):
                bound = jnp.broadcast_to(
                    bound_ref[head : head + 1, s * picks * BLOCK_TOKENS : (s + 1) * picks * BLOCK_TOKENS],
                    token_at.shape,
                )
                scores = jnp.where(token_at < bound, score_ref[head * steps + s] * scale, -jnp.inf)
                fresh = fresh_score_ref[head, s * group : (s + 1) * group]
                highest = jnp.maximum(
                    jnp.max(scores, -1, keepdims=True), jnp.max(fresh, -1, keepdims=True)
                )
                power = jnp.exp(scores - highest)
                fresh_power = jnp.exp(fresh - highest)
                inverse = 1.0 / (
                    jnp.sum(power, -1, keepdims=True) + jnp.sum(fresh_power, -1, keepdims=True)
                )
                weights.append(power * inverse)
                fresh_weights.append(fresh_power * inverse)
            fresh_ref[head * both : (head + 1) * both] = jnp.dot(
                jnp.concatenate(fresh_weights, 0).astype(jnp.bfloat16), fresh_value_ref[head],
                preferred_element_type=jnp.float32,
            )
        grouped = jnp.dot(
            jnp.concatenate(weights, 0).astype(jnp.bfloat16), regroup_ref[...],
            preferred_element_type=jnp.float32,
        )
        for h, head in enumerate(heads_here):
            lines = []
            for s in range(steps):
                line = grouped[(h * steps + s) * group : (h * steps + s + 1) * group]
                for t in range(BLOCK_TOKENS):
                    value = line[:, t // 2 * total : (t // 2 + 1) * total]
                    if t % 2 != s:
                        value = pltpu.roll(value, picks, 1)
                    lines.append(
                        jnp.where(low_half, value, 0.0) if s == 0 else jnp.where(low_half, 0.0, value)
                    )
            table = jnp.where(
                place_ref[head : head + 1] == slot_at,
                jnp.broadcast_to(sign_ref[head : head + 1], (total, total)), 0.0,
            ).astype(jnp.bfloat16)
            routed = lax.dot_general(
                jnp.concatenate(lines, 0).astype(jnp.bfloat16), table, (((1,), (1,)), ((), ())),
                preferred_element_type=jnp.float32,
            )
            for s in range(steps):
                for t in range(BLOCK_TOKENS):
                    at = (s * BLOCK_TOKENS + t) * group
                    routed_ref[t, head, s * group : (s + 1) * group] = routed[at : at + group]

    lane = lax.broadcasted_iota(jnp.int32, (both, total), 1) // share

    def wire_copy(part, j):
        target = peer(j)
        first, last = parts[part]
        return remote(
            wire_ref.at[target, pl.ds(first, last - first)],
            got_ref.at[j, pl.ds(first, last - first)],
            wire_send.at[part], wire_recv.at[part * 4 + j // depth], target,
        )

    def wires_in(part, quarter):
        first, last = parts[part]
        span = (pl.ds(max(1, quarter * depth), min(depth, quarter * depth + depth - 1)),
                pl.ds(first, last - first))
        return remote(
            wire_ref.at[span], got_ref.at[span],
            wire_send.at[part], wire_recv.at[part * 4 + quarter], peer(1),
        )

    def wires_out(part):
        first, last = parts[part]
        span = (pl.ds(1, holders - 1), pl.ds(first, last - first))
        return remote(
            wire_ref.at[span], got_ref.at[span],
            wire_send.at[part], wire_recv.at[part * 4], peer(1),
        )

    loads[4].wait()
    for at in range(portions):
        gather(0, at)
    for part, (first, last) in enumerate(parts):
        key_rows(2 * first * steps, 2 * last * steps)
        weigh(part)
        for unit in range(first, last):
            cells = [
                routed_ref[t, 2 * unit + h] for t in range(BLOCK_TOKENS) for h in range(2)
            ]
            step = 1
            while step < holders:
                low_side = lane // step % 2 == 0
                turned = list(cells)
                for at in range(holders):
                    if at // step % 2 == 0:
                        a, b = cells[at], cells[at + step]
                        turned[at] = jnp.where(
                            low_side, a, pltpu.roll(b, step * share, 1)
                        )
                        turned[at + step] = jnp.where(
                            low_side, pltpu.roll(a, total - step * share, 1), b
                        )
                cells = turned
                step *= 2
            for holder in range(holders):
                wire_ref[holder, unit] = cells[holder].astype(jnp.bfloat16)
        for j in far_first:
            wire_copy(part, j).start()

    loads[5].wait()
    others = pl.ds(1, holders - 1)
    all_asks = remote(
        send_ref.at[others], ask_ref.at[others], ask_send.at[0], ask_recv.at[0], peer(1)
    )
    all_asks.wait_recv()
    asked_ref[...] = jnp.clip(ask_ref[...], 0, pool_ref.shape[0] - 1)
    row_copy = pltpu.make_async_copy(asked_ref, row_ref, row_sem.at[0])
    row_copy.start()
    row_copy.wait()
    pltpu.make_async_copy(pool_ref, pool_ref, pool_sem.at[0]).wait()

    early = lax.broadcasted_iota(jnp.int32, (both, HEAD_SIZE), 0) < group

    def partial(unit, j):
        arrived = got_ref[j, unit] if j else wire_ref[me, unit]
        weight = jnp.maximum(
            jnp.dot(arrived, spread_ref[...], preferred_element_type=jnp.float32), 0.0
        )
        lhs, columns = [], []
        for h in range(2):
            own = weight[:, h * HEAD_SIZE : (h + 1) * HEAD_SIZE]
            lhs.append(
                jnp.concatenate(
                    [jnp.where(early, own, 0.0), jnp.where(early, 0.0, own)], 1
                ).astype(jnp.bfloat16)
            )
            columns.append(
                jnp.concatenate(
                    [
                        pool_ref[row_ref[j, 0, (s * heads + 2 * unit + h) * share + n]]
                        for s in range(steps)
                        for n in range(share)
                    ],
                    0,
                )
            )
        product = jnp.dot(
            jnp.concatenate(lhs, 0), jnp.concatenate(columns, 1),
            preferred_element_type=jnp.float32,
        )
        return jnp.concatenate([product[:both, :HEAD_SIZE], product[both:, HEAD_SIZE:]], 0)

    own_core = peer(2 * depth)
    own_side = peer(depth)

    def span(part):
        first, last = parts[part]
        return pl.ds(first * 2 * both, (last - first) * 2 * both)

    def core_copy(part, across):
        at = part * 2 + across
        return remote(
            core_out.at[across, :, span(part)], core_in.at[across, :, span(part)],
            core_send.at[at], core_recv.at[at], own_core,
        )

    def side_copy(part):
        return remote(
            side_out.at[:, span(part)], side_in.at[:, span(part)],
            side_send.at[part], side_recv.at[part], own_side,
        )

    def line_copy(part, ahead):
        return remote(
            line_out.at[ahead, span(part)], line_in.at[ahead, span(part)],
            line_send.at[part], line_recv.at[part],
            lax.rem(layer - ahead + depth, depth) * 4 + side * 2 + core,
        )

    def all_lines(part):
        rest = (pl.ds(1, depth - 1), span(part))
        return remote(
            line_out.at[rest], line_in.at[rest], line_send.at[part], line_recv.at[part], peer(1)
        )

    def values_of(part, j):
        return jnp.concatenate([partial(unit, j) for unit in range(*parts[part])], 0)

    def far_stage(part, across):
        first = 2 * depth + across * depth
        wires_in(part, 2 + across).wait_recv()
        values = [values_of(part, first + ahead) for ahead in range(depth)]
        for ahead, value in enumerate(values):
            core_out[across, ahead, span(part)] = value
        core_copy(part, across).start()

    def side_stage(part):
        wires_in(part, 1).wait_recv()
        values = [values_of(part, depth + ahead) for ahead in range(depth)]
        core_copy(part, 1).wait_recv()
        for ahead, value in enumerate(values):
            side_out[ahead, span(part)] = (value + core_in[1, ahead, span(part)]).astype(
                jnp.bfloat16
            )
        side_copy(part).start()

    def line_stage(part):
        wires_in(part, 0).wait_recv()
        values = [values_of(part, ahead) for ahead in range(1, depth)]
        core_copy(part, 0).wait_recv()
        side_copy(part).wait_recv()
        for ahead in range(1, depth):
            value = values[ahead - 1] + core_in[0, ahead, span(part)]
            value = value + side_in[ahead, span(part)].astype(jnp.float32)
            line_out[ahead, span(part)] = value.astype(jnp.bfloat16)
        for ahead in range(1, depth):
            line_copy(part, ahead).start()

    far_stage(0, 1)
    side_stage(0)
    far_stage(1, 1)
    side_stage(1)
    far_stage(0, 0)
    far_stage(2, 1)
    side_stage(2)
    line_stage(0)
    far_stage(1, 0)
    line_stage(1)
    far_stage(2, 0)
    line_stage(2)

    for part in range(len(parts)):
        value = values_of(part, 0) + fresh_ref[span(part)] + core_in[0, 0, span(part)]
        keep_ref[span(part)] = value + side_in[0, span(part)].astype(jnp.float32)
    all_asks.wait_send()
    for part in range(len(parts)):
        wires_out(part).wait_send()
        core_copy(part, 0).wait_send()
        core_copy(part, 1).wait_send()
        side_copy(part).wait_send()
    for part in range(len(parts)):
        all_lines(part).wait_recv()
        value = keep_ref[span(part)]
        for ahead in range(1, depth):
            value = value + line_in[ahead, span(part)].astype(jnp.float32)
        keep_ref[span(part)] = value
    for head in range(heads):
        for g in range(group):
            at = (head * group + g) * HEAD_SIZE
            out_ref[:, at : at + HEAD_SIZE] = jnp.concatenate(
                [
                    keep_ref[head * both + s * group + g : head * both + s * group + g + 1]
                    for s in range(steps)
                ],
                0,
            )

    for part in range(len(parts)):
        all_lines(part).wait_send()


def fused_device(
    queries, new_keys, incoming_values, key_left, right_key_factor, value_tile_store, slot_map,
    chosen, lengths,
):
    holders = lax.axis_size("store")
    steps, _, heads, picks = chosen.shape
    blocks = slot_map.shape[2]
    share = max(1, blocks // holders // 4)
    pool_here = value_tile_store.shape[0]
    group = queries.shape[2] // HEAD_SIZE // heads
    rank = key_left.shape[2]
    slots = steps * heads * share
    rows = steps * heads * group
    both = steps * group
    units = heads // 2
    depth = holders // 4
    half = HEAD_SIZE // 2
    tokens = blocks * BLOCK_TOKENS

    turns = np.arange(tokens)[:, None] * ROPE_BASE ** (-(np.arange(half) * 2.0 / HEAD_SIZE))[None]
    cosine, sine = np.cos(turns), np.sin(turns)
    table = np.concatenate([cosine, cosine, -sine, sine], 1).astype(np.float32)
    ahead = jnp.asarray(table[1 : steps + 1].reshape(2 * steps, HEAD_SIZE))
    table = jnp.asarray(table.reshape(blocks, BLOCK_TOKENS, 2 * HEAD_SIZE))
    expand = np.repeat(np.eye(steps * picks, dtype=np.float32), BLOCK_TOKENS, 1)
    deep = -(-rank // 128) * 128
    wide = BLOCK_TOKENS * 64
    regroup = np.zeros((wide, wide), np.float32)
    for t in range(BLOCK_TOKENS):
        regroup[np.arange(64) * BLOCK_TOKENS + t, t * 64 + np.arange(64)] = 1.0
    spread = np.zeros((BLOCK_TOKENS, 2, share, 2, share, BLOCK_TOKENS, 2), np.float32)
    for t in range(BLOCK_TOKENS):
        for h in range(2):
            for n in range(share):
                spread[t, h, n, h, n, t] = (1.0, -1.0)
    lines = BLOCK_TOKENS * 2 * share
    spread = spread.reshape(lines, 2 * lines)

    vmem = pl.BlockSpec(memory_space=pltpu.VMEM)
    anywhere = pl.BlockSpec(memory_space=pl.ANY)
    bf16, f32 = jnp.bfloat16, jnp.float32
    dma = pltpu.SemaphoreType.DMA
    attended = pl.pallas_call(
        functools.partial(fused_kernel, share, pool_here),
        in_specs=[pl.BlockSpec(memory_space=pltpu.SMEM)] * 2 + [vmem] * 6 + [anywhere] * 7,
        out_specs=vmem,
        out_shape=pltpu.VMEM((steps, heads * group * HEAD_SIZE), f32),
        scratch_shapes=[
            pltpu.VMEM((deep, tokens), bf16),
            pltpu.VMEM((rank, heads * HEAD_SIZE), bf16),
            pltpu.VMEM((steps * picks, steps * picks * BLOCK_TOKENS), bf16),
            pltpu.VMEM((lines, 2 * lines), bf16),
            pltpu.VMEM((wide, wide), bf16),
            pltpu.VMEM((pool_here // 2, 2 * BLOCK_TOKENS, HEAD_SIZE), bf16),
            pltpu.VMEM((blocks, BLOCK_TOKENS, deep + 2 * HEAD_SIZE), f32),
            pltpu.VMEM((holders, 1, slots), jnp.int32),
            pltpu.VMEM((holders, 1, slots), jnp.int32),
            pltpu.VMEM((holders, 1, slots), jnp.int32),
            pltpu.SMEM((holders, 1, slots), jnp.int32),
            pltpu.VMEM((heads, steps * picks), jnp.int32),
            pltpu.VMEM((heads, steps * picks), f32),
            pltpu.VMEM((heads, steps * picks * BLOCK_TOKENS), f32),
            pltpu.VMEM((steps * heads, group, HEAD_SIZE), bf16),
            pltpu.VMEM((heads, both, 8), f32),
            pltpu.VMEM((heads, 8, HEAD_SIZE), bf16),
            pltpu.VMEM((heads, deep, 2 * HEAD_SIZE), bf16),
            pltpu.VMEM((picks * BLOCK_TOKENS, 2 * HEAD_SIZE), f32),
            pltpu.VMEM((picks * BLOCK_TOKENS, 2 * HEAD_SIZE), f32),
            pltpu.VMEM((picks * BLOCK_TOKENS, 2 * HEAD_SIZE), f32),
            pltpu.VMEM((picks * BLOCK_TOKENS, 2 * HEAD_SIZE), f32),
            pltpu.VMEM((heads * steps, group, picks * BLOCK_TOKENS), f32),
            pltpu.VMEM((rows, HEAD_SIZE), f32),
            pltpu.VMEM((BLOCK_TOKENS, heads, both, holders * share), f32),
            pltpu.VMEM((holders, units, both, lines), bf16),
            pltpu.VMEM((holders, units, both, lines), bf16),
            pltpu.VMEM((2, depth, rows, HEAD_SIZE), f32),
            pltpu.VMEM((2, depth, rows, HEAD_SIZE), f32),
            pltpu.VMEM((depth, rows, HEAD_SIZE), bf16),
            pltpu.VMEM((depth, rows, HEAD_SIZE), bf16),
            pltpu.VMEM((depth, rows, HEAD_SIZE), bf16),
            pltpu.VMEM((depth, rows, HEAD_SIZE), bf16),
            pltpu.VMEM((rows, HEAD_SIZE), f32),
            dma((6,)), dma((1,)), dma((1,)), dma((1,)), dma((1,)), dma((3,)), dma((12,)),
            dma((6,)), dma((6,)), dma((3,)), dma((3,)), dma((3,)), dma((3,)),
        ],
        compiler_params=pltpu.CompilerParams(collective_id=0, has_side_effects=True),
        name="fused",
    )(
        lengths, chosen[:, 0].reshape(steps * heads, picks), ahead,
        queries[:, 0], new_keys[:, 0], incoming_values[:, 0],
        chosen[:, 0].reshape(steps * heads, picks), slot_map[0],
        right_key_factor[0], table, jnp.asarray(expand, bf16), jnp.asarray(spread, bf16),
        jnp.asarray(regroup, bf16), key_left[0].T,
        value_tile_store.reshape(pool_here // 8, 8, -1),
    )
    return attended.astype(bf16).reshape(steps, 1, -1)


def solution(mesh):
    in_specs = (
        P(None, ("groups", "store"), None),
        P(None, ("groups", "store"), None),
        P(None, ("groups", "store"), None),
        P(("groups", "store"), None, None),
        P(("groups", "store"), None, None),
        P(("groups", "store"), None),
        P(("groups", "store"), None, None),
        P(None, ("groups", "store"), None, None),
        P(("groups", "store")),
    )
    out_specs = P(None, ("groups", "store"), None)

    def body(*args):
        holders = mesh.shape["store"]
        blocks = args[6].shape[2]
        share = max(1, blocks // holders // 4)
        square = args[7].shape[0] * args[7].shape[2] == holders
        packed = args[7].shape[0] * args[7].shape[3] == holders * share
        fits = square and packed and share == 8 and holders == 16 and blocks % 128 == 0
        return (fused_device if fits else per_device)(*args)

    return jax.shard_map(
        body, mesh=mesh, in_specs=in_specs, out_specs=out_specs, check_vma=False
    )
```

```python
import functools

import jax
import jax.numpy as jnp
import numpy as np
from jax import lax
from jax.experimental import pallas as pl
from jax.experimental.pallas import tpu as pltpu
from jax.sharding import PartitionSpec as P

KEY_VALUE_HEADS = 8
HEAD_SIZE = 128
BLOCK_TOKENS = 8


ROPE_BASE = 500000.0


def apply_rotary(tensor, token_positions):
    half_dim = tensor.shape[-1] // 2
    inverse = ROPE_BASE ** (-(jnp.arange(half_dim, dtype=jnp.float32) * 2.0 / tensor.shape[-1]))
    angles = jnp.asarray(token_positions).astype(jnp.float32)[..., None] * inverse
    cosine = jnp.cos(angles)
    sine_vals = jnp.sin(angles)
    first_half = tensor[..., :half_dim]
    second_half = tensor[..., half_dim:]
    return jnp.concatenate(
        [
            first_half * cosine - second_half * sine_vals,
            second_half * cosine + first_half * sine_vals,
        ],
        -1,
    )


def fetch_tiles(requests, value_tile_store):
    tile_row_index = jnp.take(
        value_tile_store,
        lax.all_to_all(requests, "store", split_axis=0, concat_axis=0, tiled=True),
        axis=0,
    )
    return lax.all_to_all(tile_row_index, "store", split_axis=0, concat_axis=0, tiled=True)


def build_requests(flat_idx, inside, total):
    buffer = jnp.zeros((total,), jnp.int32)
    return buffer.at[flat_idx.reshape(-1)].set(inside.reshape(-1))


def attend_row(
    query_full,
    incoming_keys_full,
    incoming_values_full,
    left_rows,
    right_factor_rows,
    block_numbers,
    tile_row_index,
    length,
    step_index,
):
    query_group_size = query_full.shape[-1] // HEAD_SIZE // KEY_VALUE_HEADS
    every_head = query_group_size * KEY_VALUE_HEADS
    selected_count = block_numbers.shape[1]
    score_scale = HEAD_SIZE ** (-0.5)
    right_factor_heads = right_factor_rows.reshape(
        right_factor_rows.shape[0], KEY_VALUE_HEADS, HEAD_SIZE
    )
    token_positions = (
        block_numbers[:, :, None] * BLOCK_TOKENS + jnp.arange(BLOCK_TOKENS, dtype=jnp.int32)
    ).reshape(KEY_VALUE_HEADS, selected_count * BLOCK_TOKENS)
    picked = left_rows[token_positions]
    raw_keys = jnp.einsum(
        "htr,rhd->htd", picked, right_factor_heads, preferred_element_type=jnp.float32
    )
    cache_keys = apply_rotary(raw_keys, token_positions).astype(jnp.bfloat16)
    rotated_query = apply_rotary(
        query_full[step_index].reshape(every_head, HEAD_SIZE).astype(jnp.float32),
        length + step_index,
    ).astype(jnp.bfloat16)
    current_position = (length + jnp.arange(step_index + 1, dtype=jnp.int32))[:, None]
    current_keys = apply_rotary(
        incoming_keys_full[: step_index + 1]
        .reshape(step_index + 1, KEY_VALUE_HEADS, HEAD_SIZE)
        .astype(jnp.float32),
        current_position,
    ).astype(jnp.bfloat16)
    current_keys = jnp.transpose(current_keys, (1, 0, 2))
    current_values = jnp.transpose(
        incoming_values_full[: step_index + 1].reshape(step_index + 1, KEY_VALUE_HEADS, HEAD_SIZE),
        (1, 0, 2),
    )
    local_values = tile_row_index.reshape(KEY_VALUE_HEADS, selected_count * BLOCK_TOKENS, HEAD_SIZE)
    grouped_queries = rotated_query.reshape(KEY_VALUE_HEADS, query_group_size, HEAD_SIZE)
    cache_scores = (
        jnp.einsum("hgd,htd->hgt", grouped_queries, cache_keys, preferred_element_type=jnp.float32)
        * score_scale
    )
    inside_len = token_positions < length
    cache_scores = jnp.where(inside_len[:, None, :], cache_scores, -jnp.inf)
    fresh_scores = (
        jnp.einsum(
            "hgd,hnd->hgn", grouped_queries, current_keys, preferred_element_type=jnp.float32
        )
        * score_scale
    )
    highest = jnp.maximum(
        jnp.max(cache_scores, -1, keepdims=True), jnp.max(fresh_scores, -1, keepdims=True)
    )
    cache_exp = jnp.exp(cache_scores - highest)
    fresh_exp = jnp.exp(fresh_scores - highest)
    denominator = jnp.sum(cache_exp, -1, keepdims=True) + jnp.sum(fresh_exp, -1, keepdims=True)
    cache_weight = (cache_exp / denominator).astype(jnp.bfloat16)
    fresh_weight = (fresh_exp / denominator).astype(jnp.bfloat16)
    attended = jnp.einsum(
        "hgt,htd->hgd", cache_weight, local_values, preferred_element_type=jnp.float32
    )
    attended = attended + jnp.einsum(
        "hgn,hnd->hgd", fresh_weight, current_values, preferred_element_type=jnp.float32
    )
    return attended.reshape(every_head * HEAD_SIZE).astype(jnp.bfloat16)


def per_device(
    queries,
    new_keys,
    incoming_values,
    key_left,
    right_key_factor,
    value_tile_store,
    slot_map,
    chosen,
    lengths,
):
    nstore = lax.axis_size("store")
    local_rows = key_left.shape[0]
    nchunk = slot_map.shape[2]
    step_count = chosen.shape[0]
    selected_count = chosen.shape[3]
    keeper_share = max(1, nchunk // nstore // 4)
    tile_limit = local_rows * KEY_VALUE_HEADS * keeper_share
    pool_here = value_tile_store.shape[0]
    slot_numbers = jnp.take_along_axis(
        jnp.broadcast_to(slot_map[None], (step_count,) + slot_map.shape), chosen, axis=3
    )
    tile_keeper = slot_numbers // pool_here
    inside = slot_numbers % pool_here
    matched = tile_keeper[..., :, None] == tile_keeper[..., None, :]
    earlier = jnp.arange(selected_count)[None, :] < jnp.arange(selected_count)[:, None]
    order_in = jnp.sum(jnp.logical_and(matched, earlier), -1)
    row_head = (
        jnp.arange(local_rows, dtype=jnp.int32)[:, None, None] * KEY_VALUE_HEADS
        + jnp.arange(KEY_VALUE_HEADS, dtype=jnp.int32)[None, :, None]
    )
    position = row_head * keeper_share + order_in
    tiles_all = []
    slot_span = step_count * tile_limit
    flat_idx = (
        tile_keeper * slot_span
        + jnp.arange(step_count, dtype=jnp.int32)[:, None, None, None] * tile_limit
        + position
    )
    requests = build_requests(flat_idx, inside, nstore * slot_span).reshape(nstore, slot_span)
    received = fetch_tiles(requests, value_tile_store).reshape(nstore * slot_span, -1)
    for step_index in range(step_count):
        tiles_all.append(received[flat_idx[step_index]])
    results = []
    for step_index in range(step_count):
        per_rows = [
            attend_row(
                queries[:, 0],
                new_keys[:, 0],
                incoming_values[:, 0],
                key_left[0],
                right_key_factor[0],
                chosen[step_index, 0],
                tiles_all[step_index][0],
                lengths[0],
                step_index,
            )
        ]
        results.append(jnp.stack(per_rows))
    return jnp.stack(results)


def fused_kernel(
    share, pool_here,
    length_ref, pick_ref, ahead_ref, query_ref, new_key_ref, new_value_ref,
    chosen_ref, slot_ref, right_hbm, table_hbm, expand_hbm, spread_hbm, regroup_hbm, left_hbm,
    pool_hbm,
    out_ref,
    left_ref, right_ref, expand_ref, spread_ref, regroup_ref, pool_ref, block_ref,
    send_ref, ask_ref, asked_ref, row_ref, place_ref, sign_ref, bound_ref,
    rotated_ref, fresh_score_ref, fresh_value_ref, factor_ref, raw_even, raw_odd, turn_even, turn_odd, score_ref, fresh_ref,
    routed_ref, wire_ref, got_ref,
    core_out, core_in, side_out, side_in, line_out, line_in, keep_ref,
    in_sem, pool_sem, row_sem, ask_send, ask_recv, wire_send, wire_recv,
    core_send, core_recv, side_send, side_recv, line_send, line_recv,
):
    me = lax.axis_index("store")
    raw_refs, turn_refs = (raw_even, raw_odd), (turn_even, turn_odd)
    holders = send_ref.shape[0]
    depth = holders // 4
    rows, picks = chosen_ref.shape
    heads, blocks = slot_ref.shape
    steps = rows // heads
    rank = left_hbm.shape[0]
    deep = block_ref.shape[2] - 2 * HEAD_SIZE
    group = query_ref.shape[1] // HEAD_SIZE // heads
    both = steps * group
    half = HEAD_SIZE // 2
    units = heads // 2
    parts = ((0, units - 2), (units - 2, units - 1), (units - 1, units))
    scale = HEAD_SIZE ** (-0.5)
    core, side, layer = lax.rem(me, 2), lax.rem(me // 2, 2), me // 4

    def peer(j):
        far, across, ahead = j // (2 * depth), j // depth % 2, j % depth
        return (
            lax.rem(layer + ahead, depth) * 4
            + (1 - side if across else side) * 2
            + (1 - core if far else core)
        )

    def remote(src, dst, send, recv, target):
        return pltpu.make_async_remote_copy(
            src_ref=src, dst_ref=dst, send_sem=send, recv_sem=recv,
            device_id={"store": target}, device_id_type=pl.DeviceIdType.MESH,
        )

    barrier = pltpu.get_barrier_semaphore()

    def greet(k, _):
        pl.semaphore_signal(
            barrier, inc=1, device_id={"store": lax.rem(me + k, holders)},
            device_id_type=pl.DeviceIdType.MESH,
        )
        return 0

    lax.fori_loop(1, holders, greet, 0)

    loads = [
        pltpu.make_async_copy(src, dst, in_sem.at[at])
        for at, (src, dst) in enumerate(
            (
                (left_hbm, left_ref),
                (right_hbm, right_ref),
                (table_hbm, block_ref.at[:, :, pl.ds(deep, 2 * HEAD_SIZE)]),
                (expand_hbm, expand_ref),
                (regroup_hbm, regroup_ref),
                (spread_hbm, spread_ref),
            )
        )
    ]
    for copy in loads:
        copy.start()
    octets = pool_here // 8
    pool_copies = [
        pltpu.make_async_copy(
            pool_hbm.at[:, pl.ds(2 * q, 2), pl.ds(HEAD_SIZE * t, HEAD_SIZE)],
            pool_ref.at[pl.ds(q * octets, octets), pl.ds(2 * t, 2), :],
            pool_sem.at[0],
        )
        for q in range(4)
        for t in range(BLOCK_TOKENS)
    ]

    total = holders * share
    length = length_ref[0]
    lane_at = lax.broadcasted_iota(jnp.int32, (heads, total), 1)
    first_step = lane_at < picks
    chosen = jnp.concatenate([chosen_ref[s * heads : (s + 1) * heads] for s in range(steps)], 1)
    slot = jnp.zeros((heads, total), jnp.int32)
    for at in range(0, blocks, total):
        found = jnp.take_along_axis(slot_ref[:, at : at + total], chosen & (total - 1), axis=1)
        slot = jnp.where(chosen // total == at // total, found, slot)
    if pool_here & (pool_here - 1) == 0:
        keeper = slot >> (pool_here.bit_length() - 1)
        inside = slot & (pool_here - 1)
    else:
        keeper = lax.div(slot, jnp.full_like(slot, pool_here))
        inside = slot - keeper * pool_here
    sign_ref[...] = (1 - 2 * (inside & 1)).astype(jnp.float32)
    inside = ((inside >> 1) & 3) * octets + (inside >> 3)
    before_row = lax.broadcasted_iota(jnp.int32, (total, total), 0)
    before_lane = lax.broadcasted_iota(jnp.int32, (total, total), 1)
    before = jnp.where(
        jnp.logical_and(before_row < before_lane, before_row // picks == before_lane // picks),
        1.0, 0.0,
    ).astype(jnp.bfloat16)
    mine = [jnp.where(keeper == holder, 1.0, 0.0) for holder in range(holders)]
    counts = jnp.dot(
        jnp.concatenate(mine, 0).astype(jnp.bfloat16), before, preferred_element_type=jnp.float32
    )
    order = jnp.zeros((heads, total), jnp.float32)
    for holder in range(holders):
        order = order + mine[holder] * counts[holder * heads : (holder + 1) * heads]
    place = keeper * share + order.astype(jnp.int32)
    place_ref[...] = place
    digits = []
    for s in range(steps):
        for shift in (0, 8, 16):
            digit = ((inside >> shift) & 255).astype(jnp.float32)
            digits.append(jnp.where(first_step == (s == 0), digit, 0.0))
    slot_at = before_row
    moved = [None] * rows
    for head in range(heads):
        lines = jnp.concatenate(
            [digit[head : head + 1] for digit in digits]
            + [jnp.zeros((8 - len(digits), total), jnp.float32)], 0
        ).astype(jnp.bfloat16)
        table = jnp.where(place[head : head + 1] == slot_at, 1.0, 0.0).astype(jnp.bfloat16)
        found = lax.dot_general(
            lines, table, (((1,), (1,)), ((), ())), preferred_element_type=jnp.float32
        ).astype(jnp.int32)
        for s in range(steps):
            row = s * heads + head
            whole = found[3 * s : 3 * s + 1] + found[3 * s + 1 : 3 * s + 2] * 256
            whole = whole + found[3 * s + 2 : 3 * s + 3] * 65536
            moved[row] = pltpu.roll(whole, row * share, 1) if row else whole
    moved = jnp.concatenate(moved, 0)
    own_lanes = (
        lax.broadcasted_iota(jnp.int32, (rows, total), 1) // share
        == lax.broadcasted_iota(jnp.int32, (rows, total), 0)
    )
    for holder in range(holders):
        turned = pltpu.roll(moved, total - holder * share, 1) if holder else moved
        send_ref[holder] = jnp.sum(jnp.where(own_lanes, turned, 0), 0, keepdims=True)

    def ask_copy(j):
        target = peer(j)
        return remote(
            send_ref.at[target], ask_ref.at[j], ask_send.at[0], ask_recv.at[0], target
        )

    far_first = sorted(
        range(1, holders), key=lambda j: (-(min(j % depth, depth - j % depth)), -j)
    )
    pl.semaphore_wait(barrier, holders - 1)
    for j in far_first:
        ask_copy(j).start()
    ask_ref[0] = send_ref[me]

    loads[1].wait()
    for head in range(heads):
        factor = right_ref[:, head * HEAD_SIZE : (head + 1) * HEAD_SIZE]
        factor_ref[head, :, :HEAD_SIZE] = factor
        factor_ref[head, :, HEAD_SIZE:] = pltpu.roll(
            factor.astype(jnp.float32), half, 1
        ).astype(jnp.bfloat16)
    loads[3].wait()
    remaining = jnp.clip(length - chosen * BLOCK_TOKENS, 0, BLOCK_TOKENS)
    bound_ref[...] = jnp.dot(
        remaining.astype(jnp.float32).astype(jnp.bfloat16), expand_ref[...],
        preferred_element_type=jnp.float32,
    )
    same = jnp.where(before_row == before_lane, 1.0, 0.0).astype(jnp.bfloat16)
    loads[0].wait()
    turned_blocks = total // BLOCK_TOKENS
    for at in range(0, left_ref.shape[1], total):
        turned = lax.dot_general(
            same, left_ref[:, at : at + total], (((1,), (1,)), ((), ())),
            preferred_element_type=jnp.float32,
        )
        first = at // BLOCK_TOKENS
        block_ref[first : first + turned_blocks, :, :rank] = turned.reshape(
            turned_blocks, BLOCK_TOKENS, rank
        )
    loads[2].wait()
    for copy in pool_copies:
        copy.start()

    last = jnp.maximum(length - 1, 0)
    turn = block_ref[last // BLOCK_TOKENS, pl.ds(lax.rem(last, BLOCK_TOKENS), 1), deep:]
    last_cos, last_sin = turn[:, :HEAD_SIZE], turn[:, HEAD_SIZE:]
    spin_cos, spin_sin = [], []
    for s in range(steps):
        more_cos, more_sin = ahead_ref[2 * s : 2 * s + 1], ahead_ref[2 * s + 1 : 2 * s + 2]
        spin_cos.append(
            jnp.broadcast_to(last_cos * more_cos - last_sin * more_sin, (group, HEAD_SIZE))
        )
        spin_sin.append(
            jnp.broadcast_to(last_sin * more_cos + last_cos * more_sin, (group, HEAD_SIZE))
        )
    query_all = query_ref[...].astype(jnp.float32)
    key_all = new_key_ref[...].astype(jnp.float32)
    value_all = new_value_ref[...].astype(jnp.float32)
    fresh_cos = jnp.concatenate([spin_cos[s][:1] for s in range(steps)] + [spin_cos[0][: 8 - steps]], 0)
    fresh_sin = jnp.concatenate([spin_sin[s][:1] for s in range(steps)] + [spin_sin[0][: 8 - steps]], 0)
    both_cos = jnp.concatenate(spin_cos, 0)
    both_sin = jnp.concatenate(spin_sin, 0)
    empty = jnp.zeros((8 - steps, HEAD_SIZE), jnp.float32)
    fresh_keep = (
        lax.broadcasted_iota(jnp.int32, (both, 8), 1)
        <= lax.broadcasted_iota(jnp.int32, (both, 8), 0) // group
    )
    for head in range(heads):
        lanes = slice(head * HEAD_SIZE, (head + 1) * HEAD_SIZE)
        flat = jnp.concatenate(
            [
                query_all[s : s + 1, (head * group + g) * HEAD_SIZE : (head * group + g + 1) * HEAD_SIZE]
                for s in range(steps)
                for g in range(group)
            ],
            0,
        )
        query = (flat * both_cos + pltpu.roll(flat, half, 1) * both_sin).astype(jnp.bfloat16)
        for s in range(steps):
            rotated_ref[s * heads + head] = query[s * group : (s + 1) * group]
        flat = jnp.concatenate([key_all[:, lanes], empty], 0)
        fresh_key = (flat * fresh_cos + pltpu.roll(flat, half, 1) * fresh_sin).astype(jnp.bfloat16)
        fresh = lax.dot_general(
            query, fresh_key, (((1,), (1,)), ((), ())), preferred_element_type=jnp.float32
        ) * scale
        fresh_score_ref[head] = jnp.where(fresh_keep, fresh, -jnp.inf)
        fresh_value_ref[head] = jnp.concatenate([value_all[:, lanes], empty], 0).astype(
            jnp.bfloat16
        )

    token_at = (
        lax.broadcasted_iota(jnp.int32, (group, picks * BLOCK_TOKENS), 1) % BLOCK_TOKENS
    ).astype(jnp.float32)
    low_half = lax.broadcasted_iota(jnp.int32, (group, total), 1) < picks

    portion = 2 * total // BLOCK_TOKENS
    portions = picks // portion

    def gather(row, at):
        head, s = divmod(row, steps)
        found = [
            block_ref[pick_ref[s * heads + head, at * portion + n]] for n in range(portion)
        ]
        span = slice(2 * at * total, 2 * (at + 1) * total)
        raw_refs[row % 2][span] = jnp.dot(
            jnp.concatenate([value[:, :rank] for value in found], 0).astype(jnp.bfloat16),
            factor_ref[head], preferred_element_type=jnp.float32,
        )
        turn_refs[row % 2][span] = jnp.concatenate([value[:, deep:] for value in found], 0)

    def compare(row, at):
        head, s = divmod(row, steps)
        span = slice(2 * at * total, 2 * (at + 1) * total)
        raw = raw_refs[row % 2][span]
        keys = raw * turn_refs[row % 2][span]
        keys = keys[:, :HEAD_SIZE] + keys[:, HEAD_SIZE:]
        score_ref[row, :, span] = lax.dot_general(
            rotated_ref[s * heads + head], keys.astype(jnp.bfloat16), (((1,), (1,)), ((), ())),
            preferred_element_type=jnp.float32,
        )

    def key_rows(first, last):
        for row in range(first, last):
            for at in range(portions):
                if row + 1 < rows:
                    gather(row + 1, at)
                compare(row, at)

    def weigh(part):
        weights = []
        heads_here = range(2 * parts[part][0], 2 * parts[part][1])
        for head in heads_here:
            fresh_weights = []
            for s in range(steps):
                bound = jnp.broadcast_to(
                    bound_ref[head : head + 1, s * picks * BLOCK_TOKENS : (s + 1) * picks * BLOCK_TOKENS],
                    token_at.shape,
                )
                scores = jnp.where(token_at < bound, score_ref[head * steps + s] * scale, -jnp.inf)
                fresh = fresh_score_ref[head, s * group : (s + 1) * group]
                highest = jnp.maximum(
                    jnp.max(scores, -1, keepdims=True), jnp.max(fresh, -1, keepdims=True)
                )
                power = jnp.exp(scores - highest)
                fresh_power = jnp.exp(fresh - highest)
                inverse = 1.0 / (
                    jnp.sum(power, -1, keepdims=True) + jnp.sum(fresh_power, -1, keepdims=True)
                )
                weights.append(power * inverse)
                fresh_weights.append(fresh_power * inverse)
            fresh_ref[head * both : (head + 1) * both] = jnp.dot(
                jnp.concatenate(fresh_weights, 0).astype(jnp.bfloat16), fresh_value_ref[head],
                preferred_element_type=jnp.float32,
            )
        yield
        grouped = jnp.dot(
            jnp.concatenate(weights, 0).astype(jnp.bfloat16), regroup_ref[...],
            preferred_element_type=jnp.float32,
        )
        for h, head in enumerate(heads_here):
            lines = []
            for s in range(steps):
                line = grouped[(h * steps + s) * group : (h * steps + s + 1) * group]
                for t in range(BLOCK_TOKENS):
                    value = line[:, t // 2 * total : (t // 2 + 1) * total]
                    if t % 2 != s:
                        value = pltpu.roll(value, picks, 1)
                    lines.append(
                        jnp.where(low_half, value, 0.0) if s == 0 else jnp.where(low_half, 0.0, value)
                    )
            table = jnp.where(
                place_ref[head : head + 1] == slot_at,
                jnp.broadcast_to(sign_ref[head : head + 1], (total, total)), 0.0,
            ).astype(jnp.bfloat16)
            routed = lax.dot_general(
                jnp.concatenate(lines, 0).astype(jnp.bfloat16), table, (((1,), (1,)), ((), ())),
                preferred_element_type=jnp.float32,
            )
            for s in range(steps):
                for t in range(BLOCK_TOKENS):
                    at = (s * BLOCK_TOKENS + t) * group
                    routed_ref[t, head, s * group : (s + 1) * group] = routed[at : at + group]

    lane = lax.broadcasted_iota(jnp.int32, (both, total), 1) // share

    def wire_copy(part, j):
        target = peer(j)
        first, last = parts[part]
        return remote(
            wire_ref.at[target, pl.ds(first, last - first)],
            got_ref.at[j, pl.ds(first, last - first)],
            wire_send.at[part], wire_recv.at[part * 4 + j // depth], target,
        )

    def wires_in(part, quarter):
        first, last = parts[part]
        span = (pl.ds(max(1, quarter * depth), min(depth, quarter * depth + depth - 1)),
                pl.ds(first, last - first))
        return remote(
            wire_ref.at[span], got_ref.at[span],
            wire_send.at[part], wire_recv.at[part * 4 + quarter], peer(1),
        )

    def wires_out(part):
        first, last = parts[part]
        span = (pl.ds(1, holders - 1), pl.ds(first, last - first))
        return remote(
            wire_ref.at[span], got_ref.at[span],
            wire_send.at[part], wire_recv.at[part * 4], peer(1),
        )

    loads[4].wait()
    for at in range(portions):
        gather(0, at)
    def cross(first, last):
        for unit in range(first, last):
            cells = [
                routed_ref[t, 2 * unit + h] for t in range(BLOCK_TOKENS) for h in range(2)
            ]
            step = 1
            while step < holders:
                low_side = lane // step % 2 == 0
                turned = list(cells)
                for at in range(holders):
                    if at // step % 2 == 0:
                        a, b = cells[at], cells[at + step]
                        turned[at] = jnp.where(
                            low_side, a, pltpu.roll(b, step * share, 1)
                        )
                        turned[at + step] = jnp.where(
                            low_side, pltpu.roll(a, total - step * share, 1), b
                        )
                cells = turned
                step *= 2
            for holder in range(holders):
                wire_ref[holder, unit] = cells[holder].astype(jnp.bfloat16)
    key_rows(0, 2 * parts[0][1] * steps)
    for part, (first, last) in enumerate(parts):
        later = [
            (row, row + 1) for row in range(2 * last * steps, 2 * (last + 1) * steps) if row < rows
        ]
        for _ in weigh(part):
            if later:
                key_rows(*later.pop(0))
        if later:
            key_rows(*later.pop(0))
        cross(first, last)
        if later:
            key_rows(*later.pop(0))
        for j in far_first:
            wire_copy(part, j).start()
        for span_rows in later:
            key_rows(*span_rows)

    loads[5].wait()
    others = pl.ds(1, holders - 1)
    all_asks = remote(
        send_ref.at[others], ask_ref.at[others], ask_send.at[0], ask_recv.at[0], peer(1)
    )
    all_asks.wait_recv()
    asked_ref[...] = jnp.clip(ask_ref[...], 0, pool_ref.shape[0] - 1)
    row_copy = pltpu.make_async_copy(asked_ref, row_ref, row_sem.at[0])
    row_copy.start()
    row_copy.wait()
    pltpu.make_async_copy(pool_ref, pool_ref, pool_sem.at[0]).wait()

    early = lax.broadcasted_iota(jnp.int32, (both, HEAD_SIZE), 0) < group

    def partials(pieces):
        arrived = [got_ref[j, unit] if j else wire_ref[me, unit] for unit, j in pieces]
        weight = jnp.maximum(
            jnp.dot(
                jnp.concatenate(arrived, 0), spread_ref[...], preferred_element_type=jnp.float32
            ),
            0.0,
        )
        return [
            partial(unit, j, weight[at * both : (at + 1) * both])
            for at, (unit, j) in enumerate(pieces)
        ]

    def partial(unit, j, weight):
        lhs, columns = [], []
        for h in range(2):
            own = weight[:, h * HEAD_SIZE : (h + 1) * HEAD_SIZE]
            lhs.append(
                jnp.concatenate(
                    [jnp.where(early, own, 0.0), jnp.where(early, 0.0, own)], 1
                ).astype(jnp.bfloat16)
            )
            columns.append(
                jnp.concatenate(
                    [
                        pool_ref[row_ref[j, 0, (s * heads + 2 * unit + h) * share + n]]
                        for s in range(steps)
                        for n in range(share)
                    ],
                    0,
                )
            )
        product = jnp.dot(
            jnp.concatenate(lhs, 0), jnp.concatenate(columns, 1),
            preferred_element_type=jnp.float32,
        )
        return jnp.concatenate([product[:both, :HEAD_SIZE], product[both:, HEAD_SIZE:]], 0)

    own_core = peer(2 * depth)
    own_side = peer(depth)

    def span(part):
        first, last = parts[part]
        return pl.ds(first * 2 * both, (last - first) * 2 * both)

    def core_copy(part, across):
        at = part * 2 + across
        return remote(
            core_out.at[across, :, span(part)], core_in.at[across, :, span(part)],
            core_send.at[at], core_recv.at[at], own_core,
        )

    def side_copy(part):
        return remote(
            side_out.at[:, span(part)], side_in.at[:, span(part)],
            side_send.at[part], side_recv.at[part], own_side,
        )

    def line_copy(part, ahead):
        return remote(
            line_out.at[ahead, span(part)], line_in.at[ahead, span(part)],
            line_send.at[part], line_recv.at[part],
            lax.rem(layer - ahead + depth, depth) * 4 + side * 2 + core,
        )

    def all_lines(part):
        rest = (pl.ds(1, depth - 1), span(part))
        return remote(
            line_out.at[rest], line_in.at[rest], line_send.at[part], line_recv.at[part], peer(1)
        )

    def values_of(part, js):
        units_here = range(*parts[part])
        found = partials([(unit, j) for j in js for unit in units_here])
        count = len(units_here)
        return [
            jnp.concatenate(found[at * count : (at + 1) * count], 0) for at in range(len(js))
        ]

    def far_stage(part, across):
        first = 2 * depth + across * depth
        wires_in(part, 2 + across).wait_recv()
        values = values_of(part, range(first, first + depth))
        for ahead, value in enumerate(values):
            core_out[across, ahead, span(part)] = value
        core_copy(part, across).start()

    def side_stage(part):
        wires_in(part, 1).wait_recv()
        values = values_of(part, range(depth, 2 * depth))
        core_copy(part, 1).wait_recv()
        for ahead, value in enumerate(values):
            side_out[ahead, span(part)] = (value + core_in[1, ahead, span(part)]).astype(
                jnp.bfloat16
            )
        side_copy(part).start()

    def line_stage(part):
        wires_in(part, 0).wait_recv()
        values = values_of(part, range(1, depth))
        core_copy(part, 0).wait_recv()
        side_copy(part).wait_recv()
        for ahead in range(1, depth):
            value = values[ahead - 1] + core_in[0, ahead, span(part)]
            value = value + side_in[ahead, span(part)].astype(jnp.float32)
            line_out[ahead, span(part)] = value.astype(jnp.bfloat16)
        for ahead in reversed(range(1, depth)):
            line_copy(part, ahead).start()

    far_stage(0, 1)
    side_stage(0)
    far_stage(1, 1)
    side_stage(1)
    far_stage(0, 0)
    far_stage(2, 1)
    side_stage(2)
    line_stage(0)
    far_stage(1, 0)
    line_stage(1)
    far_stage(2, 0)
    line_stage(2)

    own = partials([(unit, 0) for unit in range(units)])
    keep_ref[...] = (
        jnp.concatenate(own, 0) + fresh_ref[...] + core_in[0, 0] + side_in[0].astype(jnp.float32)
    )
    all_asks.wait_send()
    for part in range(len(parts)):
        wires_out(part).wait_send()
        core_copy(part, 0).wait_send()
        core_copy(part, 1).wait_send()
        side_copy(part).wait_send()
    for part in range(len(parts)):
        all_lines(part).wait_recv()
        value = keep_ref[span(part)]
        for ahead in range(1, depth):
            value = value + line_in[ahead, span(part)].astype(jnp.float32)
        keep_ref[span(part)] = value
    for head in range(heads):
        for g in range(group):
            at = (head * group + g) * HEAD_SIZE
            out_ref[:, at : at + HEAD_SIZE] = jnp.concatenate(
                [
                    keep_ref[head * both + s * group + g : head * both + s * group + g + 1]
                    for s in range(steps)
                ],
                0,
            )

    for part in range(len(parts)):
        all_lines(part).wait_send()


def fused_device(
    queries, new_keys, incoming_values, key_left, right_key_factor, value_tile_store, slot_map,
    chosen, lengths,
):
    holders = lax.axis_size("store")
    steps, _, heads, picks = chosen.shape
    blocks = slot_map.shape[2]
    share = max(1, blocks // holders // 4)
    pool_here = value_tile_store.shape[0]
    group = queries.shape[2] // HEAD_SIZE // heads
    rank = key_left.shape[2]
    slots = steps * heads * share
    rows = steps * heads * group
    both = steps * group
    units = heads // 2
    depth = holders // 4
    half = HEAD_SIZE // 2
    tokens = blocks * BLOCK_TOKENS

    turns = np.arange(tokens)[:, None] * ROPE_BASE ** (-(np.arange(half) * 2.0 / HEAD_SIZE))[None]
    cosine, sine = np.cos(turns), np.sin(turns)
    table = np.concatenate([cosine, cosine, -sine, sine], 1).astype(np.float32)
    ahead = jnp.asarray(table[1 : steps + 1].reshape(2 * steps, HEAD_SIZE))
    table = jnp.asarray(table.reshape(blocks, BLOCK_TOKENS, 2 * HEAD_SIZE))
    expand = np.repeat(np.eye(steps * picks, dtype=np.float32), BLOCK_TOKENS, 1)
    deep = -(-rank // 128) * 128
    wide = BLOCK_TOKENS * 64
    regroup = np.zeros((wide, wide), np.float32)
    for t in range(BLOCK_TOKENS):
        regroup[np.arange(64) * BLOCK_TOKENS + t, t * 64 + np.arange(64)] = 1.0
    spread = np.zeros((BLOCK_TOKENS, 2, share, 2, share, BLOCK_TOKENS, 2), np.float32)
    for t in range(BLOCK_TOKENS):
        for h in range(2):
            for n in range(share):
                spread[t, h, n, h, n, t] = (1.0, -1.0)
    lines = BLOCK_TOKENS * 2 * share
    spread = spread.reshape(lines, 2 * lines)

    vmem = pl.BlockSpec(memory_space=pltpu.VMEM)
    anywhere = pl.BlockSpec(memory_space=pl.ANY)
    bf16, f32 = jnp.bfloat16, jnp.float32
    dma = pltpu.SemaphoreType.DMA
    attended = pl.pallas_call(
        functools.partial(fused_kernel, share, pool_here),
        in_specs=[pl.BlockSpec(memory_space=pltpu.SMEM)] * 2 + [vmem] * 6 + [anywhere] * 7,
        out_specs=vmem,
        out_shape=pltpu.VMEM((steps, heads * group * HEAD_SIZE), f32),
        scratch_shapes=[
            pltpu.VMEM((rank, tokens), bf16),
            pltpu.VMEM((rank, heads * HEAD_SIZE), bf16),
            pltpu.VMEM((steps * picks, steps * picks * BLOCK_TOKENS), bf16),
            pltpu.VMEM((lines, 2 * lines), bf16),
            pltpu.VMEM((wide, wide), bf16),
            pltpu.VMEM((pool_here // 2, 2 * BLOCK_TOKENS, HEAD_SIZE), bf16),
            pltpu.VMEM((blocks, BLOCK_TOKENS, deep + 2 * HEAD_SIZE), f32),
            pltpu.VMEM((holders, 1, slots), jnp.int32),
            pltpu.VMEM((holders, 1, slots), jnp.int32),
            pltpu.VMEM((holders, 1, slots), jnp.int32),
            pltpu.SMEM((holders, 1, slots), jnp.int32),
            pltpu.VMEM((heads, steps * picks), jnp.int32),
            pltpu.VMEM((heads, steps * picks), f32),
            pltpu.VMEM((heads, steps * picks * BLOCK_TOKENS), f32),
            pltpu.VMEM((steps * heads, group, HEAD_SIZE), bf16),
            pltpu.VMEM((heads, both, 8), f32),
            pltpu.VMEM((heads, 8, HEAD_SIZE), bf16),
            pltpu.VMEM((heads, rank, 2 * HEAD_SIZE), bf16),
            pltpu.VMEM((picks * BLOCK_TOKENS, 2 * HEAD_SIZE), f32),
            pltpu.VMEM((picks * BLOCK_TOKENS, 2 * HEAD_SIZE), f32),
            pltpu.VMEM((picks * BLOCK_TOKENS, 2 * HEAD_SIZE), f32),
            pltpu.VMEM((picks * BLOCK_TOKENS, 2 * HEAD_SIZE), f32),
            pltpu.VMEM((heads * steps, group, picks * BLOCK_TOKENS), f32),
            pltpu.VMEM((rows, HEAD_SIZE), f32),
            pltpu.VMEM((BLOCK_TOKENS, heads, both, holders * share), f32),
            pltpu.VMEM((holders, units, both, lines), bf16),
            pltpu.VMEM((holders, units, both, lines), bf16),
            pltpu.VMEM((2, depth, rows, HEAD_SIZE), f32),
            pltpu.VMEM((2, depth, rows, HEAD_SIZE), f32),
            pltpu.VMEM((depth, rows, HEAD_SIZE), bf16),
            pltpu.VMEM((depth, rows, HEAD_SIZE), bf16),
            pltpu.VMEM((depth, rows, HEAD_SIZE), bf16),
            pltpu.VMEM((depth, rows, HEAD_SIZE), bf16),
            pltpu.VMEM((rows, HEAD_SIZE), f32),
            dma((6,)), dma((1,)), dma((1,)), dma((1,)), dma((1,)), dma((3,)), dma((12,)),
            dma((6,)), dma((6,)), dma((3,)), dma((3,)), dma((3,)), dma((3,)),
        ],
        compiler_params=pltpu.CompilerParams(collective_id=0, has_side_effects=True),
        name="fused",
    )(
        lengths, chosen[:, 0].reshape(steps * heads, picks), ahead,
        queries[:, 0], new_keys[:, 0], incoming_values[:, 0],
        chosen[:, 0].reshape(steps * heads, picks), slot_map[0],
        right_key_factor[0], table, jnp.asarray(expand, bf16), jnp.asarray(spread, bf16),
        jnp.asarray(regroup, bf16), key_left[0].T,
        value_tile_store.reshape(pool_here // 8, 8, -1),
    )
    return attended.astype(bf16).reshape(steps, 1, -1)


def solution(mesh):
    in_specs = (
        P(None, ("groups", "store"), None),
        P(None, ("groups", "store"), None),
        P(None, ("groups", "store"), None),
        P(("groups", "store"), None, None),
        P(("groups", "store"), None, None),
        P(("groups", "store"), None),
        P(("groups", "store"), None, None),
        P(None, ("groups", "store"), None, None),
        P(("groups", "store")),
    )
    out_specs = P(None, ("groups", "store"), None)

    def body(*args):
        holders = mesh.shape["store"]
        blocks = args[6].shape[2]
        share = max(1, blocks // holders // 4)
        square = args[7].shape[0] * args[7].shape[2] == holders
        packed = args[7].shape[0] * args[7].shape[3] == holders * share
        fits = square and packed and share == 8 and holders == 16 and blocks % 128 == 0
        return (fused_device if fits else per_device)(*args)

    return jax.shard_map(
        body, mesh=mesh, in_specs=in_specs, out_specs=out_specs, check_vma=False
    )
```

```python
import functools

import jax
import jax.numpy as jnp
import numpy as np
from jax import lax
from jax.experimental import pallas as pl
from jax.experimental.pallas import tpu as pltpu
from jax.sharding import PartitionSpec as P

KEY_VALUE_HEADS = 8
HEAD_SIZE = 128
BLOCK_TOKENS = 8


ROPE_BASE = 500000.0


def apply_rotary(tensor, token_positions):
    half_dim = tensor.shape[-1] // 2
    inverse = ROPE_BASE ** (-(jnp.arange(half_dim, dtype=jnp.float32) * 2.0 / tensor.shape[-1]))
    angles = jnp.asarray(token_positions).astype(jnp.float32)[..., None] * inverse
    cosine = jnp.cos(angles)
    sine_vals = jnp.sin(angles)
    first_half = tensor[..., :half_dim]
    second_half = tensor[..., half_dim:]
    return jnp.concatenate(
        [
            first_half * cosine - second_half * sine_vals,
            second_half * cosine + first_half * sine_vals,
        ],
        -1,
    )


def fetch_tiles(requests, value_tile_store):
    tile_row_index = jnp.take(
        value_tile_store,
        lax.all_to_all(requests, "store", split_axis=0, concat_axis=0, tiled=True),
        axis=0,
    )
    return lax.all_to_all(tile_row_index, "store", split_axis=0, concat_axis=0, tiled=True)


def build_requests(flat_idx, inside, total):
    buffer = jnp.zeros((total,), jnp.int32)
    return buffer.at[flat_idx.reshape(-1)].set(inside.reshape(-1))


def attend_row(
    query_full,
    incoming_keys_full,
    incoming_values_full,
    left_rows,
    right_factor_rows,
    block_numbers,
    tile_row_index,
    length,
    step_index,
):
    query_group_size = query_full.shape[-1] // HEAD_SIZE // KEY_VALUE_HEADS
    every_head = query_group_size * KEY_VALUE_HEADS
    selected_count = block_numbers.shape[1]
    score_scale = HEAD_SIZE ** (-0.5)
    right_factor_heads = right_factor_rows.reshape(
        right_factor_rows.shape[0], KEY_VALUE_HEADS, HEAD_SIZE
    )
    token_positions = (
        block_numbers[:, :, None] * BLOCK_TOKENS + jnp.arange(BLOCK_TOKENS, dtype=jnp.int32)
    ).reshape(KEY_VALUE_HEADS, selected_count * BLOCK_TOKENS)
    picked = left_rows[token_positions]
    raw_keys = jnp.einsum(
        "htr,rhd->htd", picked, right_factor_heads, preferred_element_type=jnp.float32
    )
    cache_keys = apply_rotary(raw_keys, token_positions).astype(jnp.bfloat16)
    rotated_query = apply_rotary(
        query_full[step_index].reshape(every_head, HEAD_SIZE).astype(jnp.float32),
        length + step_index,
    ).astype(jnp.bfloat16)
    current_position = (length + jnp.arange(step_index + 1, dtype=jnp.int32))[:, None]
    current_keys = apply_rotary(
        incoming_keys_full[: step_index + 1]
        .reshape(step_index + 1, KEY_VALUE_HEADS, HEAD_SIZE)
        .astype(jnp.float32),
        current_position,
    ).astype(jnp.bfloat16)
    current_keys = jnp.transpose(current_keys, (1, 0, 2))
    current_values = jnp.transpose(
        incoming_values_full[: step_index + 1].reshape(step_index + 1, KEY_VALUE_HEADS, HEAD_SIZE),
        (1, 0, 2),
    )
    local_values = tile_row_index.reshape(KEY_VALUE_HEADS, selected_count * BLOCK_TOKENS, HEAD_SIZE)
    grouped_queries = rotated_query.reshape(KEY_VALUE_HEADS, query_group_size, HEAD_SIZE)
    cache_scores = (
        jnp.einsum("hgd,htd->hgt", grouped_queries, cache_keys, preferred_element_type=jnp.float32)
        * score_scale
    )
    inside_len = token_positions < length
    cache_scores = jnp.where(inside_len[:, None, :], cache_scores, -jnp.inf)
    fresh_scores = (
        jnp.einsum(
            "hgd,hnd->hgn", grouped_queries, current_keys, preferred_element_type=jnp.float32
        )
        * score_scale
    )
    highest = jnp.maximum(
        jnp.max(cache_scores, -1, keepdims=True), jnp.max(fresh_scores, -1, keepdims=True)
    )
    cache_exp = jnp.exp(cache_scores - highest)
    fresh_exp = jnp.exp(fresh_scores - highest)
    denominator = jnp.sum(cache_exp, -1, keepdims=True) + jnp.sum(fresh_exp, -1, keepdims=True)
    cache_weight = (cache_exp / denominator).astype(jnp.bfloat16)
    fresh_weight = (fresh_exp / denominator).astype(jnp.bfloat16)
    attended = jnp.einsum(
        "hgt,htd->hgd", cache_weight, local_values, preferred_element_type=jnp.float32
    )
    attended = attended + jnp.einsum(
        "hgn,hnd->hgd", fresh_weight, current_values, preferred_element_type=jnp.float32
    )
    return attended.reshape(every_head * HEAD_SIZE).astype(jnp.bfloat16)


def per_device(
    queries,
    new_keys,
    incoming_values,
    key_left,
    right_key_factor,
    value_tile_store,
    slot_map,
    chosen,
    lengths,
):
    nstore = lax.axis_size("store")
    local_rows = key_left.shape[0]
    nchunk = slot_map.shape[2]
    step_count = chosen.shape[0]
    selected_count = chosen.shape[3]
    keeper_share = max(1, nchunk // nstore // 4)
    tile_limit = local_rows * KEY_VALUE_HEADS * keeper_share
    pool_here = value_tile_store.shape[0]
    slot_numbers = jnp.take_along_axis(
        jnp.broadcast_to(slot_map[None], (step_count,) + slot_map.shape), chosen, axis=3
    )
    tile_keeper = slot_numbers // pool_here
    inside = slot_numbers % pool_here
    matched = tile_keeper[..., :, None] == tile_keeper[..., None, :]
    earlier = jnp.arange(selected_count)[None, :] < jnp.arange(selected_count)[:, None]
    order_in = jnp.sum(jnp.logical_and(matched, earlier), -1)
    row_head = (
        jnp.arange(local_rows, dtype=jnp.int32)[:, None, None] * KEY_VALUE_HEADS
        + jnp.arange(KEY_VALUE_HEADS, dtype=jnp.int32)[None, :, None]
    )
    position = row_head * keeper_share + order_in
    tiles_all = []
    slot_span = step_count * tile_limit
    flat_idx = (
        tile_keeper * slot_span
        + jnp.arange(step_count, dtype=jnp.int32)[:, None, None, None] * tile_limit
        + position
    )
    requests = build_requests(flat_idx, inside, nstore * slot_span).reshape(nstore, slot_span)
    received = fetch_tiles(requests, value_tile_store).reshape(nstore * slot_span, -1)
    for step_index in range(step_count):
        tiles_all.append(received[flat_idx[step_index]])
    results = []
    for step_index in range(step_count):
        per_rows = [
            attend_row(
                queries[:, 0],
                new_keys[:, 0],
                incoming_values[:, 0],
                key_left[0],
                right_key_factor[0],
                chosen[step_index, 0],
                tiles_all[step_index][0],
                lengths[0],
                step_index,
            )
        ]
        results.append(jnp.stack(per_rows))
    return jnp.stack(results)


def fused_kernel(
    share, pool_here,
    length_ref, pick_ref, ahead_ref, query_ref, new_key_ref, new_value_ref,
    chosen_ref, slot_ref, right_hbm, table_hbm, expand_hbm, spread_hbm, regroup_hbm, left_hbm,
    pool_hbm,
    out_ref,
    left_ref, right_ref, expand_ref, spread_ref, regroup_ref, pool_ref, block_ref,
    send_ref, ask_ref, asked_ref, row_ref, place_ref, sign_ref, bound_ref,
    rotated_ref, fresh_score_ref, fresh_value_ref, factor_ref, raw_even, raw_odd, turn_even, turn_odd, score_ref, fresh_ref,
    routed_ref, wire_ref, got_ref,
    core_out, core_in, last_out, last_in, keep_ref,
    in_sem, pool_sem, row_sem, ask_send, ask_recv, wire_send, wire_recv,
    core_send, core_recv, last_send, last_recv,
):
    me = lax.axis_index("store")
    raw_refs, turn_refs = (raw_even, raw_odd), (turn_even, turn_odd)
    holders = send_ref.shape[0]
    depth = holders // 4
    rows, picks = chosen_ref.shape
    heads, blocks = slot_ref.shape
    steps = rows // heads
    rank = left_hbm.shape[0]
    deep = block_ref.shape[2] - 2 * HEAD_SIZE
    group = query_ref.shape[1] // HEAD_SIZE // heads
    both = steps * group
    half = HEAD_SIZE // 2
    units = heads // 2
    parts = ((0, units - 2), (units - 2, units - 1), (units - 1, units))
    scale = HEAD_SIZE ** (-0.5)
    core, side, layer = lax.rem(me, 2), lax.rem(me // 2, 2), me // 4

    def peer(j):
        far, across, ahead = j // (2 * depth), j // depth % 2, j % depth
        return (
            lax.rem(layer + ahead, depth) * 4
            + (1 - side if across else side) * 2
            + (1 - core if far else core)
        )

    def remote(src, dst, send, recv, target):
        return pltpu.make_async_remote_copy(
            src_ref=src, dst_ref=dst, send_sem=send, recv_sem=recv,
            device_id={"store": target}, device_id_type=pl.DeviceIdType.MESH,
        )

    barrier = pltpu.get_barrier_semaphore()

    def greet(k, _):
        pl.semaphore_signal(
            barrier, inc=1, device_id={"store": lax.rem(me + k, holders)},
            device_id_type=pl.DeviceIdType.MESH,
        )
        return 0

    lax.fori_loop(1, holders, greet, 0)

    loads = [
        pltpu.make_async_copy(src, dst, in_sem.at[at])
        for at, (src, dst) in enumerate(
            (
                (left_hbm, left_ref),
                (right_hbm, right_ref),
                (table_hbm, block_ref.at[:, :, pl.ds(deep, 2 * HEAD_SIZE)]),
                (expand_hbm, expand_ref),
                (regroup_hbm, regroup_ref),
                (spread_hbm, spread_ref),
            )
        )
    ]
    for copy in loads:
        copy.start()
    octets = pool_here // 8
    pool_copies = [
        pltpu.make_async_copy(
            pool_hbm.at[:, pl.ds(2 * q, 2), pl.ds(HEAD_SIZE * t, HEAD_SIZE)],
            pool_ref.at[pl.ds(q * octets, octets), pl.ds(2 * t, 2), :],
            pool_sem.at[0],
        )
        for q in range(4)
        for t in range(BLOCK_TOKENS)
    ]

    total = holders * share
    length = length_ref[0]
    lane_at = lax.broadcasted_iota(jnp.int32, (heads, total), 1)
    first_step = lane_at < picks
    chosen = jnp.concatenate([chosen_ref[s * heads : (s + 1) * heads] for s in range(steps)], 1)
    slot = jnp.zeros((heads, total), jnp.int32)
    for at in range(0, blocks, total):
        found = jnp.take_along_axis(slot_ref[:, at : at + total], chosen & (total - 1), axis=1)
        slot = jnp.where(chosen // total == at // total, found, slot)
    if pool_here & (pool_here - 1) == 0:
        keeper = slot >> (pool_here.bit_length() - 1)
        inside = slot & (pool_here - 1)
    else:
        keeper = lax.div(slot, jnp.full_like(slot, pool_here))
        inside = slot - keeper * pool_here
    sign_ref[...] = (1 - 2 * (inside & 1)).astype(jnp.float32)
    inside = ((inside >> 1) & 3) * octets + (inside >> 3)
    before_row = lax.broadcasted_iota(jnp.int32, (total, total), 0)
    before_lane = lax.broadcasted_iota(jnp.int32, (total, total), 1)
    before = jnp.where(
        jnp.logical_and(before_row < before_lane, before_row // picks == before_lane // picks),
        1.0, 0.0,
    ).astype(jnp.bfloat16)
    mine = [jnp.where(keeper == holder, 1.0, 0.0) for holder in range(holders)]
    counts = jnp.dot(
        jnp.concatenate(mine, 0).astype(jnp.bfloat16), before, preferred_element_type=jnp.float32
    )
    order = jnp.zeros((heads, total), jnp.float32)
    for holder in range(holders):
        order = order + mine[holder] * counts[holder * heads : (holder + 1) * heads]
    place = keeper * share + order.astype(jnp.int32)
    place_ref[...] = place
    digits = []
    for s in range(steps):
        for shift in (0, 8, 16):
            digit = ((inside >> shift) & 255).astype(jnp.float32)
            digits.append(jnp.where(first_step == (s == 0), digit, 0.0))
    slot_at = before_row
    moved = [None] * rows
    for head in range(heads):
        lines = jnp.concatenate(
            [digit[head : head + 1] for digit in digits]
            + [jnp.zeros((8 - len(digits), total), jnp.float32)], 0
        ).astype(jnp.bfloat16)
        table = jnp.where(place[head : head + 1] == slot_at, 1.0, 0.0).astype(jnp.bfloat16)
        found = lax.dot_general(
            lines, table, (((1,), (1,)), ((), ())), preferred_element_type=jnp.float32
        ).astype(jnp.int32)
        for s in range(steps):
            row = s * heads + head
            whole = found[3 * s : 3 * s + 1] + found[3 * s + 1 : 3 * s + 2] * 256
            whole = whole + found[3 * s + 2 : 3 * s + 3] * 65536
            moved[row] = pltpu.roll(whole, row * share, 1) if row else whole
    moved = jnp.concatenate(moved, 0)
    own_lanes = (
        lax.broadcasted_iota(jnp.int32, (rows, total), 1) // share
        == lax.broadcasted_iota(jnp.int32, (rows, total), 0)
    )
    for holder in range(holders):
        turned = pltpu.roll(moved, total - holder * share, 1) if holder else moved
        send_ref[holder] = jnp.sum(jnp.where(own_lanes, turned, 0), 0, keepdims=True)

    def ask_copy(j):
        target = peer(j)
        return remote(
            send_ref.at[target], ask_ref.at[j], ask_send.at[0], ask_recv.at[0], target
        )

    turn_of = (3, 2, 1, 0)
    far_first = sorted(
        range(1, holders),
        key=lambda j: (turn_of[j // depth], -min(j % depth, depth - j % depth)),
    )
    pl.semaphore_wait(barrier, holders - 1)
    for j in far_first:
        ask_copy(j).start()
    ask_ref[0] = send_ref[me]

    loads[1].wait()
    for head in range(heads):
        factor = right_ref[:, head * HEAD_SIZE : (head + 1) * HEAD_SIZE]
        factor_ref[head, :, :HEAD_SIZE] = factor
        factor_ref[head, :, HEAD_SIZE:] = pltpu.roll(
            factor.astype(jnp.float32), half, 1
        ).astype(jnp.bfloat16)
    loads[3].wait()
    remaining = jnp.clip(length - chosen * BLOCK_TOKENS, 0, BLOCK_TOKENS)
    bound_ref[...] = jnp.dot(
        remaining.astype(jnp.float32).astype(jnp.bfloat16), expand_ref[...],
        preferred_element_type=jnp.float32,
    )
    same = jnp.where(before_row == before_lane, 1.0, 0.0).astype(jnp.bfloat16)
    loads[0].wait()
    turned_blocks = total // BLOCK_TOKENS
    for at in range(0, left_ref.shape[1], total):
        if at // total % 2 == 1:
            turned = left_ref[:, at : at + total].astype(jnp.float32).T
        else:
            turned = lax.dot_general(
                same, left_ref[:, at : at + total], (((1,), (1,)), ((), ())),
                preferred_element_type=jnp.float32,
            )
        first = at // BLOCK_TOKENS
        block_ref[first : first + turned_blocks, :, :rank] = turned.reshape(
            turned_blocks, BLOCK_TOKENS, rank
        )
    loads[2].wait()
    for copy in pool_copies:
        copy.start()

    last = jnp.maximum(length - 1, 0)
    turn = block_ref[last // BLOCK_TOKENS, pl.ds(lax.rem(last, BLOCK_TOKENS), 1), deep:]
    last_cos, last_sin = turn[:, :HEAD_SIZE], turn[:, HEAD_SIZE:]
    spin_cos, spin_sin = [], []
    for s in range(steps):
        more_cos, more_sin = ahead_ref[2 * s : 2 * s + 1], ahead_ref[2 * s + 1 : 2 * s + 2]
        spin_cos.append(
            jnp.broadcast_to(last_cos * more_cos - last_sin * more_sin, (group, HEAD_SIZE))
        )
        spin_sin.append(
            jnp.broadcast_to(last_sin * more_cos + last_cos * more_sin, (group, HEAD_SIZE))
        )
    query_all = query_ref[...].astype(jnp.float32)
    key_all = new_key_ref[...].astype(jnp.float32)
    value_all = new_value_ref[...].astype(jnp.float32)
    fresh_cos = jnp.concatenate([spin_cos[s][:1] for s in range(steps)] + [spin_cos[0][: 8 - steps]], 0)
    fresh_sin = jnp.concatenate([spin_sin[s][:1] for s in range(steps)] + [spin_sin[0][: 8 - steps]], 0)
    both_cos = jnp.concatenate(spin_cos, 0)
    both_sin = jnp.concatenate(spin_sin, 0)
    empty = jnp.zeros((8 - steps, HEAD_SIZE), jnp.float32)
    fresh_keep = (
        lax.broadcasted_iota(jnp.int32, (both, 8), 1)
        <= lax.broadcasted_iota(jnp.int32, (both, 8), 0) // group
    )
    for head in range(heads):
        lanes = slice(head * HEAD_SIZE, (head + 1) * HEAD_SIZE)
        flat = jnp.concatenate(
            [
                query_all[s : s + 1, (head * group + g) * HEAD_SIZE : (head * group + g + 1) * HEAD_SIZE]
                for s in range(steps)
                for g in range(group)
            ],
            0,
        )
        query = (flat * both_cos + pltpu.roll(flat, half, 1) * both_sin).astype(jnp.bfloat16)
        for s in range(steps):
            rotated_ref[s * heads + head] = query[s * group : (s + 1) * group]
        flat = jnp.concatenate([key_all[:, lanes], empty], 0)
        fresh_key = (flat * fresh_cos + pltpu.roll(flat, half, 1) * fresh_sin).astype(jnp.bfloat16)
        fresh = lax.dot_general(
            query, fresh_key, (((1,), (1,)), ((), ())), preferred_element_type=jnp.float32
        ) * scale
        fresh_score_ref[head] = jnp.where(fresh_keep, fresh, -jnp.inf)
        fresh_value_ref[head] = jnp.concatenate([value_all[:, lanes], empty], 0).astype(
            jnp.bfloat16
        )

    token_at = (
        lax.broadcasted_iota(jnp.int32, (group, picks * BLOCK_TOKENS), 1) % BLOCK_TOKENS
    ).astype(jnp.float32)
    low_half = lax.broadcasted_iota(jnp.int32, (group, total), 1) < picks

    portion = 2 * total // BLOCK_TOKENS
    portions = picks // portion

    def gather(row, at):
        head, s = divmod(row, steps)
        found = [
            block_ref[pick_ref[s * heads + head, at * portion + n]] for n in range(portion)
        ]
        span = slice(2 * at * total, 2 * (at + 1) * total)
        raw_refs[row % 2][span] = jnp.dot(
            jnp.concatenate([value[:, :rank] for value in found], 0).astype(jnp.bfloat16),
            factor_ref[head], preferred_element_type=jnp.float32,
        )
        turn_refs[row % 2][span] = jnp.concatenate([value[:, deep:] for value in found], 0)

    def compare(row, at):
        head, s = divmod(row, steps)
        span = slice(2 * at * total, 2 * (at + 1) * total)
        raw = raw_refs[row % 2][span]
        keys = raw * turn_refs[row % 2][span]
        keys = keys[:, :HEAD_SIZE] + keys[:, HEAD_SIZE:]
        score_ref[row, :, span] = lax.dot_general(
            rotated_ref[s * heads + head], keys.astype(jnp.bfloat16), (((1,), (1,)), ((), ())),
            preferred_element_type=jnp.float32,
        )

    def key_rows(first, last):
        for row in range(first, last):
            for at in range(portions):
                if row + 1 < rows:
                    gather(row + 1, at)
                compare(row, at)

    def weigh(part):
        weights = []
        heads_here = range(2 * parts[part][0], 2 * parts[part][1])
        for head in heads_here:
            fresh_weights = []
            for s in range(steps):
                bound = jnp.broadcast_to(
                    bound_ref[head : head + 1, s * picks * BLOCK_TOKENS : (s + 1) * picks * BLOCK_TOKENS],
                    token_at.shape,
                )
                scores = jnp.where(token_at < bound, score_ref[head * steps + s] * scale, -jnp.inf)
                fresh = fresh_score_ref[head, s * group : (s + 1) * group]
                highest = jnp.maximum(
                    jnp.max(scores, -1, keepdims=True), jnp.max(fresh, -1, keepdims=True)
                )
                power = jnp.exp(scores - highest)
                fresh_power = jnp.exp(fresh - highest)
                inverse = 1.0 / (
                    jnp.sum(power, -1, keepdims=True) + jnp.sum(fresh_power, -1, keepdims=True)
                )
                weights.append(power * inverse)
                fresh_weights.append(fresh_power * inverse)
            fresh_ref[head * both : (head + 1) * both] = jnp.dot(
                jnp.concatenate(fresh_weights, 0).astype(jnp.bfloat16), fresh_value_ref[head],
                preferred_element_type=jnp.float32,
            )
        yield
        grouped = jnp.dot(
            jnp.concatenate(weights, 0).astype(jnp.bfloat16), regroup_ref[...],
            preferred_element_type=jnp.float32,
        )
        for h, head in enumerate(heads_here):
            lines = []
            for s in range(steps):
                line = grouped[(h * steps + s) * group : (h * steps + s + 1) * group]
                for t in range(BLOCK_TOKENS):
                    value = line[:, t // 2 * total : (t // 2 + 1) * total]
                    if t % 2 != s:
                        value = pltpu.roll(value, picks, 1)
                    lines.append(
                        jnp.where(low_half, value, 0.0) if s == 0 else jnp.where(low_half, 0.0, value)
                    )
            table = jnp.where(
                place_ref[head : head + 1] == slot_at,
                jnp.broadcast_to(sign_ref[head : head + 1], (total, total)), 0.0,
            ).astype(jnp.bfloat16)
            routed = lax.dot_general(
                jnp.concatenate(lines, 0).astype(jnp.bfloat16), table, (((1,), (1,)), ((), ())),
                preferred_element_type=jnp.float32,
            )
            for s in range(steps):
                for t in range(BLOCK_TOKENS):
                    at = (s * BLOCK_TOKENS + t) * group
                    routed_ref[t, head, s * group : (s + 1) * group] = routed[at : at + group]

    lane = lax.broadcasted_iota(jnp.int32, (both, total), 1) // share

    def wire_copy(part, j):
        target = peer(j)
        first, last = parts[part]
        return remote(
            wire_ref.at[target, pl.ds(first, last - first)],
            got_ref.at[j, pl.ds(first, last - first)],
            wire_send.at[part], wire_recv.at[part * 4 + j // depth], target,
        )

    def wires_in(part, quarter):
        first, last = parts[part]
        span = (pl.ds(max(1, quarter * depth), min(depth, quarter * depth + depth - 1)),
                pl.ds(first, last - first))
        return remote(
            wire_ref.at[span], got_ref.at[span],
            wire_send.at[part], wire_recv.at[part * 4 + quarter], peer(1),
        )

    def wires_out(part):
        first, last = parts[part]
        span = (pl.ds(1, holders - 1), pl.ds(first, last - first))
        return remote(
            wire_ref.at[span], got_ref.at[span],
            wire_send.at[part], wire_recv.at[part * 4], peer(1),
        )

    loads[4].wait()
    for at in range(portions):
        gather(0, at)
    def cross(first, last):
        for unit in range(first, last):
            cells = [
                routed_ref[t, 2 * unit + h] for t in range(BLOCK_TOKENS) for h in range(2)
            ]
            step = 1
            while step < holders:
                low_side = lane // step % 2 == 0
                turned = list(cells)
                for at in range(holders):
                    if at // step % 2 == 0:
                        a, b = cells[at], cells[at + step]
                        turned[at] = jnp.where(
                            low_side, a, pltpu.roll(b, step * share, 1)
                        )
                        turned[at + step] = jnp.where(
                            low_side, pltpu.roll(a, total - step * share, 1), b
                        )
                cells = turned
                step *= 2
            for holder in range(holders):
                wire_ref[holder, unit] = cells[holder].astype(jnp.bfloat16)
    others = pl.ds(1, holders - 1)
    all_asks = remote(
        send_ref.at[others], ask_ref.at[others], ask_send.at[0], ask_recv.at[0], peer(1)
    )
    row_copy = pltpu.make_async_copy(asked_ref, row_ref, row_sem.at[0])
    key_rows(0, 2 * parts[0][1] * steps)
    for part, (first, last) in enumerate(parts):
        later = [
            (row, row + 1) for row in range(2 * last * steps, 2 * (last + 1) * steps) if row < rows
        ]
        for _ in weigh(part):
            if later:
                key_rows(*later.pop(0))
        if later:
            key_rows(*later.pop(0))
        cross(first, last)
        if later:
            key_rows(*later.pop(0))
        for j in far_first:
            wire_copy(part, j).start()
        if part == 1:
            all_asks.wait_recv()
            asked_ref[...] = jnp.clip(ask_ref[...], 0, pool_ref.shape[0] - 1)
            row_copy.start()
        for span_rows in later:
            key_rows(*span_rows)

    loads[5].wait()
    row_copy.wait()
    pltpu.make_async_copy(pool_ref, pool_ref, pool_sem.at[0]).wait()

    early = lax.broadcasted_iota(jnp.int32, (both, HEAD_SIZE), 0) < group

    def partials(pieces):
        arrived = [got_ref[j, unit] if j else wire_ref[me, unit] for unit, j in pieces]
        weight = jnp.maximum(
            jnp.dot(
                jnp.concatenate(arrived, 0), spread_ref[...], preferred_element_type=jnp.float32
            ),
            0.0,
        )
        return [
            partial(unit, j, weight[at * both : (at + 1) * both])
            for at, (unit, j) in enumerate(pieces)
        ]

    def partial(unit, j, weight):
        lhs, columns = [], []
        for h in range(2):
            own = weight[:, h * HEAD_SIZE : (h + 1) * HEAD_SIZE]
            lhs.append(
                jnp.concatenate(
                    [jnp.where(early, own, 0.0), jnp.where(early, 0.0, own)], 1
                ).astype(jnp.bfloat16)
            )
            columns.append(
                jnp.concatenate(
                    [
                        pool_ref[row_ref[j, 0, (s * heads + 2 * unit + h) * share + n]]
                        for s in range(steps)
                        for n in range(share)
                    ],
                    0,
                )
            )
        product = jnp.dot(
            jnp.concatenate(lhs, 0), jnp.concatenate(columns, 1),
            preferred_element_type=jnp.float32,
        )
        return jnp.concatenate([product[:both, :HEAD_SIZE], product[both:, HEAD_SIZE:]], 0)

    own_core = peer(2 * depth)

    def span(part):
        first, last = parts[part]
        return pl.ds(first * 2 * both, (last - first) * 2 * both)

    def core_copy(part, across):
        at = part * 2 + across
        return remote(
            core_out.at[across, :, span(part)], core_in.at[across, :, span(part)],
            core_send.at[at], core_recv.at[at], own_core,
        )

    def values_of(part, js):
        units_here = range(*parts[part])
        found = partials([(unit, j) for j in js for unit in units_here])
        count = len(units_here)
        return [
            jnp.concatenate(found[at * count : (at + 1) * count], 0) for at in range(len(js))
        ]

    def far_stage(part, across):
        first = 2 * depth + across * depth
        wires_in(part, 2 + across).wait_recv()
        values = values_of(part, range(first, first + depth))
        for ahead, value in enumerate(values):
            core_out[across, ahead, span(part)] = value
        core_copy(part, across).start()

    def direct_copy(part, slot):
        across, ahead = slot // depth, slot % depth
        return remote(
            last_out.at[slot, span(part)], last_in.at[slot, span(part)],
            last_send.at[part], last_recv.at[part],
            lax.rem(layer - ahead + depth, depth) * 4
            + (1 - side if across else side) * 2 + core,
        )

    def all_direct(part):
        every = (pl.ds(1, 2 * depth - 1), span(part))
        return remote(
            last_out.at[every], last_in.at[every], last_send.at[part], last_recv.at[part], peer(1)
        )

    def near_stage(part):
        wires_in(part, 1).wait_recv()
        wires_in(part, 0).wait_recv()
        values = values_of(part, range(1, 2 * depth))
        core_copy(part, 1).wait_recv()
        core_copy(part, 0).wait_recv()
        for slot in range(1, 2 * depth):
            last_out[slot, span(part)] = (
                values[slot - 1] + core_in[slot // depth, slot % depth, span(part)]
            ).astype(jnp.bfloat16)
        for slot in reversed(range(1, 2 * depth)):
            direct_copy(part, slot).start()

    def finish(part):
        all_direct(part).wait_recv()
        value = keep_ref[span(part)]
        for slot in range(1, 2 * depth):
            value = value + last_in[slot, span(part)].astype(jnp.float32)
        keep_ref[span(part)] = value
        for head in range(2 * parts[part][0], 2 * parts[part][1]):
            for g in range(group):
                at = (head * group + g) * HEAD_SIZE
                out_ref[:, at : at + HEAD_SIZE] = jnp.concatenate(
                    [
                        keep_ref[head * both + s * group + g : head * both + s * group + g + 1]
                        for s in range(steps)
                    ],
                    0,
                )

    for part in range(len(parts)):
        far_stage(part, 1)
        far_stage(part, 0)
        near_stage(part)
    own = partials([(unit, 0) for unit in range(units)])
    keep_ref[...] = jnp.concatenate(own, 0) + fresh_ref[...] + core_in[0, 0]
    all_asks.wait_send()
    for part in range(len(parts)):
        wires_out(part).wait_send()
        core_copy(part, 0).wait_send()
        core_copy(part, 1).wait_send()
    for part in range(len(parts)):
        finish(part)
    for part in range(len(parts)):
        all_direct(part).wait_send()


def fused_device(
    queries, new_keys, incoming_values, key_left, right_key_factor, value_tile_store, slot_map,
    chosen, lengths,
):
    holders = lax.axis_size("store")
    steps, _, heads, picks = chosen.shape
    blocks = slot_map.shape[2]
    share = max(1, blocks // holders // 4)
    pool_here = value_tile_store.shape[0]
    group = queries.shape[2] // HEAD_SIZE // heads
    rank = key_left.shape[2]
    slots = steps * heads * share
    rows = steps * heads * group
    both = steps * group
    units = heads // 2
    depth = holders // 4
    half = HEAD_SIZE // 2
    tokens = blocks * BLOCK_TOKENS

    turns = np.arange(tokens)[:, None] * ROPE_BASE ** (-(np.arange(half) * 2.0 / HEAD_SIZE))[None]
    cosine, sine = np.cos(turns), np.sin(turns)
    table = np.concatenate([cosine, cosine, -sine, sine], 1).astype(np.float32)
    ahead = jnp.asarray(table[1 : steps + 1].reshape(2 * steps, HEAD_SIZE))
    table = jnp.asarray(table.reshape(blocks, BLOCK_TOKENS, 2 * HEAD_SIZE))
    expand = np.repeat(np.eye(steps * picks, dtype=np.float32), BLOCK_TOKENS, 1)
    deep = -(-rank // 128) * 128
    wide = BLOCK_TOKENS * 64
    regroup = np.zeros((wide, wide), np.float32)
    for t in range(BLOCK_TOKENS):
        regroup[np.arange(64) * BLOCK_TOKENS + t, t * 64 + np.arange(64)] = 1.0
    spread = np.zeros((BLOCK_TOKENS, 2, share, 2, share, BLOCK_TOKENS, 2), np.float32)
    for t in range(BLOCK_TOKENS):
        for h in range(2):
            for n in range(share):
                spread[t, h, n, h, n, t] = (1.0, -1.0)
    lines = BLOCK_TOKENS * 2 * share
    spread = spread.reshape(lines, 2 * lines)

    vmem = pl.BlockSpec(memory_space=pltpu.VMEM)
    anywhere = pl.BlockSpec(memory_space=pl.ANY)
    bf16, f32 = jnp.bfloat16, jnp.float32
    dma = pltpu.SemaphoreType.DMA
    attended = pl.pallas_call(
        functools.partial(fused_kernel, share, pool_here),
        in_specs=[pl.BlockSpec(memory_space=pltpu.SMEM)] * 2 + [vmem] * 6 + [anywhere] * 7,
        out_specs=vmem,
        out_shape=pltpu.VMEM((steps, heads * group * HEAD_SIZE), f32),
        scratch_shapes=[
            pltpu.VMEM((rank, tokens), bf16),
            pltpu.VMEM((rank, heads * HEAD_SIZE), bf16),
            pltpu.VMEM((steps * picks, steps * picks * BLOCK_TOKENS), bf16),
            pltpu.VMEM((lines, 2 * lines), bf16),
            pltpu.VMEM((wide, wide), bf16),
            pltpu.VMEM((pool_here // 2, 2 * BLOCK_TOKENS, HEAD_SIZE), bf16),
            pltpu.VMEM((blocks, BLOCK_TOKENS, deep + 2 * HEAD_SIZE), f32),
            pltpu.VMEM((holders, 1, slots), jnp.int32),
            pltpu.VMEM((holders, 1, slots), jnp.int32),
            pltpu.VMEM((holders, 1, slots), jnp.int32),
            pltpu.SMEM((holders, 1, slots), jnp.int32),
            pltpu.VMEM((heads, steps * picks), jnp.int32),
            pltpu.VMEM((heads, steps * picks), f32),
            pltpu.VMEM((heads, steps * picks * BLOCK_TOKENS), f32),
            pltpu.VMEM((steps * heads, group, HEAD_SIZE), bf16),
            pltpu.VMEM((heads, both, 8), f32),
            pltpu.VMEM((heads, 8, HEAD_SIZE), bf16),
            pltpu.VMEM((heads, rank, 2 * HEAD_SIZE), bf16),
            pltpu.VMEM((picks * BLOCK_TOKENS, 2 * HEAD_SIZE), f32),
            pltpu.VMEM((picks * BLOCK_TOKENS, 2 * HEAD_SIZE), f32),
            pltpu.VMEM((picks * BLOCK_TOKENS, 2 * HEAD_SIZE), f32),
            pltpu.VMEM((picks * BLOCK_TOKENS, 2 * HEAD_SIZE), f32),
            pltpu.VMEM((heads * steps, group, picks * BLOCK_TOKENS), f32),
            pltpu.VMEM((rows, HEAD_SIZE), f32),
            pltpu.VMEM((BLOCK_TOKENS, heads, both, holders * share), f32),
            pltpu.VMEM((holders, units, both, lines), bf16),
            pltpu.VMEM((holders, units, both, lines), bf16),
            pltpu.VMEM((2, depth, rows, HEAD_SIZE), f32),
            pltpu.VMEM((2, depth, rows, HEAD_SIZE), f32),
            pltpu.VMEM((2 * depth, rows, HEAD_SIZE), bf16),
            pltpu.VMEM((2 * depth, rows, HEAD_SIZE), bf16),
            pltpu.VMEM((rows, HEAD_SIZE), f32),
            dma((6,)), dma((1,)), dma((1,)), dma((1,)), dma((1,)), dma((3,)), dma((12,)),
            dma((6,)), dma((6,)), dma((3,)), dma((3,)),
        ],
        compiler_params=pltpu.CompilerParams(collective_id=0, has_side_effects=True),
        name="fused",
    )(
        lengths, chosen[:, 0].reshape(steps * heads, picks), ahead,
        queries[:, 0], new_keys[:, 0], incoming_values[:, 0],
        chosen[:, 0].reshape(steps * heads, picks), slot_map[0],
        right_key_factor[0], table, jnp.asarray(expand, bf16), jnp.asarray(spread, bf16),
        jnp.asarray(regroup, bf16), key_left[0].T,
        value_tile_store.reshape(pool_here // 8, 8, -1),
    )
    return attended.astype(bf16).reshape(steps, 1, -1)


def solution(mesh):
    in_specs = (
        P(None, ("groups", "store"), None),
        P(None, ("groups", "store"), None),
        P(None, ("groups", "store"), None),
        P(("groups", "store"), None, None),
        P(("groups", "store"), None, None),
        P(("groups", "store"), None),
        P(("groups", "store"), None, None),
        P(None, ("groups", "store"), None, None),
        P(("groups", "store")),
    )
    out_specs = P(None, ("groups", "store"), None)

    def body(*args):
        holders = mesh.shape["store"]
        blocks = args[6].shape[2]
        share = max(1, blocks // holders // 4)
        square = args[7].shape[0] * args[7].shape[2] == holders
        packed = args[7].shape[0] * args[7].shape[3] == holders * share
        fits = square and packed and share == 8 and holders == 16 and blocks % 128 == 0
        return (fused_device if fits else per_device)(*args)

    return jax.shard_map(
        body, mesh=mesh, in_specs=in_specs, out_specs=out_specs, check_vma=False
    )
```

```python
import functools

import jax
import jax.numpy as jnp
import numpy as np
from jax import lax
from jax.experimental import pallas as pl
from jax.experimental.pallas import tpu as pltpu
from jax.sharding import PartitionSpec as P

KEY_VALUE_HEADS = 8
HEAD_SIZE = 128
BLOCK_TOKENS = 8


ROPE_BASE = 500000.0


def apply_rotary(tensor, token_positions):
    half_dim = tensor.shape[-1] // 2
    inverse = ROPE_BASE ** (-(jnp.arange(half_dim, dtype=jnp.float32) * 2.0 / tensor.shape[-1]))
    angles = jnp.asarray(token_positions).astype(jnp.float32)[..., None] * inverse
    cosine = jnp.cos(angles)
    sine_vals = jnp.sin(angles)
    first_half = tensor[..., :half_dim]
    second_half = tensor[..., half_dim:]
    return jnp.concatenate(
        [
            first_half * cosine - second_half * sine_vals,
            second_half * cosine + first_half * sine_vals,
        ],
        -1,
    )


def fetch_tiles(requests, value_tile_store):
    tile_row_index = jnp.take(
        value_tile_store,
        lax.all_to_all(requests, "store", split_axis=0, concat_axis=0, tiled=True),
        axis=0,
    )
    return lax.all_to_all(tile_row_index, "store", split_axis=0, concat_axis=0, tiled=True)


def build_requests(flat_idx, inside, total):
    buffer = jnp.zeros((total,), jnp.int32)
    return buffer.at[flat_idx.reshape(-1)].set(inside.reshape(-1))


def attend_row(
    query_full,
    incoming_keys_full,
    incoming_values_full,
    left_rows,
    right_factor_rows,
    block_numbers,
    tile_row_index,
    length,
    step_index,
):
    query_group_size = query_full.shape[-1] // HEAD_SIZE // KEY_VALUE_HEADS
    every_head = query_group_size * KEY_VALUE_HEADS
    selected_count = block_numbers.shape[1]
    score_scale = HEAD_SIZE ** (-0.5)
    right_factor_heads = right_factor_rows.reshape(
        right_factor_rows.shape[0], KEY_VALUE_HEADS, HEAD_SIZE
    )
    token_positions = (
        block_numbers[:, :, None] * BLOCK_TOKENS + jnp.arange(BLOCK_TOKENS, dtype=jnp.int32)
    ).reshape(KEY_VALUE_HEADS, selected_count * BLOCK_TOKENS)
    picked = left_rows[token_positions]
    raw_keys = jnp.einsum(
        "htr,rhd->htd", picked, right_factor_heads, preferred_element_type=jnp.float32
    )
    cache_keys = apply_rotary(raw_keys, token_positions).astype(jnp.bfloat16)
    rotated_query = apply_rotary(
        query_full[step_index].reshape(every_head, HEAD_SIZE).astype(jnp.float32),
        length + step_index,
    ).astype(jnp.bfloat16)
    current_position = (length + jnp.arange(step_index + 1, dtype=jnp.int32))[:, None]
    current_keys = apply_rotary(
        incoming_keys_full[: step_index + 1]
        .reshape(step_index + 1, KEY_VALUE_HEADS, HEAD_SIZE)
        .astype(jnp.float32),
        current_position,
    ).astype(jnp.bfloat16)
    current_keys = jnp.transpose(current_keys, (1, 0, 2))
    current_values = jnp.transpose(
        incoming_values_full[: step_index + 1].reshape(step_index + 1, KEY_VALUE_HEADS, HEAD_SIZE),
        (1, 0, 2),
    )
    local_values = tile_row_index.reshape(KEY_VALUE_HEADS, selected_count * BLOCK_TOKENS, HEAD_SIZE)
    grouped_queries = rotated_query.reshape(KEY_VALUE_HEADS, query_group_size, HEAD_SIZE)
    cache_scores = (
        jnp.einsum("hgd,htd->hgt", grouped_queries, cache_keys, preferred_element_type=jnp.float32)
        * score_scale
    )
    inside_len = token_positions < length
    cache_scores = jnp.where(inside_len[:, None, :], cache_scores, -jnp.inf)
    fresh_scores = (
        jnp.einsum(
            "hgd,hnd->hgn", grouped_queries, current_keys, preferred_element_type=jnp.float32
        )
        * score_scale
    )
    highest = jnp.maximum(
        jnp.max(cache_scores, -1, keepdims=True), jnp.max(fresh_scores, -1, keepdims=True)
    )
    cache_exp = jnp.exp(cache_scores - highest)
    fresh_exp = jnp.exp(fresh_scores - highest)
    denominator = jnp.sum(cache_exp, -1, keepdims=True) + jnp.sum(fresh_exp, -1, keepdims=True)
    cache_weight = (cache_exp / denominator).astype(jnp.bfloat16)
    fresh_weight = (fresh_exp / denominator).astype(jnp.bfloat16)
    attended = jnp.einsum(
        "hgt,htd->hgd", cache_weight, local_values, preferred_element_type=jnp.float32
    )
    attended = attended + jnp.einsum(
        "hgn,hnd->hgd", fresh_weight, current_values, preferred_element_type=jnp.float32
    )
    return attended.reshape(every_head * HEAD_SIZE).astype(jnp.bfloat16)


def per_device(
    queries,
    new_keys,
    incoming_values,
    key_left,
    right_key_factor,
    value_tile_store,
    slot_map,
    chosen,
    lengths,
):
    nstore = lax.axis_size("store")
    local_rows = key_left.shape[0]
    nchunk = slot_map.shape[2]
    step_count = chosen.shape[0]
    selected_count = chosen.shape[3]
    keeper_share = max(1, nchunk // nstore // 4)
    tile_limit = local_rows * KEY_VALUE_HEADS * keeper_share
    pool_here = value_tile_store.shape[0]
    slot_numbers = jnp.take_along_axis(
        jnp.broadcast_to(slot_map[None], (step_count,) + slot_map.shape), chosen, axis=3
    )
    tile_keeper = slot_numbers // pool_here
    inside = slot_numbers % pool_here
    matched = tile_keeper[..., :, None] == tile_keeper[..., None, :]
    earlier = jnp.arange(selected_count)[None, :] < jnp.arange(selected_count)[:, None]
    order_in = jnp.sum(jnp.logical_and(matched, earlier), -1)
    row_head = (
        jnp.arange(local_rows, dtype=jnp.int32)[:, None, None] * KEY_VALUE_HEADS
        + jnp.arange(KEY_VALUE_HEADS, dtype=jnp.int32)[None, :, None]
    )
    position = row_head * keeper_share + order_in
    tiles_all = []
    slot_span = step_count * tile_limit
    flat_idx = (
        tile_keeper * slot_span
        + jnp.arange(step_count, dtype=jnp.int32)[:, None, None, None] * tile_limit
        + position
    )
    requests = build_requests(flat_idx, inside, nstore * slot_span).reshape(nstore, slot_span)
    received = fetch_tiles(requests, value_tile_store).reshape(nstore * slot_span, -1)
    for step_index in range(step_count):
        tiles_all.append(received[flat_idx[step_index]])
    results = []
    for step_index in range(step_count):
        per_rows = [
            attend_row(
                queries[:, 0],
                new_keys[:, 0],
                incoming_values[:, 0],
                key_left[0],
                right_key_factor[0],
                chosen[step_index, 0],
                tiles_all[step_index][0],
                lengths[0],
                step_index,
            )
        ]
        results.append(jnp.stack(per_rows))
    return jnp.stack(results)


def fused_kernel(
    share, pool_here,
    length_ref, pick_ref, ahead_ref, query_ref, new_key_ref, new_value_ref,
    chosen_ref, slot_ref, right_hbm, table_hbm, expand_hbm, spread_hbm, regroup_hbm, left_hbm,
    pool_hbm,
    out_ref,
    left_ref, right_ref, expand_ref, spread_ref, regroup_ref, pool_ref, block_ref,
    send_ref, ask_ref, asked_ref, row_ref, place_ref, sign_ref, bound_ref,
    rotated_ref, fresh_score_ref, fresh_value_ref, factor_ref, raw_even, raw_odd, turn_even, turn_odd, score_ref, fresh_ref,
    routed_ref, wire_ref, got_ref,
    core_out, core_in, last_out, last_in, keep_ref,
    in_sem, pool_sem, row_sem, ask_send, ask_recv, wire_send, wire_recv,
    core_send, core_recv, last_send, last_recv,
):
    me = lax.axis_index("store")
    raw_refs, turn_refs = (raw_even, raw_odd), (turn_even, turn_odd)
    holders = send_ref.shape[0]
    depth = holders // 4
    rows, picks = chosen_ref.shape
    heads, blocks = slot_ref.shape
    steps = rows // heads
    rank = left_hbm.shape[0]
    deep = block_ref.shape[2] - 2 * HEAD_SIZE
    group = query_ref.shape[1] // HEAD_SIZE // heads
    both = steps * group
    half = HEAD_SIZE // 2
    units = heads // 2
    parts = ((0, units - 2), (units - 2, units))
    scale = HEAD_SIZE ** (-0.5)
    core, side, layer = lax.rem(me, 2), lax.rem(me // 2, 2), me // 4

    def peer(j):
        far, across, ahead = j // (2 * depth), j // depth % 2, j % depth
        return (
            lax.rem(layer + ahead, depth) * 4
            + (1 - side if across else side) * 2
            + (1 - core if far else core)
        )

    def remote(src, dst, send, recv, target):
        return pltpu.make_async_remote_copy(
            src_ref=src, dst_ref=dst, send_sem=send, recv_sem=recv,
            device_id={"store": target}, device_id_type=pl.DeviceIdType.MESH,
        )

    barrier = pltpu.get_barrier_semaphore()

    def greet(k, _):
        pl.semaphore_signal(
            barrier, inc=1, device_id={"store": lax.rem(me + k, holders)},
            device_id_type=pl.DeviceIdType.MESH,
        )
        return 0

    loads = [
        pltpu.make_async_copy(src, dst, in_sem.at[at])
        for at, (src, dst) in enumerate(
            (
                (left_hbm, left_ref),
                (right_hbm, right_ref),
                (table_hbm, block_ref.at[:, :, pl.ds(deep, 2 * HEAD_SIZE)]),
                (expand_hbm, expand_ref),
                (regroup_hbm, regroup_ref),
                (spread_hbm, spread_ref),
            )
        )
    ]
    for copy in loads:
        copy.start()
    lax.fori_loop(1, holders, greet, 0)

    octets = pool_here // 8
    pool_copies = [
        pltpu.make_async_copy(
            pool_hbm.at[:, pl.ds(2 * q, 2), pl.ds(HEAD_SIZE * t, HEAD_SIZE)],
            pool_ref.at[pl.ds(q * octets, octets), pl.ds(2 * t, 2), :],
            pool_sem.at[0],
        )
        for q in range(4)
        for t in range(BLOCK_TOKENS)
    ]

    total = holders * share
    length = length_ref[0]
    lane_at = lax.broadcasted_iota(jnp.int32, (heads, total), 1)
    first_step = lane_at < picks
    chosen = jnp.concatenate([chosen_ref[s * heads : (s + 1) * heads] for s in range(steps)], 1)
    slot = jnp.zeros((heads, total), jnp.int32)
    for at in range(0, blocks, total):
        found = jnp.take_along_axis(slot_ref[:, at : at + total], chosen & (total - 1), axis=1)
        slot = jnp.where(chosen // total == at // total, found, slot)
    if pool_here & (pool_here - 1) == 0:
        keeper = slot >> (pool_here.bit_length() - 1)
        inside = slot & (pool_here - 1)
    else:
        keeper = lax.div(slot, jnp.full_like(slot, pool_here))
        inside = slot - keeper * pool_here
    sign_ref[...] = (1 - 2 * (inside & 1)).astype(jnp.float32)
    inside = ((inside >> 1) & 3) * octets + (inside >> 3)
    before_row = lax.broadcasted_iota(jnp.int32, (total, total), 0)
    before_lane = lax.broadcasted_iota(jnp.int32, (total, total), 1)
    before = jnp.where(
        jnp.logical_and(before_row < before_lane, before_row // picks == before_lane // picks),
        1.0, 0.0,
    ).astype(jnp.bfloat16)
    mine = [jnp.where(keeper == holder, 1.0, 0.0) for holder in range(holders)]
    counts = jnp.dot(
        jnp.concatenate(mine, 0).astype(jnp.bfloat16), before, preferred_element_type=jnp.float32
    )
    order = jnp.zeros((heads, total), jnp.float32)
    for holder in range(holders):
        order = order + mine[holder] * counts[holder * heads : (holder + 1) * heads]
    place = keeper * share + order.astype(jnp.int32)
    place_ref[...] = place
    digits = []
    for s in range(steps):
        for shift in (0, 8, 16):
            digit = ((inside >> shift) & 255).astype(jnp.float32)
            digits.append(jnp.where(first_step == (s == 0), digit, 0.0))
    slot_at = before_row
    moved = [None] * rows
    for head in range(heads):
        lines = jnp.concatenate(
            [digit[head : head + 1] for digit in digits]
            + [jnp.zeros((8 - len(digits), total), jnp.float32)], 0
        ).astype(jnp.bfloat16)
        table = jnp.where(place[head : head + 1] == slot_at, 1.0, 0.0).astype(jnp.bfloat16)
        found = lax.dot_general(
            lines, table, (((1,), (1,)), ((), ())), preferred_element_type=jnp.float32
        ).astype(jnp.int32)
        for s in range(steps):
            row = s * heads + head
            whole = found[3 * s : 3 * s + 1] + found[3 * s + 1 : 3 * s + 2] * 256
            whole = whole + found[3 * s + 2 : 3 * s + 3] * 65536
            moved[row] = pltpu.roll(whole, row * share, 1) if row else whole
    moved = jnp.concatenate(moved, 0)
    own_lanes = (
        lax.broadcasted_iota(jnp.int32, (rows, total), 1) // share
        == lax.broadcasted_iota(jnp.int32, (rows, total), 0)
    )
    for holder in range(holders):
        turned = pltpu.roll(moved, total - holder * share, 1) if holder else moved
        send_ref[holder] = jnp.sum(jnp.where(own_lanes, turned, 0), 0, keepdims=True)

    def ask_copy(j):
        target = peer(j)
        return remote(
            send_ref.at[target], ask_ref.at[j], ask_send.at[0], ask_recv.at[0], target
        )

    turn_of = (3, 2, 1, 0)
    far_first = sorted(
        range(1, holders),
        key=lambda j: (turn_of[j // depth], -min(j % depth, depth - j % depth)),
    )
    pl.semaphore_wait(barrier, holders - 1)
    for j in far_first:
        ask_copy(j).start()
    ask_ref[0] = send_ref[me]

    loads[1].wait()
    for head in range(heads):
        factor = right_ref[:, head * HEAD_SIZE : (head + 1) * HEAD_SIZE]
        factor_ref[head, :, :HEAD_SIZE] = factor
        factor_ref[head, :, HEAD_SIZE:] = pltpu.roll(
            factor.astype(jnp.float32), half, 1
        ).astype(jnp.bfloat16)
    loads[3].wait()
    remaining = jnp.clip(length - chosen * BLOCK_TOKENS, 0, BLOCK_TOKENS)
    bound_ref[...] = jnp.dot(
        remaining.astype(jnp.float32).astype(jnp.bfloat16), expand_ref[...],
        preferred_element_type=jnp.float32,
    )
    same = jnp.where(before_row == before_lane, 1.0, 0.0).astype(jnp.bfloat16)
    loads[0].wait()
    turned_blocks = total // BLOCK_TOKENS
    for at in range(0, left_ref.shape[1], total):
        if at // total % 2 == 1:
            turned = left_ref[:, at : at + total].astype(jnp.float32).T
        else:
            turned = lax.dot_general(
                same, left_ref[:, at : at + total], (((1,), (1,)), ((), ())),
                preferred_element_type=jnp.float32,
            )
        first = at // BLOCK_TOKENS
        block_ref[first : first + turned_blocks, :, :rank] = turned.reshape(
            turned_blocks, BLOCK_TOKENS, rank
        )
    loads[2].wait()
    for copy in pool_copies:
        copy.start()

    last = jnp.maximum(length - 1, 0)
    turn = block_ref[last // BLOCK_TOKENS, pl.ds(lax.rem(last, BLOCK_TOKENS), 1), deep:]
    last_cos, last_sin = turn[:, :HEAD_SIZE], turn[:, HEAD_SIZE:]
    spin_cos, spin_sin = [], []
    for s in range(steps):
        more_cos, more_sin = ahead_ref[2 * s : 2 * s + 1], ahead_ref[2 * s + 1 : 2 * s + 2]
        spin_cos.append(
            jnp.broadcast_to(last_cos * more_cos - last_sin * more_sin, (group, HEAD_SIZE))
        )
        spin_sin.append(
            jnp.broadcast_to(last_sin * more_cos + last_cos * more_sin, (group, HEAD_SIZE))
        )
    query_all = query_ref[...].astype(jnp.float32)
    key_all = new_key_ref[...].astype(jnp.float32)
    value_all = new_value_ref[...].astype(jnp.float32)
    fresh_cos = jnp.concatenate([spin_cos[s][:1] for s in range(steps)] + [spin_cos[0][: 8 - steps]], 0)
    fresh_sin = jnp.concatenate([spin_sin[s][:1] for s in range(steps)] + [spin_sin[0][: 8 - steps]], 0)
    both_cos = jnp.concatenate(spin_cos, 0)
    both_sin = jnp.concatenate(spin_sin, 0)
    empty = jnp.zeros((8 - steps, HEAD_SIZE), jnp.float32)
    fresh_keep = (
        lax.broadcasted_iota(jnp.int32, (both, 8), 1)
        <= lax.broadcasted_iota(jnp.int32, (both, 8), 0) // group
    )
    for head in range(heads):
        lanes = slice(head * HEAD_SIZE, (head + 1) * HEAD_SIZE)
        flat = jnp.concatenate(
            [
                query_all[s : s + 1, (head * group + g) * HEAD_SIZE : (head * group + g + 1) * HEAD_SIZE]
                for s in range(steps)
                for g in range(group)
            ],
            0,
        )
        query = (flat * both_cos + pltpu.roll(flat, half, 1) * both_sin).astype(jnp.bfloat16)
        for s in range(steps):
            rotated_ref[s * heads + head] = query[s * group : (s + 1) * group]
        flat = jnp.concatenate([key_all[:, lanes], empty], 0)
        fresh_key = (flat * fresh_cos + pltpu.roll(flat, half, 1) * fresh_sin).astype(jnp.bfloat16)
        fresh = lax.dot_general(
            query, fresh_key, (((1,), (1,)), ((), ())), preferred_element_type=jnp.float32
        ) * scale
        fresh_score_ref[head] = jnp.where(fresh_keep, fresh, -jnp.inf)
        fresh_value_ref[head] = jnp.concatenate([value_all[:, lanes], empty], 0).astype(
            jnp.bfloat16
        )

    token_at = (
        lax.broadcasted_iota(jnp.int32, (group, picks * BLOCK_TOKENS), 1) % BLOCK_TOKENS
    ).astype(jnp.float32)
    low_half = lax.broadcasted_iota(jnp.int32, (group, total), 1) < picks

    portion = 4 * total // BLOCK_TOKENS
    portions = picks // portion

    def gather(row, at):
        head, s = divmod(row, steps)
        found = [
            block_ref[pick_ref[s * heads + head, at * portion + n]] for n in range(portion)
        ]
        span = slice(4 * at * total, 4 * (at + 1) * total)
        raw_refs[row % 2][span] = jnp.dot(
            jnp.concatenate([value[:, :rank] for value in found], 0).astype(jnp.bfloat16),
            factor_ref[head], preferred_element_type=jnp.float32,
        )
        turn_refs[row % 2][span] = jnp.concatenate([value[:, deep:] for value in found], 0)

    def compare(row, at):
        head, s = divmod(row, steps)
        span = slice(4 * at * total, 4 * (at + 1) * total)
        raw = raw_refs[row % 2][span]
        keys = raw * turn_refs[row % 2][span]
        keys = keys[:, :HEAD_SIZE] + keys[:, HEAD_SIZE:]
        score_ref[row, :, span] = lax.dot_general(
            rotated_ref[s * heads + head], keys.astype(jnp.bfloat16), (((1,), (1,)), ((), ())),
            preferred_element_type=jnp.float32,
        )

    def key_rows(first, last):
        for row in range(first, last):
            for at in range(portions):
                if row + 1 < rows:
                    gather(row + 1, at)
                compare(row, at)

    def weigh(part):
        weights = []
        heads_here = range(2 * parts[part][0], 2 * parts[part][1])
        for head in heads_here:
            fresh_weights = []
            for s in range(steps):
                bound = jnp.broadcast_to(
                    bound_ref[head : head + 1, s * picks * BLOCK_TOKENS : (s + 1) * picks * BLOCK_TOKENS],
                    token_at.shape,
                )
                scores = jnp.where(token_at < bound, score_ref[head * steps + s] * scale, -jnp.inf)
                fresh = fresh_score_ref[head, s * group : (s + 1) * group]
                highest = jnp.maximum(
                    jnp.max(scores, -1, keepdims=True), jnp.max(fresh, -1, keepdims=True)
                )
                power = jnp.exp(scores - highest)
                fresh_power = jnp.exp(fresh - highest)
                inverse = 1.0 / (
                    jnp.sum(power, -1, keepdims=True) + jnp.sum(fresh_power, -1, keepdims=True)
                )
                weights.append(power * inverse)
                fresh_weights.append(fresh_power * inverse)
            fresh_ref[head * both : (head + 1) * both] = jnp.dot(
                jnp.concatenate(fresh_weights, 0).astype(jnp.bfloat16), fresh_value_ref[head],
                preferred_element_type=jnp.float32,
            )
        yield
        grouped = jnp.dot(
            jnp.concatenate(weights, 0).astype(jnp.bfloat16), regroup_ref[...],
            preferred_element_type=jnp.float32,
        )
        for h, head in enumerate(heads_here):
            lines = []
            for s in range(steps):
                line = grouped[(h * steps + s) * group : (h * steps + s + 1) * group]
                for t in range(BLOCK_TOKENS):
                    value = line[:, t // 2 * total : (t // 2 + 1) * total]
                    if t % 2 != s:
                        value = pltpu.roll(value, picks, 1)
                    lines.append(
                        jnp.where(low_half, value, 0.0) if s == 0 else jnp.where(low_half, 0.0, value)
                    )
            table = jnp.where(
                place_ref[head : head + 1] == slot_at,
                jnp.broadcast_to(sign_ref[head : head + 1], (total, total)), 0.0,
            ).astype(jnp.bfloat16)
            routed = lax.dot_general(
                jnp.concatenate(lines, 0).astype(jnp.bfloat16), table, (((1,), (1,)), ((), ())),
                preferred_element_type=jnp.float32,
            )
            for s in range(steps):
                for t in range(BLOCK_TOKENS):
                    at = (s * BLOCK_TOKENS + t) * group
                    routed_ref[t, head, s * group : (s + 1) * group] = routed[at : at + group]

    lane = lax.broadcasted_iota(jnp.int32, (both, total), 1) // share

    def wire_copy(part, j):
        target = peer(j)
        first, last = parts[part]
        return remote(
            wire_ref.at[target, pl.ds(first, last - first)],
            got_ref.at[j, pl.ds(first, last - first)],
            wire_send.at[part], wire_recv.at[part * 4 + j // depth], target,
        )

    def wires_in(part, quarter):
        first, last = parts[part]
        span = (pl.ds(max(1, quarter * depth), min(depth, quarter * depth + depth - 1)),
                pl.ds(first, last - first))
        return remote(
            wire_ref.at[span], got_ref.at[span],
            wire_send.at[part], wire_recv.at[part * 4 + quarter], peer(1),
        )

    def wires_out(part):
        first, last = parts[part]
        span = (pl.ds(1, holders - 1), pl.ds(first, last - first))
        return remote(
            wire_ref.at[span], got_ref.at[span],
            wire_send.at[part], wire_recv.at[part * 4], peer(1),
        )

    loads[4].wait()
    for at in range(portions):
        gather(0, at)
    def cross(first, last):
        for unit in range(first, last):
            cells = [
                routed_ref[t, 2 * unit + h] for t in range(BLOCK_TOKENS) for h in range(2)
            ]
            step = 1
            while step < holders:
                low_side = lane // step % 2 == 0
                turned = list(cells)
                for at in range(holders):
                    if at // step % 2 == 0:
                        a, b = cells[at], cells[at + step]
                        turned[at] = jnp.where(
                            low_side, a, pltpu.roll(b, step * share, 1)
                        )
                        turned[at + step] = jnp.where(
                            low_side, pltpu.roll(a, total - step * share, 1), b
                        )
                cells = turned
                step *= 2
            for holder in range(holders):
                wire_ref[holder, unit] = cells[holder].astype(jnp.bfloat16)
    others = pl.ds(1, holders - 1)
    all_asks = remote(
        send_ref.at[others], ask_ref.at[others], ask_send.at[0], ask_recv.at[0], peer(1)
    )
    row_copy = pltpu.make_async_copy(asked_ref, row_ref, row_sem.at[0])
    key_rows(0, 2 * parts[0][1] * steps)
    for part, (first, last) in enumerate(parts):
        later = [
            (row, row + 1)
            for row in range(
                2 * last * steps, 2 * parts[min(part + 1, len(parts) - 1)][1] * steps
            )
        ]
        for _ in weigh(part):
            if later:
                key_rows(*later.pop(0))
        if later:
            key_rows(*later.pop(0))
        cross(first, last)
        for j in far_first:
            wire_copy(part, j).start()
        if part == 0:
            all_asks.wait_recv()
            asked_ref[...] = jnp.clip(ask_ref[...], 0, pool_ref.shape[0] - 1)
            row_copy.start()
        for span_rows in later:
            key_rows(*span_rows)

    loads[5].wait()
    row_copy.wait()
    pltpu.make_async_copy(pool_ref, pool_ref, pool_sem.at[0]).wait()

    early = lax.broadcasted_iota(jnp.int32, (both, HEAD_SIZE), 0) < group

    def partials(pieces):
        arrived = [got_ref[j, unit] if j else wire_ref[me, unit] for unit, j in pieces]
        weight = jnp.maximum(
            jnp.dot(
                jnp.concatenate(arrived, 0), spread_ref[...], preferred_element_type=jnp.float32
            ),
            0.0,
        )
        return [
            partial(unit, j, weight[at * both : (at + 1) * both])
            for at, (unit, j) in enumerate(pieces)
        ]

    def partial(unit, j, weight):
        lhs, columns = [], []
        for h in range(2):
            own = weight[:, h * HEAD_SIZE : (h + 1) * HEAD_SIZE]
            lhs.append(
                jnp.concatenate(
                    [jnp.where(early, own, 0.0), jnp.where(early, 0.0, own)], 1
                ).astype(jnp.bfloat16)
            )
            columns.append(
                jnp.concatenate(
                    [
                        pool_ref[row_ref[j, 0, (s * heads + 2 * unit + h) * share + n]]
                        for s in range(steps)
                        for n in range(share)
                    ],
                    0,
                )
            )
        product = jnp.dot(
            jnp.concatenate(lhs, 0), jnp.concatenate(columns, 1),
            preferred_element_type=jnp.float32,
        )
        return jnp.concatenate([product[:both, :HEAD_SIZE], product[both:, HEAD_SIZE:]], 0)

    own_core = peer(2 * depth)

    def span(part):
        first, last = parts[part]
        return pl.ds(first * 2 * both, (last - first) * 2 * both)

    def core_copy(part, across):
        at = part * 2 + across
        return remote(
            core_out.at[across, :, span(part)], core_in.at[across, :, span(part)],
            core_send.at[at], core_recv.at[at], own_core,
        )

    def values_of(part, js):
        units_here = range(*parts[part])
        found = partials([(unit, j) for j in js for unit in units_here])
        count = len(units_here)
        return [
            jnp.concatenate(found[at * count : (at + 1) * count], 0) for at in range(len(js))
        ]

    def far_stage(part, across):
        first = 2 * depth + across * depth
        wires_in(part, 2 + across).wait_recv()
        values = values_of(part, range(first, first + depth))
        for ahead, value in enumerate(values):
            core_out[across, ahead, span(part)] = value
        core_copy(part, across).start()

    def direct_copy(part, slot):
        across, ahead = slot // depth, slot % depth
        return remote(
            last_out.at[slot, span(part)], last_in.at[slot, span(part)],
            last_send.at[part], last_recv.at[part],
            lax.rem(layer - ahead + depth, depth) * 4
            + (1 - side if across else side) * 2 + core,
        )

    def all_direct(part):
        every = (pl.ds(1, 2 * depth - 1), span(part))
        return remote(
            last_out.at[every], last_in.at[every], last_send.at[part], last_recv.at[part], peer(1)
        )

    def near_stage(part):
        wires_in(part, 1).wait_recv()
        wires_in(part, 0).wait_recv()
        values = values_of(part, range(1, 2 * depth))
        core_copy(part, 1).wait_recv()
        core_copy(part, 0).wait_recv()
        for slot in range(1, 2 * depth):
            last_out[slot, span(part)] = (
                values[slot - 1] + core_in[slot // depth, slot % depth, span(part)]
            ).astype(jnp.bfloat16)
        for slot in reversed(range(1, 2 * depth)):
            direct_copy(part, slot).start()

    def finish(part):
        all_direct(part).wait_recv()
        value = keep_ref[span(part)]
        for slot in range(1, 2 * depth):
            value = value + last_in[slot, span(part)].astype(jnp.float32)
        keep_ref[span(part)] = value
        for head in range(2 * parts[part][0], 2 * parts[part][1]):
            for g in range(group):
                at = (head * group + g) * HEAD_SIZE
                out_ref[:, at : at + HEAD_SIZE] = jnp.concatenate(
                    [
                        keep_ref[head * both + s * group + g : head * both + s * group + g + 1]
                        for s in range(steps)
                    ],
                    0,
                )

    for part in range(len(parts)):
        far_stage(part, 1)
        far_stage(part, 0)
        near_stage(part)
    own = partials([(unit, 0) for unit in range(units)])
    keep_ref[...] = jnp.concatenate(own, 0) + fresh_ref[...] + core_in[0, 0]
    all_asks.wait_send()
    for part in range(len(parts)):
        wires_out(part).wait_send()
        core_copy(part, 0).wait_send()
        core_copy(part, 1).wait_send()
    for part in range(len(parts)):
        finish(part)
    for part in range(len(parts)):
        all_direct(part).wait_send()


def fused_device(
    queries, new_keys, incoming_values, key_left, right_key_factor, value_tile_store, slot_map,
    chosen, lengths,
):
    holders = lax.axis_size("store")
    steps, _, heads, picks = chosen.shape
    blocks = slot_map.shape[2]
    share = max(1, blocks // holders // 4)
    pool_here = value_tile_store.shape[0]
    group = queries.shape[2] // HEAD_SIZE // heads
    rank = key_left.shape[2]
    slots = steps * heads * share
    rows = steps * heads * group
    both = steps * group
    units = heads // 2
    depth = holders // 4
    half = HEAD_SIZE // 2
    tokens = blocks * BLOCK_TOKENS

    turns = np.arange(tokens)[:, None] * ROPE_BASE ** (-(np.arange(half) * 2.0 / HEAD_SIZE))[None]
    cosine, sine = np.cos(turns), np.sin(turns)
    table = np.concatenate([cosine, cosine, -sine, sine], 1).astype(np.float32)
    ahead = jnp.asarray(table[1 : steps + 1].reshape(2 * steps, HEAD_SIZE))
    table = jnp.asarray(table.reshape(blocks, BLOCK_TOKENS, 2 * HEAD_SIZE))
    expand = np.repeat(np.eye(steps * picks, dtype=np.float32), BLOCK_TOKENS, 1)
    deep = -(-rank // 128) * 128
    wide = BLOCK_TOKENS * 64
    regroup = np.zeros((wide, wide), np.float32)
    for t in range(BLOCK_TOKENS):
        regroup[np.arange(64) * BLOCK_TOKENS + t, t * 64 + np.arange(64)] = 1.0
    spread = np.zeros((BLOCK_TOKENS, 2, share, 2, share, BLOCK_TOKENS, 2), np.float32)
    for t in range(BLOCK_TOKENS):
        for h in range(2):
            for n in range(share):
                spread[t, h, n, h, n, t] = (1.0, -1.0)
    lines = BLOCK_TOKENS * 2 * share
    spread = spread.reshape(lines, 2 * lines)

    vmem = pl.BlockSpec(memory_space=pltpu.VMEM)
    anywhere = pl.BlockSpec(memory_space=pl.ANY)
    bf16, f32 = jnp.bfloat16, jnp.float32
    dma = pltpu.SemaphoreType.DMA
    attended = pl.pallas_call(
        functools.partial(fused_kernel, share, pool_here),
        in_specs=[pl.BlockSpec(memory_space=pltpu.SMEM)] * 2 + [vmem] * 6 + [anywhere] * 7,
        out_specs=vmem,
        out_shape=pltpu.VMEM((steps, heads * group * HEAD_SIZE), f32),
        scratch_shapes=[
            pltpu.VMEM((rank, tokens), bf16),
            pltpu.VMEM((rank, heads * HEAD_SIZE), bf16),
            pltpu.VMEM((steps * picks, steps * picks * BLOCK_TOKENS), bf16),
            pltpu.VMEM((lines, 2 * lines), bf16),
            pltpu.VMEM((wide, wide), bf16),
            pltpu.VMEM((pool_here // 2, 2 * BLOCK_TOKENS, HEAD_SIZE), bf16),
            pltpu.VMEM((blocks, BLOCK_TOKENS, deep + 2 * HEAD_SIZE), f32),
            pltpu.VMEM((holders, 1, slots), jnp.int32),
            pltpu.VMEM((holders, 1, slots), jnp.int32),
            pltpu.VMEM((holders, 1, slots), jnp.int32),
            pltpu.SMEM((holders, 1, slots), jnp.int32),
            pltpu.VMEM((heads, steps * picks), jnp.int32),
            pltpu.VMEM((heads, steps * picks), f32),
            pltpu.VMEM((heads, steps * picks * BLOCK_TOKENS), f32),
            pltpu.VMEM((steps * heads, group, HEAD_SIZE), bf16),
            pltpu.VMEM((heads, both, 8), f32),
            pltpu.VMEM((heads, 8, HEAD_SIZE), bf16),
            pltpu.VMEM((heads, rank, 2 * HEAD_SIZE), bf16),
            pltpu.VMEM((picks * BLOCK_TOKENS, 2 * HEAD_SIZE), f32),
            pltpu.VMEM((picks * BLOCK_TOKENS, 2 * HEAD_SIZE), f32),
            pltpu.VMEM((picks * BLOCK_TOKENS, 2 * HEAD_SIZE), f32),
            pltpu.VMEM((picks * BLOCK_TOKENS, 2 * HEAD_SIZE), f32),
            pltpu.VMEM((heads * steps, group, picks * BLOCK_TOKENS), f32),
            pltpu.VMEM((rows, HEAD_SIZE), f32),
            pltpu.VMEM((BLOCK_TOKENS, heads, both, holders * share), f32),
            pltpu.VMEM((holders, units, both, lines), bf16),
            pltpu.VMEM((holders, units, both, lines), bf16),
            pltpu.VMEM((2, depth, rows, HEAD_SIZE), f32),
            pltpu.VMEM((2, depth, rows, HEAD_SIZE), f32),
            pltpu.VMEM((2 * depth, rows, HEAD_SIZE), bf16),
            pltpu.VMEM((2 * depth, rows, HEAD_SIZE), bf16),
            pltpu.VMEM((rows, HEAD_SIZE), f32),
            dma((6,)), dma((1,)), dma((1,)), dma((1,)), dma((1,)), dma((3,)), dma((12,)),
            dma((6,)), dma((6,)), dma((3,)), dma((3,)),
        ],
        compiler_params=pltpu.CompilerParams(collective_id=0, has_side_effects=True),
        name="fused",
    )(
        lengths, chosen[:, 0].reshape(steps * heads, picks), ahead,
        queries[:, 0], new_keys[:, 0], incoming_values[:, 0],
        chosen[:, 0].reshape(steps * heads, picks), slot_map[0],
        right_key_factor[0], table, jnp.asarray(expand, bf16), jnp.asarray(spread, bf16),
        jnp.asarray(regroup, bf16), key_left[0].T,
        value_tile_store.reshape(pool_here // 8, 8, -1),
    )
    return attended.astype(bf16).reshape(steps, 1, -1)


def solution(mesh):
    in_specs = (
        P(None, ("groups", "store"), None),
        P(None, ("groups", "store"), None),
        P(None, ("groups", "store"), None),
        P(("groups", "store"), None, None),
        P(("groups", "store"), None, None),
        P(("groups", "store"), None),
        P(("groups", "store"), None, None),
        P(None, ("groups", "store"), None, None),
        P(("groups", "store")),
    )
    out_specs = P(None, ("groups", "store"), None)

    def body(*args):
        holders = mesh.shape["store"]
        blocks = args[6].shape[2]
        share = max(1, blocks // holders // 4)
        square = args[7].shape[0] * args[7].shape[2] == holders
        packed = args[7].shape[0] * args[7].shape[3] == holders * share
        fits = square and packed and share == 8 and holders == 16 and blocks % 128 == 0
        return (fused_device if fits else per_device)(*args)

    return jax.shard_map(
        body, mesh=mesh, in_specs=in_specs, out_specs=out_specs, check_vma=False
    )
```

```python
import functools

import jax
import jax.numpy as jnp
import numpy as np
from jax import lax
from jax.experimental import pallas as pl
from jax.experimental.pallas import tpu as pltpu
from jax.sharding import PartitionSpec as P

KEY_VALUE_HEADS = 8
HEAD_SIZE = 128
BLOCK_TOKENS = 8


ROPE_BASE = 500000.0


def apply_rotary(tensor, token_positions):
    half_dim = tensor.shape[-1] // 2
    inverse = ROPE_BASE ** (-(jnp.arange(half_dim, dtype=jnp.float32) * 2.0 / tensor.shape[-1]))
    angles = jnp.asarray(token_positions).astype(jnp.float32)[..., None] * inverse
    cosine = jnp.cos(angles)
    sine_vals = jnp.sin(angles)
    first_half = tensor[..., :half_dim]
    second_half = tensor[..., half_dim:]
    return jnp.concatenate(
        [
            first_half * cosine - second_half * sine_vals,
            second_half * cosine + first_half * sine_vals,
        ],
        -1,
    )


def fetch_tiles(requests, value_tile_store):
    tile_row_index = jnp.take(
        value_tile_store,
        lax.all_to_all(requests, "store", split_axis=0, concat_axis=0, tiled=True),
        axis=0,
    )
    return lax.all_to_all(tile_row_index, "store", split_axis=0, concat_axis=0, tiled=True)


def build_requests(flat_idx, inside, total):
    buffer = jnp.zeros((total,), jnp.int32)
    return buffer.at[flat_idx.reshape(-1)].set(inside.reshape(-1))


def attend_row(
    query_full,
    incoming_keys_full,
    incoming_values_full,
    left_rows,
    right_factor_rows,
    block_numbers,
    tile_row_index,
    length,
    step_index,
):
    query_group_size = query_full.shape[-1] // HEAD_SIZE // KEY_VALUE_HEADS
    every_head = query_group_size * KEY_VALUE_HEADS
    selected_count = block_numbers.shape[1]
    score_scale = HEAD_SIZE ** (-0.5)
    right_factor_heads = right_factor_rows.reshape(
        right_factor_rows.shape[0], KEY_VALUE_HEADS, HEAD_SIZE
    )
    token_positions = (
        block_numbers[:, :, None] * BLOCK_TOKENS + jnp.arange(BLOCK_TOKENS, dtype=jnp.int32)
    ).reshape(KEY_VALUE_HEADS, selected_count * BLOCK_TOKENS)
    picked = left_rows[token_positions]
    raw_keys = jnp.einsum(
        "htr,rhd->htd", picked, right_factor_heads, preferred_element_type=jnp.float32
    )
    cache_keys = apply_rotary(raw_keys, token_positions).astype(jnp.bfloat16)
    rotated_query = apply_rotary(
        query_full[step_index].reshape(every_head, HEAD_SIZE).astype(jnp.float32),
        length + step_index,
    ).astype(jnp.bfloat16)
    current_position = (length + jnp.arange(step_index + 1, dtype=jnp.int32))[:, None]
    current_keys = apply_rotary(
        incoming_keys_full[: step_index + 1]
        .reshape(step_index + 1, KEY_VALUE_HEADS, HEAD_SIZE)
        .astype(jnp.float32),
        current_position,
    ).astype(jnp.bfloat16)
    current_keys = jnp.transpose(current_keys, (1, 0, 2))
    current_values = jnp.transpose(
        incoming_values_full[: step_index + 1].reshape(step_index + 1, KEY_VALUE_HEADS, HEAD_SIZE),
        (1, 0, 2),
    )
    local_values = tile_row_index.reshape(KEY_VALUE_HEADS, selected_count * BLOCK_TOKENS, HEAD_SIZE)
    grouped_queries = rotated_query.reshape(KEY_VALUE_HEADS, query_group_size, HEAD_SIZE)
    cache_scores = (
        jnp.einsum("hgd,htd->hgt", grouped_queries, cache_keys, preferred_element_type=jnp.float32)
        * score_scale
    )
    inside_len = token_positions < length
    cache_scores = jnp.where(inside_len[:, None, :], cache_scores, -jnp.inf)
    fresh_scores = (
        jnp.einsum(
            "hgd,hnd->hgn", grouped_queries, current_keys, preferred_element_type=jnp.float32
        )
        * score_scale
    )
    highest = jnp.maximum(
        jnp.max(cache_scores, -1, keepdims=True), jnp.max(fresh_scores, -1, keepdims=True)
    )
    cache_exp = jnp.exp(cache_scores - highest)
    fresh_exp = jnp.exp(fresh_scores - highest)
    denominator = jnp.sum(cache_exp, -1, keepdims=True) + jnp.sum(fresh_exp, -1, keepdims=True)
    cache_weight = (cache_exp / denominator).astype(jnp.bfloat16)
    fresh_weight = (fresh_exp / denominator).astype(jnp.bfloat16)
    attended = jnp.einsum(
        "hgt,htd->hgd", cache_weight, local_values, preferred_element_type=jnp.float32
    )
    attended = attended + jnp.einsum(
        "hgn,hnd->hgd", fresh_weight, current_values, preferred_element_type=jnp.float32
    )
    return attended.reshape(every_head * HEAD_SIZE).astype(jnp.bfloat16)


def per_device(
    queries,
    new_keys,
    incoming_values,
    key_left,
    right_key_factor,
    value_tile_store,
    slot_map,
    chosen,
    lengths,
):
    nstore = lax.axis_size("store")
    local_rows = key_left.shape[0]
    nchunk = slot_map.shape[2]
    step_count = chosen.shape[0]
    selected_count = chosen.shape[3]
    keeper_share = max(1, nchunk // nstore // 4)
    tile_limit = local_rows * KEY_VALUE_HEADS * keeper_share
    pool_here = value_tile_store.shape[0]
    slot_numbers = jnp.take_along_axis(
        jnp.broadcast_to(slot_map[None], (step_count,) + slot_map.shape), chosen, axis=3
    )
    tile_keeper = slot_numbers // pool_here
    inside = slot_numbers % pool_here
    matched = tile_keeper[..., :, None] == tile_keeper[..., None, :]
    earlier = jnp.arange(selected_count)[None, :] < jnp.arange(selected_count)[:, None]
    order_in = jnp.sum(jnp.logical_and(matched, earlier), -1)
    row_head = (
        jnp.arange(local_rows, dtype=jnp.int32)[:, None, None] * KEY_VALUE_HEADS
        + jnp.arange(KEY_VALUE_HEADS, dtype=jnp.int32)[None, :, None]
    )
    position = row_head * keeper_share + order_in
    tiles_all = []
    slot_span = step_count * tile_limit
    flat_idx = (
        tile_keeper * slot_span
        + jnp.arange(step_count, dtype=jnp.int32)[:, None, None, None] * tile_limit
        + position
    )
    requests = build_requests(flat_idx, inside, nstore * slot_span).reshape(nstore, slot_span)
    received = fetch_tiles(requests, value_tile_store).reshape(nstore * slot_span, -1)
    for step_index in range(step_count):
        tiles_all.append(received[flat_idx[step_index]])
    results = []
    for step_index in range(step_count):
        per_rows = [
            attend_row(
                queries[:, 0],
                new_keys[:, 0],
                incoming_values[:, 0],
                key_left[0],
                right_key_factor[0],
                chosen[step_index, 0],
                tiles_all[step_index][0],
                lengths[0],
                step_index,
            )
        ]
        results.append(jnp.stack(per_rows))
    return jnp.stack(results)


def fused_kernel(
    share, pool_here,
    length_ref, pick_ref, ahead_ref, query_ref, new_key_ref, new_value_ref,
    chosen_ref, slot_ref, right_hbm, table_hbm, expand_hbm, spread_hbm, regroup_hbm, left_hbm,
    pool_hbm,
    out_ref,
    left_ref, right_ref, expand_ref, spread_ref, regroup_ref, pool_ref, block_ref,
    send_ref, ask_ref, asked_ref, row_ref, place_ref, sign_ref, bound_ref,
    rotated_ref, fresh_score_ref, fresh_value_ref, factor_ref, raw_even, raw_odd, turn_even, turn_odd, score_ref, fresh_ref,
    routed_ref, wire_ref, got_ref,
    core_out, core_in, last_out, last_in, keep_ref,
    in_sem, pool_sem, row_sem, ask_send, ask_recv, wire_send, wire_recv,
    core_send, core_recv, last_send, last_recv,
):
    me = lax.axis_index("store")
    raw_refs, turn_refs = (raw_even, raw_odd), (turn_even, turn_odd)
    holders = send_ref.shape[0]
    depth = holders // 4
    rows, picks = chosen_ref.shape
    heads, blocks = slot_ref.shape
    steps = rows // heads
    rank = left_hbm.shape[0]
    deep = block_ref.shape[2] - 2 * HEAD_SIZE
    group = query_ref.shape[1] // HEAD_SIZE // heads
    both = steps * group
    half = HEAD_SIZE // 2
    units = heads // 2
    parts = ((0, units - 2), (units - 2, units))
    scale = HEAD_SIZE ** (-0.5)
    core, side, layer = lax.rem(me, 2), lax.rem(me // 2, 2), me // 4

    def peer(j):
        far, across, ahead = j // (2 * depth), j // depth % 2, j % depth
        return (
            lax.rem(layer + ahead, depth) * 4
            + (1 - side if across else side) * 2
            + (1 - core if far else core)
        )

    def remote(src, dst, send, recv, target):
        return pltpu.make_async_remote_copy(
            src_ref=src, dst_ref=dst, send_sem=send, recv_sem=recv,
            device_id={"store": target}, device_id_type=pl.DeviceIdType.MESH,
        )

    barrier = pltpu.get_barrier_semaphore()

    def greet(k, _):
        pl.semaphore_signal(
            barrier, inc=1, device_id={"store": lax.rem(me + k, holders)},
            device_id_type=pl.DeviceIdType.MESH,
        )
        return 0

    loads = [
        pltpu.make_async_copy(src, dst, in_sem.at[at])
        for at, (src, dst) in enumerate(
            (
                (left_hbm, left_ref),
                (right_hbm, right_ref),
                (table_hbm, block_ref.at[:, :, pl.ds(deep, 2 * HEAD_SIZE)]),
                (expand_hbm, expand_ref),
                (regroup_hbm, regroup_ref),
                (spread_hbm, spread_ref),
            )
        )
    ]
    for copy in loads:
        copy.start()
    lax.fori_loop(1, holders, greet, 0)

    octets = pool_here // 8
    pool_copies = [
        pltpu.make_async_copy(
            pool_hbm.at[:, pl.ds(2 * q, 2), pl.ds(HEAD_SIZE * t, HEAD_SIZE)],
            pool_ref.at[pl.ds(q * octets, octets), pl.ds(2 * t, 2), :],
            pool_sem.at[0],
        )
        for q in range(4)
        for t in range(BLOCK_TOKENS)
    ]

    total = holders * share
    length = length_ref[0]
    lane_at = lax.broadcasted_iota(jnp.int32, (heads, total), 1)
    first_step = lane_at < picks
    chosen = jnp.concatenate([chosen_ref[s * heads : (s + 1) * heads] for s in range(steps)], 1)
    slot = jnp.zeros((heads, total), jnp.int32)
    for at in range(0, blocks, total):
        found = jnp.take_along_axis(slot_ref[:, at : at + total], chosen & (total - 1), axis=1)
        slot = jnp.where(chosen // total == at // total, found, slot)
    if pool_here & (pool_here - 1) == 0:
        keeper = slot >> (pool_here.bit_length() - 1)
        inside = slot & (pool_here - 1)
    else:
        keeper = lax.div(slot, jnp.full_like(slot, pool_here))
        inside = slot - keeper * pool_here
    sign_ref[...] = (1 - 2 * (inside & 1)).astype(jnp.float32)
    inside = ((inside >> 1) & 3) * octets + (inside >> 3)
    before_row = lax.broadcasted_iota(jnp.int32, (total, total), 0)
    before_lane = lax.broadcasted_iota(jnp.int32, (total, total), 1)
    before = jnp.where(
        jnp.logical_and(before_row < before_lane, before_row // picks == before_lane // picks),
        1.0, 0.0,
    ).astype(jnp.bfloat16)
    mine = [jnp.where(keeper == holder, 1.0, 0.0) for holder in range(holders)]
    counts = jnp.dot(
        jnp.concatenate(mine, 0).astype(jnp.bfloat16), before, preferred_element_type=jnp.float32
    )
    order = jnp.zeros((heads, total), jnp.float32)
    for holder in range(holders):
        order = order + mine[holder] * counts[holder * heads : (holder + 1) * heads]
    place = keeper * share + order.astype(jnp.int32)
    place_ref[...] = place
    digits = []
    for s in range(steps):
        for shift in (0, 8, 16):
            digit = ((inside >> shift) & 255).astype(jnp.float32)
            digits.append(jnp.where(first_step == (s == 0), digit, 0.0))
    slot_at = before_row
    moved = [None] * rows
    for head in range(heads):
        lines = jnp.concatenate(
            [digit[head : head + 1] for digit in digits]
            + [jnp.zeros((8 - len(digits), total), jnp.float32)], 0
        ).astype(jnp.bfloat16)
        table = jnp.where(place[head : head + 1] == slot_at, 1.0, 0.0).astype(jnp.bfloat16)
        found = lax.dot_general(
            lines, table, (((1,), (1,)), ((), ())), preferred_element_type=jnp.float32
        ).astype(jnp.int32)
        for s in range(steps):
            row = s * heads + head
            whole = found[3 * s : 3 * s + 1] + found[3 * s + 1 : 3 * s + 2] * 256
            whole = whole + found[3 * s + 2 : 3 * s + 3] * 65536
            moved[row] = pltpu.roll(whole, row * share, 1) if row else whole
    moved = jnp.concatenate(moved, 0)
    own_lanes = (
        lax.broadcasted_iota(jnp.int32, (rows, total), 1) // share
        == lax.broadcasted_iota(jnp.int32, (rows, total), 0)
    )
    for holder in range(holders):
        turned = pltpu.roll(moved, total - holder * share, 1) if holder else moved
        send_ref[holder] = jnp.sum(jnp.where(own_lanes, turned, 0), 0, keepdims=True)

    def ask_copy(j):
        target = peer(j)
        return remote(
            send_ref.at[target], ask_ref.at[j], ask_send.at[0], ask_recv.at[0], target
        )

    turn_of = (3, 2, 1, 0)
    far_first = sorted(
        range(1, holders),
        key=lambda j: (turn_of[j // depth], -min(j % depth, depth - j % depth)),
    )
    pl.semaphore_wait(barrier, holders - 1)
    for j in far_first:
        ask_copy(j).start()
    ask_ref[0] = send_ref[me]

    loads[1].wait()
    for head in range(heads):
        factor = right_ref[:, head * HEAD_SIZE : (head + 1) * HEAD_SIZE]
        factor_ref[head, :, :HEAD_SIZE] = factor
        factor_ref[head, :, HEAD_SIZE:] = pltpu.roll(
            factor.astype(jnp.float32), half, 1
        ).astype(jnp.bfloat16)
    loads[3].wait()
    remaining = jnp.clip(length - chosen * BLOCK_TOKENS, 0, BLOCK_TOKENS)
    bound_ref[...] = jnp.dot(
        remaining.astype(jnp.float32).astype(jnp.bfloat16), expand_ref[...],
        preferred_element_type=jnp.float32,
    )
    same = jnp.where(before_row == before_lane, 1.0, 0.0).astype(jnp.bfloat16)
    loads[0].wait()
    turned_blocks = total // BLOCK_TOKENS
    for at in range(0, left_ref.shape[1], total):
        if at // total % 3 != 0:
            turned = left_ref[:, at : at + total].astype(jnp.float32).T
        else:
            turned = lax.dot_general(
                same, left_ref[:, at : at + total], (((1,), (1,)), ((), ())),
                preferred_element_type=jnp.float32,
            )
        first = at // BLOCK_TOKENS
        block_ref[first : first + turned_blocks, :, :rank] = turned.reshape(
            turned_blocks, BLOCK_TOKENS, rank
        )
    loads[2].wait()
    for copy in pool_copies:
        copy.start()

    last = jnp.maximum(length - 1, 0)
    turn = block_ref[last // BLOCK_TOKENS, pl.ds(lax.rem(last, BLOCK_TOKENS), 1), deep:]
    last_cos, last_sin = turn[:, :HEAD_SIZE], turn[:, HEAD_SIZE:]
    spin_cos, spin_sin = [], []
    for s in range(steps):
        more_cos, more_sin = ahead_ref[2 * s : 2 * s + 1], ahead_ref[2 * s + 1 : 2 * s + 2]
        spin_cos.append(
            jnp.broadcast_to(last_cos * more_cos - last_sin * more_sin, (group, HEAD_SIZE))
        )
        spin_sin.append(
            jnp.broadcast_to(last_sin * more_cos + last_cos * more_sin, (group, HEAD_SIZE))
        )
    query_all = query_ref[...].astype(jnp.float32)
    key_all = new_key_ref[...].astype(jnp.float32)
    value_all = new_value_ref[...].astype(jnp.float32)
    fresh_cos = jnp.concatenate([spin_cos[s][:1] for s in range(steps)] + [spin_cos[0][: 8 - steps]], 0)
    fresh_sin = jnp.concatenate([spin_sin[s][:1] for s in range(steps)] + [spin_sin[0][: 8 - steps]], 0)
    both_cos = jnp.concatenate(spin_cos, 0)
    both_sin = jnp.concatenate(spin_sin, 0)
    empty = jnp.zeros((8 - steps, HEAD_SIZE), jnp.float32)
    fresh_keep = (
        lax.broadcasted_iota(jnp.int32, (both, 8), 1)
        <= lax.broadcasted_iota(jnp.int32, (both, 8), 0) // group
    )
    for head in range(heads):
        lanes = slice(head * HEAD_SIZE, (head + 1) * HEAD_SIZE)
        flat = jnp.concatenate(
            [
                query_all[s : s + 1, (head * group + g) * HEAD_SIZE : (head * group + g + 1) * HEAD_SIZE]
                for s in range(steps)
                for g in range(group)
            ],
            0,
        )
        query = (flat * both_cos + pltpu.roll(flat, half, 1) * both_sin).astype(jnp.bfloat16)
        for s in range(steps):
            rotated_ref[s * heads + head] = query[s * group : (s + 1) * group]
        flat = jnp.concatenate([key_all[:, lanes], empty], 0)
        fresh_key = (flat * fresh_cos + pltpu.roll(flat, half, 1) * fresh_sin).astype(jnp.bfloat16)
        fresh = lax.dot_general(
            query, fresh_key, (((1,), (1,)), ((), ())), preferred_element_type=jnp.float32
        ) * scale
        fresh_score_ref[head] = jnp.where(fresh_keep, fresh, -jnp.inf)
        fresh_value_ref[head] = jnp.concatenate([value_all[:, lanes], empty], 0).astype(
            jnp.bfloat16
        )

    token_at = (
        lax.broadcasted_iota(jnp.int32, (group, picks * BLOCK_TOKENS), 1) % BLOCK_TOKENS
    ).astype(jnp.float32)
    low_half = lax.broadcasted_iota(jnp.int32, (group, total), 1) < picks

    portion = 4 * total // BLOCK_TOKENS
    portions = picks // portion

    def gather(row, at):
        head, s = divmod(row, steps)
        found = [
            block_ref[pick_ref[s * heads + head, at * portion + n]] for n in range(portion)
        ]
        span = slice(4 * at * total, 4 * (at + 1) * total)
        raw_refs[row % 2][span] = jnp.dot(
            jnp.concatenate([value[:, :rank] for value in found], 0).astype(jnp.bfloat16),
            factor_ref[head], preferred_element_type=jnp.float32,
        )
        turn_refs[row % 2][span] = jnp.concatenate([value[:, deep:] for value in found], 0)

    def compare(row, at):
        head, s = divmod(row, steps)
        span = slice(4 * at * total, 4 * (at + 1) * total)
        raw = raw_refs[row % 2][span]
        keys = raw * turn_refs[row % 2][span]
        keys = keys[:, :HEAD_SIZE] + keys[:, HEAD_SIZE:]
        score_ref[row, :, span] = lax.dot_general(
            rotated_ref[s * heads + head], keys.astype(jnp.bfloat16), (((1,), (1,)), ((), ())),
            preferred_element_type=jnp.float32,
        )

    def key_rows(first, last):
        for row in range(first, last):
            for at in range(portions):
                if row + 1 < rows:
                    gather(row + 1, at)
                compare(row, at)

    def weigh(part):
        weights = []
        heads_here = range(2 * parts[part][0], 2 * parts[part][1])
        for head in heads_here:
            fresh_weights = []
            for s in range(steps):
                bound = jnp.broadcast_to(
                    bound_ref[head : head + 1, s * picks * BLOCK_TOKENS : (s + 1) * picks * BLOCK_TOKENS],
                    token_at.shape,
                )
                scores = jnp.where(token_at < bound, score_ref[head * steps + s] * scale, -jnp.inf)
                fresh = fresh_score_ref[head, s * group : (s + 1) * group]
                highest = jnp.maximum(
                    jnp.max(scores, -1, keepdims=True), jnp.max(fresh, -1, keepdims=True)
                )
                power = jnp.exp(scores - highest)
                fresh_power = jnp.exp(fresh - highest)
                inverse = 1.0 / (
                    jnp.sum(power, -1, keepdims=True) + jnp.sum(fresh_power, -1, keepdims=True)
                )
                weights.append(power * inverse)
                fresh_weights.append(fresh_power * inverse)
            fresh_ref[head * both : (head + 1) * both] = jnp.dot(
                jnp.concatenate(fresh_weights, 0).astype(jnp.bfloat16), fresh_value_ref[head],
                preferred_element_type=jnp.float32,
            )
        yield
        grouped = jnp.dot(
            jnp.concatenate(weights, 0).astype(jnp.bfloat16), regroup_ref[...],
            preferred_element_type=jnp.float32,
        )
        for h, head in enumerate(heads_here):
            lines = []
            for s in range(steps):
                line = grouped[(h * steps + s) * group : (h * steps + s + 1) * group]
                for t in range(BLOCK_TOKENS):
                    value = line[:, t // 2 * total : (t // 2 + 1) * total]
                    if t % 2 != s:
                        value = pltpu.roll(value, picks, 1)
                    lines.append(
                        jnp.where(low_half, value, 0.0) if s == 0 else jnp.where(low_half, 0.0, value)
                    )
            table = jnp.where(
                place_ref[head : head + 1] == slot_at,
                jnp.broadcast_to(sign_ref[head : head + 1], (total, total)), 0.0,
            ).astype(jnp.bfloat16)
            routed = lax.dot_general(
                jnp.concatenate(lines, 0).astype(jnp.bfloat16), table, (((1,), (1,)), ((), ())),
                preferred_element_type=jnp.float32,
            )
            for s in range(steps):
                for t in range(BLOCK_TOKENS):
                    at = (s * BLOCK_TOKENS + t) * group
                    routed_ref[t, head, s * group : (s + 1) * group] = routed[at : at + group]

    lane = lax.broadcasted_iota(jnp.int32, (both, total), 1) // share

    def wire_copy(part, j):
        target = peer(j)
        first, last = parts[part]
        return remote(
            wire_ref.at[target, pl.ds(first, last - first)],
            got_ref.at[j, pl.ds(first, last - first)],
            wire_send.at[part], wire_recv.at[part * 4 + j // depth], target,
        )

    def wires_in(part, quarter):
        first, last = parts[part]
        span = (pl.ds(max(1, quarter * depth), min(depth, quarter * depth + depth - 1)),
                pl.ds(first, last - first))
        return remote(
            wire_ref.at[span], got_ref.at[span],
            wire_send.at[part], wire_recv.at[part * 4 + quarter], peer(1),
        )

    def wires_out(part):
        first, last = parts[part]
        span = (pl.ds(1, holders - 1), pl.ds(first, last - first))
        return remote(
            wire_ref.at[span], got_ref.at[span],
            wire_send.at[part], wire_recv.at[part * 4], peer(1),
        )

    loads[4].wait()
    for at in range(portions):
        gather(0, at)
    def cross(first, last):
        for unit in range(first, last):
            cells = [
                routed_ref[t, 2 * unit + h] for t in range(BLOCK_TOKENS) for h in range(2)
            ]
            step = 1
            while step < holders:
                low_side = lane // step % 2 == 0
                turned = list(cells)
                for at in range(holders):
                    if at // step % 2 == 0:
                        a, b = cells[at], cells[at + step]
                        turned[at] = jnp.where(
                            low_side, a, pltpu.roll(b, step * share, 1)
                        )
                        turned[at + step] = jnp.where(
                            low_side, pltpu.roll(a, total - step * share, 1), b
                        )
                cells = turned
                step *= 2
            for holder in range(holders):
                wire_ref[holder, unit] = cells[holder].astype(jnp.bfloat16)
    others = pl.ds(1, holders - 1)
    all_asks = remote(
        send_ref.at[others], ask_ref.at[others], ask_send.at[0], ask_recv.at[0], peer(1)
    )
    row_copy = pltpu.make_async_copy(asked_ref, row_ref, row_sem.at[0])
    key_rows(0, 2 * parts[0][1] * steps)
    for part, (first, last) in enumerate(parts):
        later = [
            (row, row + 1)
            for row in range(
                2 * last * steps, 2 * parts[min(part + 1, len(parts) - 1)][1] * steps
            )
        ]
        for _ in weigh(part):
            if later:
                key_rows(*later.pop(0))
        if later:
            key_rows(*later.pop(0))
        cross(first, last)
        for j in far_first:
            wire_copy(part, j).start()
        if part == 0:
            all_asks.wait_recv()
            asked_ref[...] = jnp.clip(ask_ref[...], 0, pool_ref.shape[0] - 1)
            row_copy.start()
        for span_rows in later:
            key_rows(*span_rows)

    loads[5].wait()
    row_copy.wait()
    pltpu.make_async_copy(pool_ref, pool_ref, pool_sem.at[0]).wait()

    early = lax.broadcasted_iota(jnp.int32, (both, HEAD_SIZE), 0) < group

    def partials(pieces):
        arrived = [got_ref[j, unit] if j else wire_ref[me, unit] for unit, j in pieces]
        weight = jnp.maximum(
            jnp.dot(
                jnp.concatenate(arrived, 0), spread_ref[...], preferred_element_type=jnp.float32
            ),
            0.0,
        )
        return [
            partial(unit, j, weight[at * both : (at + 1) * both])
            for at, (unit, j) in enumerate(pieces)
        ]

    def partial(unit, j, weight):
        lhs, columns = [], []
        for h in range(2):
            own = weight[:, h * HEAD_SIZE : (h + 1) * HEAD_SIZE]
            lhs.append(
                jnp.concatenate(
                    [jnp.where(early, own, 0.0), jnp.where(early, 0.0, own)], 1
                ).astype(jnp.bfloat16)
            )
            columns.append(
                jnp.concatenate(
                    [
                        pool_ref[row_ref[j, 0, (s * heads + 2 * unit + h) * share + n]]
                        for s in range(steps)
                        for n in range(share)
                    ],
                    0,
                )
            )
        product = jnp.dot(
            jnp.concatenate(lhs, 0), jnp.concatenate(columns, 1),
            preferred_element_type=jnp.float32,
        )
        return jnp.concatenate([product[:both, :HEAD_SIZE], product[both:, HEAD_SIZE:]], 0)

    own_core = peer(2 * depth)

    def span(part):
        first, last = parts[part]
        return pl.ds(first * 2 * both, (last - first) * 2 * both)

    def core_copy(part, across):
        at = part * 2 + across
        return remote(
            core_out.at[across, :, span(part)], core_in.at[across, :, span(part)],
            core_send.at[at], core_recv.at[at], own_core,
        )

    def values_of(part, js):
        units_here = range(*parts[part])
        found = partials([(unit, j) for j in js for unit in units_here])
        count = len(units_here)
        return [
            jnp.concatenate(found[at * count : (at + 1) * count], 0) for at in range(len(js))
        ]

    def far_stage(part, across):
        first = 2 * depth + across * depth
        wires_in(part, 2 + across).wait_recv()
        values = values_of(part, range(first, first + depth))
        for ahead, value in enumerate(values):
            core_out[across, ahead, span(part)] = value
        core_copy(part, across).start()

    def direct_copy(part, slot):
        across, ahead = slot // depth, slot % depth
        return remote(
            last_out.at[slot, span(part)], last_in.at[slot, span(part)],
            last_send.at[part], last_recv.at[part],
            lax.rem(layer - ahead + depth, depth) * 4
            + (1 - side if across else side) * 2 + core,
        )

    def all_direct(part):
        every = (pl.ds(1, 2 * depth - 1), span(part))
        return remote(
            last_out.at[every], last_in.at[every], last_send.at[part], last_recv.at[part], peer(1)
        )

    def near_stage(part, across):
        wires_in(part, across).wait_recv()
        slots = range(max(1, across * depth), (across + 1) * depth)
        values = values_of(part, slots)
        core_copy(part, across).wait_recv()
        for slot, value in zip(slots, values):
            last_out[slot, span(part)] = (
                value + core_in[across, slot % depth, span(part)]
            ).astype(jnp.bfloat16)
        for slot in reversed(slots):
            direct_copy(part, slot).start()

    def finish(part):
        all_direct(part).wait_recv()
        value = keep_ref[span(part)]
        for slot in range(1, 2 * depth):
            value = value + last_in[slot, span(part)].astype(jnp.float32)
        keep_ref[span(part)] = value
        for head in range(2 * parts[part][0], 2 * parts[part][1]):
            for g in range(group):
                at = (head * group + g) * HEAD_SIZE
                out_ref[:, at : at + HEAD_SIZE] = jnp.concatenate(
                    [
                        keep_ref[head * both + s * group + g : head * both + s * group + g + 1]
                        for s in range(steps)
                    ],
                    0,
                )

    for part in range(len(parts)):
        far_stage(part, 1)
        far_stage(part, 0)
        near_stage(part, 1)
        near_stage(part, 0)
        if part == 0:
            own = partials([(unit, 0) for unit in range(units)])
    keep_ref[...] = jnp.concatenate(own, 0) + fresh_ref[...] + core_in[0, 0]
    all_asks.wait_send()
    for part in range(len(parts)):
        wires_out(part).wait_send()
        core_copy(part, 0).wait_send()
        core_copy(part, 1).wait_send()
    for part in range(len(parts)):
        finish(part)
    for part in range(len(parts)):
        all_direct(part).wait_send()


def fused_device(
    queries, new_keys, incoming_values, key_left, right_key_factor, value_tile_store, slot_map,
    chosen, lengths,
):
    holders = lax.axis_size("store")
    steps, _, heads, picks = chosen.shape
    blocks = slot_map.shape[2]
    share = max(1, blocks // holders // 4)
    pool_here = value_tile_store.shape[0]
    group = queries.shape[2] // HEAD_SIZE // heads
    rank = key_left.shape[2]
    slots = steps * heads * share
    rows = steps * heads * group
    both = steps * group
    units = heads // 2
    depth = holders // 4
    half = HEAD_SIZE // 2
    tokens = blocks * BLOCK_TOKENS

    turns = np.arange(tokens)[:, None] * ROPE_BASE ** (-(np.arange(half) * 2.0 / HEAD_SIZE))[None]
    cosine, sine = np.cos(turns), np.sin(turns)
    table = np.concatenate([cosine, cosine, -sine, sine], 1).astype(np.float32)
    ahead = jnp.asarray(table[1 : steps + 1].reshape(2 * steps, HEAD_SIZE))
    table = jnp.asarray(table.reshape(blocks, BLOCK_TOKENS, 2 * HEAD_SIZE))
    expand = np.repeat(np.eye(steps * picks, dtype=np.float32), BLOCK_TOKENS, 1)
    deep = -(-rank // 128) * 128
    wide = BLOCK_TOKENS * 64
    regroup = np.zeros((wide, wide), np.float32)
    for t in range(BLOCK_TOKENS):
        regroup[np.arange(64) * BLOCK_TOKENS + t, t * 64 + np.arange(64)] = 1.0
    spread = np.zeros((BLOCK_TOKENS, 2, share, 2, share, BLOCK_TOKENS, 2), np.float32)
    for t in range(BLOCK_TOKENS):
        for h in range(2):
            for n in range(share):
                spread[t, h, n, h, n, t] = (1.0, -1.0)
    lines = BLOCK_TOKENS * 2 * share
    spread = spread.reshape(lines, 2 * lines)

    vmem = pl.BlockSpec(memory_space=pltpu.VMEM)
    anywhere = pl.BlockSpec(memory_space=pl.ANY)
    bf16, f32 = jnp.bfloat16, jnp.float32
    dma = pltpu.SemaphoreType.DMA
    attended = pl.pallas_call(
        functools.partial(fused_kernel, share, pool_here),
        in_specs=[pl.BlockSpec(memory_space=pltpu.SMEM)] * 2 + [vmem] * 6 + [anywhere] * 7,
        out_specs=vmem,
        out_shape=pltpu.VMEM((steps, heads * group * HEAD_SIZE), f32),
        scratch_shapes=[
            pltpu.VMEM((rank, tokens), bf16),
            pltpu.VMEM((rank, heads * HEAD_SIZE), bf16),
            pltpu.VMEM((steps * picks, steps * picks * BLOCK_TOKENS), bf16),
            pltpu.VMEM((lines, 2 * lines), bf16),
            pltpu.VMEM((wide, wide), bf16),
            pltpu.VMEM((pool_here // 2, 2 * BLOCK_TOKENS, HEAD_SIZE), bf16),
            pltpu.VMEM((blocks, BLOCK_TOKENS, deep + 2 * HEAD_SIZE), f32),
            pltpu.VMEM((holders, 1, slots), jnp.int32),
            pltpu.VMEM((holders, 1, slots), jnp.int32),
            pltpu.VMEM((holders, 1, slots), jnp.int32),
            pltpu.SMEM((holders, 1, slots), jnp.int32),
            pltpu.VMEM((heads, steps * picks), jnp.int32),
            pltpu.VMEM((heads, steps * picks), f32),
            pltpu.VMEM((heads, steps * picks * BLOCK_TOKENS), f32),
            pltpu.VMEM((steps * heads, group, HEAD_SIZE), bf16),
            pltpu.VMEM((heads, both, 8), f32),
            pltpu.VMEM((heads, 8, HEAD_SIZE), bf16),
            pltpu.VMEM((heads, rank, 2 * HEAD_SIZE), bf16),
            pltpu.VMEM((picks * BLOCK_TOKENS, 2 * HEAD_SIZE), f32),
            pltpu.VMEM((picks * BLOCK_TOKENS, 2 * HEAD_SIZE), f32),
            pltpu.VMEM((picks * BLOCK_TOKENS, 2 * HEAD_SIZE), f32),
            pltpu.VMEM((picks * BLOCK_TOKENS, 2 * HEAD_SIZE), f32),
            pltpu.VMEM((heads * steps, group, picks * BLOCK_TOKENS), f32),
            pltpu.VMEM((rows, HEAD_SIZE), f32),
            pltpu.VMEM((BLOCK_TOKENS, heads, both, holders * share), f32),
            pltpu.VMEM((holders, units, both, lines), bf16),
            pltpu.VMEM((holders, units, both, lines), bf16),
            pltpu.VMEM((2, depth, rows, HEAD_SIZE), f32),
            pltpu.VMEM((2, depth, rows, HEAD_SIZE), f32),
            pltpu.VMEM((2 * depth, rows, HEAD_SIZE), bf16),
            pltpu.VMEM((2 * depth, rows, HEAD_SIZE), bf16),
            pltpu.VMEM((rows, HEAD_SIZE), f32),
            dma((6,)), dma((1,)), dma((1,)), dma((1,)), dma((1,)), dma((3,)), dma((12,)),
            dma((6,)), dma((6,)), dma((3,)), dma((3,)),
        ],
        compiler_params=pltpu.CompilerParams(collective_id=0, has_side_effects=True),
        name="fused",
    )(
        lengths, chosen[:, 0].reshape(steps * heads, picks), ahead,
        queries[:, 0], new_keys[:, 0], incoming_values[:, 0],
        chosen[:, 0].reshape(steps * heads, picks), slot_map[0],
        right_key_factor[0], table, jnp.asarray(expand, bf16), jnp.asarray(spread, bf16),
        jnp.asarray(regroup, bf16), key_left[0].T,
        value_tile_store.reshape(pool_here // 8, 8, -1),
    )
    return attended.astype(bf16).reshape(steps, 1, -1)


def solution(mesh):
    in_specs = (
        P(None, ("groups", "store"), None),
        P(None, ("groups", "store"), None),
        P(None, ("groups", "store"), None),
        P(("groups", "store"), None, None),
        P(("groups", "store"), None, None),
        P(("groups", "store"), None),
        P(("groups", "store"), None, None),
        P(None, ("groups", "store"), None, None),
        P(("groups", "store")),
    )
    out_specs = P(None, ("groups", "store"), None)

    def body(*args):
        holders = mesh.shape["store"]
        blocks = args[6].shape[2]
        share = max(1, blocks // holders // 4)
        square = args[7].shape[0] * args[7].shape[2] == holders
        packed = args[7].shape[0] * args[7].shape[3] == holders * share
        fits = square and packed and share == 8 and holders == 16 and blocks % 128 == 0
        return (fused_device if fits else per_device)(*args)

    return jax.shard_map(
        body, mesh=mesh, in_specs=in_specs, out_specs=out_specs, check_vma=False
    )
```
